32 devices in a mesh: gx: 4 (over y, x), gy: 8 (over z, core).
Axes of the slice: x: 2, y: 2, z: 4, core: 2. Of those that a mesh axis runs over, the one named last changes fastest.
Arguments:
- gradient: float32 [16, 512, 1024], P(None, 'gy', 'gx'), may hold values from -6 to 6
- members: float32 [8, 16, 256, 512], P(None, None, 'gy', 'gx'), may hold values from -6 to 6
Outputs:
- covariance_product: float32 [16, 512, 1024], P(None, 'gy', 'gx')
The draws below stay inside these ranges and needn't reach their ends.
All inputs are finite; a program needn't handle non-finite values.
Results may differ from the reference program's by a relative error of at most 0.0001.
Values sent between devices are 32-bit elements; how exact they have to be, the bound alone decides.
No kernel may reach another device: no remote copies, remote signals or barrier semaphores. Data moves between devices by JAX's collectives and lax.ppermute only.
A program may use at most 128 MiB of HBM per device.

```python
import jax
import jax.numpy as jnp
from jax import lax

LEV = 16
MEM = 8
NYF = 512
NXF = 1024
NYE = 256
NXE = 512


def level_of(own_key, extent, cuts, low, top_value):
    loudness, own = 1.0, jax.random.fold_in(own_key, 6)
    for dim, blocks in cuts:
        steps = jnp.exp(jax.random.uniform(jax.random.fold_in(own, dim), (blocks,), jnp.float32, low / len(cuts), top_value / len(cuts)))
        loudness = loudness * jnp.repeat(steps, extent[dim] // blocks).reshape([-1 if axis == dim else 1 for axis in range(len(extent))])
    return loudness


def normal_values(own_key, dims, width, bound, split=(), kind=jnp.bfloat16):
    gain = level_of(own_key, dims, split, -0.22, 0.18) if split else 1.0
    values = jax.random.normal(own_key, dims, jnp.float32) * width * gain
    return jnp.minimum(jnp.maximum(values, -bound), bound).astype(kind)


def setup_inputs(seed: int = 0) -> dict:
    key_list = jax.random.split(jax.random.key(seed), 3)
    gradient = normal_values(key_list[0], (LEV, NYF, NXF), 1.0, 6.0, ((1, 8), (2, 4)), jnp.float32)
    members = normal_values(key_list[1], (MEM, LEV, NYE, NXE), 1.0, 6.0, ((2, 8), (3, 4)), jnp.float32)
    return {"gradient": gradient, "members": members}


beta_raw = [(1.0 - (offset - 4) ** 2 / 25.0) ** 2 for offset in range(9)]
beta_taps = [value / sum(beta_raw) for value in beta_raw]
generations = ((1, 0.5), (2, 0.075), (4, 0.0125))


def convolve(padded):
    across = padded.shape[-1] - 8
    result = beta_taps[0] * padded[..., 0:across]
    for offset in range(1, 9):
        result = result + beta_taps[offset] * padded[..., offset:offset + across]
    height = result.shape[-2] - 8
    output = beta_taps[0] * result[..., 0:height, :]
    for offset in range(1, 9):
        output = output + beta_taps[offset] * result[..., offset:offset + height, :]
    return output


def coarsen(field, factor):
    shape = field.shape
    lead = tuple(shape[:-2])
    return field.reshape(lead + (shape[-2] // factor, factor, shape[-1] // factor, factor)).sum(axis=(-3, -1))


def refine(field, factor):
    return jnp.repeat(jnp.repeat(field, factor, axis=-2), factor, axis=-1)


def pad_rim(field):
    return jnp.pad(field, ((0, 0), (4, 4), (4, 4)))


def localise(member_field):
    total = jnp.zeros(member_field.shape, jnp.float32)
    for factor, weight in generations:
        block = coarsen(member_field, factor)
        once = convolve(pad_rim(block))
        twice = convolve(pad_rim(once))
        total = total + weight * refine(twice, factor)
    return total


def reference(gradient, members):
    odd = gradient[:, :, 1::2]
    earlier = jnp.pad(odd[:, :, :-1], ((0, 0), (0, 0), (1, 0)))
    across = gradient[:, :, 0::2] + 0.5 * (odd + earlier)
    odd_rows = across[:, 1::2, :]
    earlier_rows = jnp.pad(odd_rows[:, :-1, :], ((0, 0), (1, 0), (0, 0)))
    coarse = across[:, 0::2, :] + 0.5 * (odd_rows + earlier_rows)

    def per_member(member):
        return member * localise(member * coarse)

    weighted = lax.map(per_member, members)
    combined = jnp.sum(weighted, axis=0) / (MEM - 1)
    later_rows = jnp.pad(combined[:, 1:, :], ((0, 0), (0, 1), (0, 0)))
    half_rows = 0.5 * (combined + later_rows)
    rows = jnp.stack([combined, half_rows], axis=2).reshape(LEV, 2 * NYE, NXE)
    later_cols = jnp.pad(rows[:, :, 1:], ((0, 0), (0, 0), (0, 1)))
    half_cols = 0.5 * (rows + later_cols)
    return jnp.stack([rows, half_cols], axis=3).reshape(LEV, NYF, NXF)
```

```python
import functools

import jax
import jax.numpy as jnp
import numpy as np
from jax import lax
from jax.experimental import pallas as pl
from jax.experimental.pallas import tpu as pltpu
from jax.sharding import PartitionSpec as P

beta_raw = [(1.0 - (offset - 4) ** 2 / 25.0) ** 2 for offset in range(9)]
beta_taps = [value / sum(beta_raw) for value in beta_raw]
generations = ((1, 0.5), (2, 0.075), (4, 0.0125))

LANES = 128
GROUP = 8
EXTRA2, EXTRA4, EXTRA1 = 96, 97, 98
EDGE = 120
BF16, F32 = jnp.bfloat16, jnp.float32


def twice_filter(width, first, last):
    low, high = (0 if first else -99), (width - 1 if last else width + 99)
    table = np.zeros((width + 17, width + 1))
    for source in range(-8, width + 9):
        if not low <= source <= high:
            continue
        for middle in range(source - 4, source + 5):
            if not low <= middle <= high:
                continue
            for target in range(max(0, middle - 4), min(width, middle + 4) + 1):
                if target <= high:
                    table[source + 8, target] += beta_taps[middle - source + 4] * beta_taps[target - middle + 4]
    return table


def column_table(width, first, last):
    filters = {factor: twice_filter(width // factor, first, last) for factor, _ in generations}
    base = {1: 0, 2: LANES, 4: LANES + width // 2}
    extra = {1: LANES + EXTRA1, 2: LANES + EXTRA2, 4: LANES + EXTRA4}

    def row(places):
        out = np.zeros(2 * LANES)
        for factor, place in places.items():
            count = width // factor
            out[base[factor]:base[factor] + count] += filters[factor][place + 8, :count]
            out[extra[factor]] += filters[factor][place + 8, count]
        return out

    rows = [row({1: c, 2: c // 2, 4: c // 4}) for c in range(width)]
    rows += [row({1: c, 2: c // 2, 4: c // 4}) for c in range(-8, 0)]
    rows += [row({2: c, 4: c // 2}) for c in range(-8, -4)]
    rows += [row({4: c}) for c in range(-8, -4)]
    rows += [row({1: c, 2: c // 2, 4: c // 4}) for c in range(width, width + 8)] + [row({1: width + 8})]
    half, quarter = width // 2, width // 4
    rows += [row({2: c, 4: c // 2}) for c in range(half + 4, half + 8)] + [row({2: half + 8})]
    rows += [row({4: c}) for c in range(quarter + 4, quarter + 9)]
    return np.stack(rows)


def message_lanes():
    places = []
    for line in range(GROUP):
        places += [(0, line * 8 + c, c, 1, line) for c in range(8)]
        places += [(1, line * 9 + c, 16 + c, 1, line) for c in range(9)]
    for line in range(0, GROUP, 2):
        places += [(0, 64 + line // 2 * 4 + c, 8 + c, 2, line) for c in range(4)]
        places += [(1, 72 + line // 2 * 5 + c, 25 + c, 2, line) for c in range(5)]
    for line in range(0, GROUP, 4):
        places += [(0, 80 + line // 4 * 4 + c, 12 + c, 4, line) for c in range(4)]
        places += [(1, 92 + line // 4 * 5 + c, 30 + c, 4, line) for c in range(5)]
    return places


def packing_table(width):
    table = np.zeros((GROUP, width, 2 * LANES), np.float32)
    east = list(range(width - 8, width)) + [width // 2 - 8 + c for c in range(4)] + [width // 4 - 8 + c for c in range(4)]
    west = list(range(9)) + [4 + c for c in range(5)] + [4 + c for c in range(5)]
    for side, lane, compact, factor, line in message_lanes():
        start = (west[compact - 16] if side else east[compact]) * factor
        table[line:line + factor, start:start + factor, side * LANES + lane] = 1.0
    return table


def placing_table():
    table = np.zeros((GROUP, 2 * LANES, 36), np.float32)
    for side, lane, compact, factor, line in message_lanes():
        table[line, side * LANES + lane, compact] = 1.0
    for line in range(GROUP):
        table[line, EDGE + line, 35] = 1.0
        table[line, LANES + EDGE + line, 16] = 1.0
    return table


def restriction_table(width):
    table = np.zeros((2 * width, 2 * LANES), np.float32)
    for i in range(width):
        table[2 * i, i] += 1.0
        table[2 * i + 1, i] += 0.5
        table[2 * i + 1, i + 1] += 0.5
    return table


def refining_table(width):
    table = np.zeros((2, LANES, 2 * LANES), np.float32)
    for i in range(width):
        table[0, i // 2, i] = 1.0
        table[1, width // 2 + i // 4, i] = 1.0
    table[0, EXTRA2, LANES + EXTRA1] = 1.0
    table[1, EXTRA4, LANES + EXTRA1] = 1.0
    return table


def interpolation_table(width):
    table = np.zeros((2 * LANES, 2 * width), np.float32)
    for i in range(width):
        table[i, 2 * i] += 1.0
        table[i, 2 * i + 1] += 0.5
        table[i + 1 if i + 1 < width else LANES + EXTRA1, 2 * i + 1] += 0.5
    return table


def split(value):
    high = value.astype(BF16)
    return high, (value - high.astype(F32)).astype(BF16)


def mul(a, b):
    return jnp.dot(a, b, preferred_element_type=F32)


def exact_dot(value, table):
    high, low = split(value)
    return mul(high, table) + mul(low, table)


def pack_kernel(levels, height, place, gradient, members, south, restrict, packing,
                coarse_out, products, message_a, message_b, across, east):
    blocks = height // GROUP
    rows = members.reshape(8 * levels * height, LANES)
    tile = gradient[...].reshape(levels * 2 * height, gradient.shape[2])
    value = exact_dot(tile, restrict[...]).reshape(levels, 2 * height, 2 * LANES)
    below = exact_dot(south[...], restrict[...])
    for half in range(2):
        lanes = slice(half * LANES, (half + 1) * LANES)
        across[half, :, 8:, :] = value[:, :, lanes]
        for level in range(levels):
            across[half, level, 7:8, :] = below[level:level + 1, lanes]
    lane = lax.broadcasted_iota(jnp.int32, (GROUP, LANES), 1)
    line_of = lax.broadcasted_iota(jnp.int32, (GROUP, LANES), 0)

    def level_step(level, _):
        for half in range(2):
            value = across[half, level, pl.ds(8, height, 2), :] + 0.5 * (
                across[half, level, pl.ds(9, height, 2), :] + across[half, level, pl.ds(7, height, 2), :]
            )
            if half == 0:
                coarse_out[level] = value
            else:
                east[...] = value
        for block in range(blocks):
            place_rows = pl.ds(pl.multiple_of((level * blocks + block) * 8, 8), 8)
            edge = jnp.zeros((GROUP, LANES), F32)
            for line in range(GROUP):
                y = block * GROUP + line
                member = rows[pl.ds(level * height + y, 8, levels * height), :]
                products[line, place_rows, :] = member * coarse_out[level, y:y + 1, :]
                edge = jnp.where(lane == EDGE + line, pltpu.roll(member, EDGE + line, 1), edge)
            column = jnp.broadcast_to(east[block * GROUP:(block + 1) * GROUP, 0:1], (GROUP, LANES))
            column = jnp.sum(jnp.where(lane == EDGE + line_of, column, 0.0), axis=0, keepdims=True)
            message_a[place_rows, :] = jnp.broadcast_to(column, (GROUP, LANES))
            message_b[place_rows, :] = edge
        return 0

    lax.fori_loop(0, levels, level_step, 0)
    total = jnp.zeros((levels * blocks * 8, 2 * LANES), F32)
    for line in range(GROUP):
        total = total + exact_dot(products[line], packing[line])
    to_east = total[:, :LANES] + message_a[...]
    to_west = total[:, LANES:] + message_b[...]
    even = place[0] == 0
    message_a[...] = jnp.where(even, to_east, to_west)
    message_b[...] = jnp.where(even, to_west, to_east)


def columns_kernel(levels, height, place, products, own_a, own_b, got_a, got_b, own_high, own_low, halo_high, halo_low,
                   filtered, message_a, message_b):
    blocks = height // GROUP
    count = levels * blocks * 8
    lane = lax.broadcasted_iota(jnp.int32, (count, LANES), 1)
    even = place[0] == 0
    own_east, own_west = jnp.where(even, own_a[...], own_b[...]), jnp.where(even, own_b[...], own_a[...])
    west, east = jnp.where(even, got_b[...], got_a[...]), jnp.where(even, got_a[...], got_b[...])
    halo = jnp.concatenate(
        [jnp.where(lane >= EDGE, west * own_west, west), jnp.where(lane >= EDGE, east * own_east, east)], axis=1
    )
    halo_h, halo_l = split(halo)
    for line in range(GROUP):
        high, low = split(products[line])
        value = mul(high, own_high[...]) + mul(low, own_high[...]) + mul(high, own_low[...])
        value = value + (mul(halo_h, halo_high[line]) + mul(halo_l, halo_high[line]) + mul(halo_h, halo_low[line]))
        filtered[line] = value
    small = lax.broadcasted_iota(jnp.int32, (8, LANES), 1)
    second = (small < 64) | (small == EXTRA2)
    first = small == EXTRA1
    up_a = place[1] == 0
    start_a, start_b = jnp.where(up_a, blocks - 1, 0), jnp.where(up_a, 0, blocks - 1)
    coarse_a, coarse_b = jnp.where(up_a, blocks - 2, 0), jnp.where(up_a, 0, blocks - 2)

    def at(level, block, line):
        return filtered[line, pl.ds(pl.multiple_of((level * blocks + block) * 8, 8), 8), LANES:]

    def level_step(level, _):
        fourth = []
        for block in range(blocks):
            for half in range(2):
                fourth.append(sum(at(level, block, half * 4 + k) for k in range(1, 4)) + at(level, block, half * 4))
        for message, start, coarse in ((message_a, start_a, coarse_a), (message_b, start_b, coarse_b)):
            rows = pl.ds(pl.multiple_of((level * blocks + start) * 8, 8), 8)
            for line in range(GROUP):
                message[level, line] = filtered[line, rows, :LANES]
                block, pair = coarse + line // 4, line % 4
                pairs = at(level, block, 2 * pair) + at(level, block, 2 * pair + 1)
                value = jnp.where(second, pairs, fourth[line])
                message[level, 8 + line] = jnp.where(first, filtered[line, rows, LANES:], value)
        return 0

    lax.fori_loop(0, levels, level_step, 0)


def combine_kernel(levels, height, place, filtered, got_a, got_b, members, east_a, east_b, refining, combined,
                   fine, pairs, second_up, fourth_up, weighted):
    blocks = height // GROUP
    rows = members.reshape(8 * levels * height, LANES)
    up_a = place[1] == 0
    low, high = place[2].astype(F32), place[3].astype(F32)
    even = place[0] == 0
    lane = lax.broadcasted_iota(jnp.int32, (8, LANES), 1)
    second = (lane < 64) | (lane == EXTRA2)
    taps = [jnp.float32(tap) for tap in beta_taps[:5]]
    scale = jnp.where(second, jnp.float32(generations[1][1]), jnp.float32(generations[2][1]))

    def convolve(window):
        value = taps[4] * window[4]
        for k in range(4):
            value = value + taps[k] * (window[k] + window[8 - k])
        return value

    def filter_twice(load, count, keep, store):
        once, window = [], []
        for r in range(-8, count + 8):
            window.append(load(r))
            if len(window) > 9:
                window.pop(0)
            if len(window) == 9:
                once.append(keep(r - 4, convolve(window)))
                if len(once) > 9:
                    once.pop(0)
                if len(once) == 9:
                    store(r - 8, convolve(once))

    def level_step(level, _):
        def at(y, lanes):
            return filtered[y % 8, pl.ds(pl.multiple_of((level * blocks + y // 8) * 8, 8), 8), lanes]

        def north(r):
            return jnp.where(up_a, got_a[level, r], got_b[level, r])

        def south(r):
            return jnp.where(up_a, got_b[level, r], got_a[level, r])

        def edges(r, value):
            return value * low if r < 0 else value * high if r >= height else value

        def load_first(r):
            return south(r + 8) if r < 0 else north(r - height) if r >= height else at(r, slice(0, LANES))

        def load_extra(r):
            return south(r + 16) if r < 0 else north(r - height + 8) if r >= height else at(r, slice(LANES, 2 * LANES))

        def store_first(r, value):
            fine[0, r] = value

        def store_extra(r, value):
            fine[1, r] = value

        filter_twice(load_first, height, edges, store_first)
        filter_twice(load_extra, height, edges, store_extra)

        half, quarter = height // 2, height // 4

        def pair(r):
            return at(2 * r, slice(LANES, 2 * LANES)) + at(2 * r + 1, slice(LANES, 2 * LANES))

        def load_coarse(r):
            if r < 0:
                return south(r + 16)
            if r >= half:
                return north(r - half + 8)
            if r < quarter:
                return jnp.where(second, pair(r), pair(2 * r) + pair(2 * r + 1))
            return jnp.where(second, pair(r), north(r - quarter + 8))

        def keep_coarse(r, value):
            if r < 0:
                return value * low
            if r >= half:
                return value * high
            if quarter <= r < quarter + 4:
                return jnp.where(second, value, value * high)
            return value

        def store_coarse(r, value):
            pairs[pl.ds(pl.multiple_of((level * half + r) * 8, 8), 8), :] = value * scale

        filter_twice(load_coarse, half, keep_coarse, store_coarse)
        start = pl.multiple_of(level * half * 8, 8)
        second_up[...] = exact_dot(pairs[pl.ds(start, half * 8), :], refining[0])
        fourth_up[...] = exact_dot(pairs[pl.ds(start, quarter * 8), :], refining[1])
        weight = jnp.float32(generations[0][1])
        for block in range(blocks):
            message_rows = pl.ds(pl.multiple_of((level * blocks + block) * 8, 8), 8)
            from_east = jnp.where(even, east_a[message_rows, :], east_b[message_rows, :])
            for line in range(GROUP):
                y = block * GROUP + line
                member = rows[pl.ds(level * height + y, 8, levels * height), :]
                edge = pltpu.roll(from_east, (EXTRA1 - EDGE - line) % LANES, 1)
                for part, factor in ((0, member), (1, edge)):
                    lanes = slice(part * LANES, (part + 1) * LANES)
                    value = weight * fine[part, y]
                    value = value + second_up[y // 2 * 8:y // 2 * 8 + 8, lanes] + fourth_up[y // 4 * 8:y // 4 * 8 + 8, lanes]
                    weighted[part, line * 8:line * 8 + 8, :] = factor * value
            for part in range(2):
                total = weighted[part, pl.ds(0, 8, 8), :]
                for m in range(1, 8):
                    total = total + weighted[part, pl.ds(m, 8, 8), :]
                combined[level, block * GROUP:(block + 1) * GROUP, part * LANES:(part + 1) * LANES] = total * (1.0 / 7.0)
        return 0

    lax.fori_loop(0, levels, level_step, 0)


def interpolate_kernel(levels, height, combined, north, interpolation, out, extended, rows):
    for level in range(levels):
        extended[0:height, :] = combined[level]
        extended[height:height + 1, :] = north[level:level + 1, :]
        for half in range(2):
            lanes = slice(half * LANES, (half + 1) * LANES)
            here = extended[0:height, lanes]
            rows[half, level, pl.ds(0, height, 2), :] = here
            rows[half, level, pl.ds(1, height, 2), :] = 0.5 * (here + extended[1:height + 1, lanes])
    value = exact_dot(
        jnp.concatenate([rows[half].reshape(levels * 2 * height, LANES) for half in range(2)], axis=1), interpolation[...]
    )
    out[...] = value.reshape(levels, 2 * height, out.shape[2])


def partner(index, size, second):
    other = ((index + 1) ^ 1) - 1 if second else index ^ 1
    return other if 0 <= other < size else None


def swap(value, axis, second):
    size = lax.axis_size(axis)
    pairs = [(i, partner(i, size, second)) for i in range(size)]
    return lax.ppermute(value, axis, [(i, j) for i, j in pairs if j is not None])


def call(kernel, outs, scratch, *args):
    smem = pl.BlockSpec(memory_space=pltpu.SMEM)
    vmem = pl.BlockSpec(memory_space=pltpu.VMEM)
    return pl.pallas_call(
        kernel,
        out_shape=tuple(jax.ShapeDtypeStruct(shape, F32) for shape in outs),
        in_specs=[smem if a.dtype == jnp.int32 else vmem for a in args],
        out_specs=tuple(vmem for _ in outs),
        scratch_shapes=[pltpu.VMEM(shape, F32) for shape in scratch],
    )(*args)


def shards(gradient, members):
    levels, fine_height, fine_width = gradient.shape
    count, _, height, width = members.shape
    assert count == 8 and width == LANES and height % 32 == 0
    blocks = height // GROUP
    group_rows = levels * blocks * 8
    gx, gy = lax.axis_index("gx"), lax.axis_index("gy")
    nx, ny = lax.axis_size("gx"), lax.axis_size("gy")
    assert nx > 1
    place = jnp.stack([gx % 2, gy % 2, (gy > 0).astype(jnp.int32), (gy < ny - 1).astype(jnp.int32)]).astype(jnp.int32)

    up = [(i, i + 1) for i in range(ny - 1)]
    south = lax.ppermute(gradient[:, -1, :], "gy", up)

    case = jnp.where(gx == 0, 0, jnp.where(gx == nx - 1, 2, 1))
    tables = np.stack([column_table(width, i == 0, i == 2) for i in range(3)]).astype(np.float32)
    high_tables = tables.astype(BF16)
    low_tables = (tables - high_tables.astype(np.float32)).astype(BF16)
    high, low = (lax.dynamic_index_in_dim(jnp.asarray(t), case, 0, keepdims=False) for t in (high_tables, low_tables))
    placing = jnp.asarray(placing_table(), BF16).reshape(GROUP * 2 * LANES, 36)
    order = list(range(width, width + 35)) + [0]
    compact_high, compact_low = high[np.array(order)], low[np.array(order)]
    halo_high = mul(placing, compact_high).astype(BF16).reshape(GROUP, 2 * LANES, 2 * LANES)
    halo_low = mul(placing, compact_low).astype(BF16).reshape(GROUP, 2 * LANES, 2 * LANES)

    coarse, products, own_a, own_b = call(
        functools.partial(pack_kernel, levels, height),
        [(levels, height, LANES), (GROUP, group_rows, LANES), (group_rows, LANES), (group_rows, LANES)],
        [(2, levels, 8 + 2 * height, LANES), (height, LANES)],
        place, gradient, members, south, jnp.asarray(restriction_table(width), BF16), jnp.asarray(packing_table(width), BF16),
    )
    got_a, got_b = swap(own_a, "gx", False), swap(own_b, "gx", True)
    filtered, rows_a, rows_b = call(
        functools.partial(columns_kernel, levels, height),
        [(GROUP, group_rows, 2 * LANES), (levels, 16, 8, LANES), (levels, 16, 8, LANES)],
        [],
        place, products, own_a, own_b, got_a, got_b, high[:width], low[:width], halo_high, halo_low,
    )
    far_b, far_a = swap(rows_b, "gy", True), swap(rows_a, "gy", False)
    (combined,) = call(
        functools.partial(combine_kernel, levels, height),
        [(levels, height, 2 * LANES)],
        [(2, height, 8, LANES), (levels * height // 2 * 8, LANES), (height // 2 * 8, 2 * LANES),
         (height // 4 * 8, 2 * LANES), (2, 64, LANES)],
        place, filtered, far_a, far_b, members, got_a, got_b, jnp.asarray(refining_table(width), BF16),
    )
    north = lax.ppermute(combined[:, 0, :], "gy", [(j, i) for i, j in up])
    (out,) = call(
        functools.partial(interpolate_kernel, levels, height),
        [(levels, fine_height, fine_width)],
        [(height + 8, 2 * LANES), (2, levels, 2 * height, LANES)],
        combined, north, jnp.asarray(interpolation_table(width), BF16),
    )
    return out


def solution(mesh):
    in_specs = (P(None, "gy", "gx"), P(None, None, "gy", "gx"))
    out_specs = P(None, "gy", "gx")
    return jax.shard_map(shards, mesh=mesh, in_specs=in_specs, out_specs=out_specs, check_vma=False)
```

```python
import functools

import jax
import jax.numpy as jnp
import numpy as np
from jax import lax
from jax.experimental import pallas as pl
from jax.experimental.pallas import tpu as pltpu
from jax.sharding import PartitionSpec as P

beta_raw = [(1.0 - (offset - 4) ** 2 / 25.0) ** 2 for offset in range(9)]
beta_taps = [value / sum(beta_raw) for value in beta_raw]
generations = ((1, 0.5), (2, 0.075), (4, 0.0125))

LANES = 128
GROUP = 8
SLOT = 16
EDGE = 15
EXTRA2, EXTRA4, EXTRA1 = 96, 97, 98
CHUNKS = 1
VMEM_LIMIT = 20 * 2**20
BF16, F32 = jnp.bfloat16, jnp.float32
double_taps = [
    sum(beta_taps[k + 4] * beta_taps[offset - k + 4] for k in range(-4, 5) if -4 <= offset - k <= 4) for offset in range(9)
]
edge_taps = [
    [sum(beta_taps[i - k + 4] * beta_taps[k - j + 4] for k in range(-4, 0) if i - k <= 4 and j - k <= 4) for j in range(4)]
    for i in range(4)
]

def twice_filter(width, first, last):
    low, high = (0 if first else -99), (width - 1 if last else width + 99)
    table = np.zeros((width + 17, width + 1))
    for source in range(-8, width + 9):
        if not low <= source <= high:
            continue
        for middle in range(source - 4, source + 5):
            if not low <= middle <= high:
                continue
            for target in range(max(0, middle - 4), min(width, middle + 4) + 1):
                if target <= high:
                    table[source + 8, target] += beta_taps[middle - source + 4] * beta_taps[target - middle + 4]
    return table


def column_table(width, first, last):
    filters = {factor: twice_filter(width // factor, first, last) for factor, _ in generations}
    base = {1: 0, 2: LANES, 4: LANES + width // 2}
    extra = {1: LANES + EXTRA1, 2: LANES + EXTRA2, 4: LANES + EXTRA4}

    def row(places):
        out = np.zeros(2 * LANES)
        for factor, place in places.items():
            count = width // factor
            out[base[factor]:base[factor] + count] += filters[factor][place + 8, :count]
            out[extra[factor]] += filters[factor][place + 8, count]
        return out

    rows = [row({1: c, 2: c // 2, 4: c // 4}) for c in range(width)]
    rows += [row({1: c, 2: c // 2, 4: c // 4}) for c in range(-8, 0)]
    rows += [row({2: c, 4: c // 2}) for c in range(-8, -4)]
    rows += [row({4: c}) for c in range(-8, -4)]
    rows += [row({1: c, 2: c // 2, 4: c // 4}) for c in range(width, width + 8)] + [row({1: width + 8})]
    half, quarter = width // 2, width // 4
    rows += [row({2: c, 4: c // 2}) for c in range(half + 4, half + 8)] + [row({2: half + 8})]
    rows += [row({4: c}) for c in range(quarter + 4, quarter + 9)]
    return np.stack(rows)


def message_lanes():
    places = []
    for line in range(GROUP):
        places += [(0, line * SLOT + c, c, 1, line) for c in range(8)]
        places += [(1, line * SLOT + c, 16 + c, 1, line) for c in range(9)]
        if line % 2 == 0:
            places += [(0, line * SLOT + 8 + c, 8 + c, 2, line) for c in range(4)]
            places += [(1, line * SLOT + 9 + c, 25 + c, 2, line) for c in range(5)]
        if line % 4 == 1:
            places += [(0, line * SLOT + 8 + c, 12 + c, 4, line - 1) for c in range(4)]
            places += [(1, line * SLOT + 9 + c, 30 + c, 4, line - 1) for c in range(5)]
    return places


def packing_table(width):
    table = np.zeros((GROUP, width, 2 * LANES), np.float32)
    east = list(range(width - 8, width)) + [width // 2 - 8 + c for c in range(4)] + [width // 4 - 8 + c for c in range(4)]
    west = list(range(9)) + [4 + c for c in range(5)] + [4 + c for c in range(5)]
    for side, lane, compact, factor, line in message_lanes():
        start = (west[compact - 16] if side else east[compact]) * factor
        table[line:line + factor, start:start + factor, side * LANES + lane] = 1.0
    return table


def halo_table(columns, width):
    table = np.zeros((2, 2 * SLOT, 2 * LANES))
    outer = columns[width:]
    for side, lane, compact, factor, line in message_lanes():
        if line < 2 and lane < 2 * SLOT:
            table[lane // SLOT, side * SLOT + lane % SLOT] = outer[compact]
    table[:, EDGE] = columns[0]
    table[:, SLOT + EDGE] = outer[16]
    return table


def restriction_table(width):
    table = np.zeros((2 * width, 2 * LANES), np.float32)
    for i in range(width):
        table[2 * i, i] += 1.0
        table[2 * i + 1, i] += 0.5
        table[2 * i + 1, i + 1] += 0.5
    return table


def refining_table(width):
    table = np.zeros((LANES, 2 * LANES), np.float32)
    for i in range(width):
        table[i // 2, i] = 1.0
        table[width // 2 + i // 4, i] = 1.0
    table[EXTRA2, LANES + EXTRA1] = 1.0
    table[EXTRA4, LANES + EXTRA1] = 1.0
    return table


def interpolation_table(width):
    table = np.zeros((2 * LANES, 2 * width), np.float32)
    for i in range(width):
        table[i, 2 * i] += 1.0
        table[i, 2 * i + 1] += 0.5
        table[i + 1 if i + 1 < width else LANES + EXTRA1, 2 * i + 1] += 0.5
    return table


def split(value):
    high = value.astype(BF16)
    return high, (value - high.astype(F32)).astype(BF16)


def mul(a, b):
    return jnp.dot(a, b, preferred_element_type=F32)


def exact_dot(value, table):
    high, low = split(value)
    return mul(high, table) + mul(low, table)


def three_dots(value, high_table, low_table):
    high, low = split(value)
    return mul(high, high_table) + mul(low, high_table) + mul(high, low_table)


def column_case():
    gx, nx = lax.axis_index("gx"), lax.axis_size("gx")
    return jnp.where(gx == 0, 0, jnp.where(gx == nx - 1, 2, 1))


def tile(index):
    return pl.ds(pl.multiple_of(index * 8, 8), 8)


def pack_kernel(chunk, levels, height, gradient, members, south, restrict, packing, products, message_a, message_b, across, coarse):
    blocks = height // GROUP
    first = chunk * levels
    all_levels = members.shape[1]
    rows = members.reshape(8 * all_levels * height, LANES)
    fine = gradient[first:first + levels].reshape(levels * 2 * height, gradient.shape[2])
    value = exact_dot(fine, restrict[...]).reshape(levels, 2 * height, 2 * LANES)
    below = exact_dot(south[...], restrict[...])
    for half in range(2):
        lanes = slice(half * LANES, (half + 1) * LANES)
        across[half, :, 8:, :] = value[:, :, lanes]
        for level in range(levels):
            across[half, level, 7:8, :] = below[first + level:first + level + 1, lanes]
    lane = lax.broadcasted_iota(jnp.int32, (GROUP, LANES), 1)
    line_of = lax.broadcasted_iota(jnp.int32, (GROUP, LANES), 0)

    def level_step(level, _):
        for half in range(2):
            coarse[half] = across[half, level, pl.ds(8, height, 2), :] + 0.5 * (
                across[half, level, pl.ds(9, height, 2), :] + across[half, level, pl.ds(7, height, 2), :]
            )
        for block in range(blocks):
            place_rows = tile(level * blocks + block)
            edge = jnp.zeros((GROUP, LANES), F32)
            for line in range(GROUP):
                y = block * GROUP + line
                member = rows[pl.ds((first + level) * height + y, 8, all_levels * height), :]
                products[line, place_rows, :] = member * coarse[0, y:y + 1, :]
                spot = line * SLOT + EDGE
                edge = jnp.where(lane == spot, pltpu.roll(member, spot, 1), edge)
            column = jnp.broadcast_to(coarse[1, block * GROUP:(block + 1) * GROUP, 0:1], (GROUP, LANES))
            column = jnp.sum(jnp.where(lane == line_of * SLOT + EDGE, column, 0.0), axis=0, keepdims=True)
            message_a[place_rows, :] = jnp.broadcast_to(column, (GROUP, LANES))
            message_b[place_rows, :] = edge
        return 0

    lax.fori_loop(0, levels, level_step, 0)
    total = jnp.zeros((levels * blocks * 8, 2 * LANES), F32)
    for line in range(0, GROUP, 2):
        value = jnp.concatenate([products[line], products[line + 1]], axis=1)
        total = total + exact_dot(value, packing[line * LANES:(line + 2) * LANES, :])
    to_east = total[:, :LANES] + message_a[...]
    to_west = total[:, LANES:] + message_b[...]
    even = lax.axis_index("gx") % 2 == 0
    message_a[...] = jnp.where(even, to_east, to_west)
    message_b[...] = jnp.where(even, to_west, to_east)


def own_columns_kernel(levels, height, products, high_tables, low_tables, halo_highs, halo_lows, filtered, halo_high, halo_low):
    groups = levels * height // GROUP
    case = column_case()
    for variant in range(4):
        for source, target in ((halo_highs, halo_high), (halo_lows, halo_low)):
            target[variant] = jnp.zeros((LANES, 2 * LANES), BF16)
            kind = variant % 2
            target[variant, variant * SLOT:(variant + 1) * SLOT, :] = source[case, kind, :SLOT, :]
            target[variant, 64 + variant * SLOT:64 + (variant + 1) * SLOT, :] = source[case, kind, SLOT:, :]
    high, low = high_tables[case], low_tables[case]
    for line in range(GROUP):
        filtered[:, line] = three_dots(products[line], high, low).reshape(groups, 8, 2 * LANES)


def columns_kernel(levels, height, partial, own_a, own_b, got_a, got_b, halo_high, halo_low, filtered, message_a, message_b):
    blocks = height // GROUP
    groups = levels * blocks
    lane = lax.broadcasted_iota(jnp.int32, (groups * 8, LANES), 1)
    even = lax.axis_index("gx") % 2 == 0
    own_east, own_west = jnp.where(even, own_a[...], own_b[...]), jnp.where(even, own_b[...], own_a[...])
    west, east = jnp.where(even, got_b[...], got_a[...]), jnp.where(even, got_a[...], got_b[...])
    spot = lane % SLOT == EDGE
    west = jnp.where(spot, west * own_west, west)
    east = jnp.where(spot, east * own_east, east)
    halves = [
        split(jnp.where(lane < 64, west, pltpu.roll(east, 64, 1))),
        split(jnp.where(lane < 64, pltpu.roll(west, 64, 1), east)),
    ]
    for line in range(GROUP):
        high, low = halves[line // 4]
        value = mul(high, halo_high[line % 4]) + mul(low, halo_high[line % 4]) + mul(high, halo_low[line % 4])
        filtered[:, line] = partial[:, line] + value.reshape(groups, 8, 2 * LANES)
    small = lax.broadcasted_iota(jnp.int32, (8, LANES), 1)
    second = (small < 64) | (small == EXTRA2)
    first = small == EXTRA1
    up_a = lax.axis_index("gy") % 2 == 0
    start_a, start_b = jnp.where(up_a, blocks - 1, 0), jnp.where(up_a, 0, blocks - 1)
    coarse_a, coarse_b = jnp.where(up_a, blocks - 2, 0), jnp.where(up_a, 0, blocks - 2)

    def level_step(level, _):
        def at(block, line):
            return filtered[level * blocks + block, line, :, LANES:]

        fourth = []
        for block in range(blocks):
            for half in range(2):
                fourth.append(sum(at(block, half * 4 + k) for k in range(1, 4)) + at(block, half * 4))
        for message, start, coarse in ((message_a, start_a, coarse_a), (message_b, start_b, coarse_b)):
            for line in range(GROUP):
                message[level, line] = filtered[level * blocks + start, line, :, :LANES]
                block, pair = coarse + line // 4, line % 4
                pairs = at(block, 2 * pair) + at(block, 2 * pair + 1)
                value = jnp.where(second, pairs, fourth[line])
                message[level, 8 + line] = jnp.where(first, at(start, line), value)
        return 0

    lax.fori_loop(0, levels, level_step, 0)


def convolve_own(load, count, low_edges, high_edges, store):
    rows = {}

    def row(r):
        if r not in rows:
            rows[r] = load(r)
        return rows[r]

    for r in range(count):
        value = double_taps[0] * row(r)
        for k in range(1, 9):
            near = [row(q) for q in (r - k, r + k) if 0 <= q < count]
            if near:
                value = value + double_taps[k] * (near[0] if len(near) == 1 else near[0] + near[1])
        if r < 4:
            fix = edge_taps[r][0] * row(0)
            for j in range(1, 4):
                fix = fix + edge_taps[r][j] * row(j)
            value = value - low_edges * fix
        for flag, end in high_edges:
            i = end - 1 - r
            if 0 <= i < 4:
                fix = edge_taps[i][0] * row(end - 1)
                for j in range(1, 4):
                    fix = fix + edge_taps[i][j] * row(end - 1 - j)
                value = value - flag * fix
        store(r, value)
        rows.pop(r - 8, None)


def own_rows_kernel(levels, height, filtered, east_a, east_b, fine, extra, coarse, edge):
    blocks = height // GROUP
    half, quarter = height // 2, height // 4
    gy, ny = lax.axis_index("gy"), lax.axis_size("gy")
    low, high = jnp.where(gy == 0, 1.0, 0.0).astype(F32), jnp.where(gy == ny - 1, 1.0, 0.0).astype(F32)
    even = lax.axis_index("gx") % 2 == 0
    lane = lax.broadcasted_iota(jnp.int32, (8, LANES), 1)
    second = (lane < 64) | (lane == EXTRA2)
    high_second, high_fourth = jnp.where(second, high, 0.0), jnp.where(second, 0.0, high)

    def level_step(level, _):
        def at(y, part):
            return filtered[level * blocks + y // 8, y % 8, :, part * LANES:(part + 1) * LANES]

        def store_to(ref):
            def store(r, value):
                ref[level, r] = value
            return store

        for part, ref in ((0, fine), (1, extra)):
            convolve_own(lambda r: at(r, part), height, low, [(high, height)], store_to(ref))

        def pair(r):
            return at(2 * r, 1) + at(2 * r + 1, 1)

        def load_coarse(r):
            return jnp.where(second, pair(r), pair(2 * r) + pair(2 * r + 1) if r < quarter else 0.0)

        convolve_own(load_coarse, half, low, [(high_second, half), (high_fourth, quarter)], store_to(coarse))
        for block in range(blocks):
            rows = tile(level * blocks + block)
            east = jnp.where(even, east_a[rows, :], east_b[rows, :])
            for line in range(GROUP):
                edge[level, block * GROUP + line] = pltpu.roll(east, (EXTRA1 - EDGE - line * SLOT) % LANES, 1)
        return 0

    lax.fori_loop(0, levels, level_step, 0)


def combine_kernel(chunk, levels, height, fine, extra, coarse, edge, got_a, got_b, members, refining, combined, first_row,
                   stacked, refined, weighted):
    blocks = height // GROUP
    half, quarter = height // 2, height // 4
    first = chunk * levels
    all_levels = members.shape[1]
    rows = members.reshape(8 * all_levels * height, LANES)
    up_a = lax.axis_index("gy") % 2 == 0
    lane = lax.broadcasted_iota(jnp.int32, (8, LANES), 1)
    second = (lane < 64) | (lane == EXTRA2)
    scale = jnp.where(second, jnp.float32(generations[1][1]), jnp.float32(generations[2][1]))
    weight = jnp.float32(generations[0][1])

    def outside(load):
        values = [load(j) for j in range(8)]
        result = []
        for i in range(8):
            total = double_taps[i + 1] * values[0]
            for j in range(1, 8 - i):
                total = total + double_taps[i + 1 + j] * values[j]
            result.append(total)
        return result

    def level_step(level, _):
        def north(r):
            return jnp.where(up_a, got_a[level, r], got_b[level, r])

        def south(r):
            return jnp.where(up_a, got_b[level, r], got_a[level, r])

        fine_south = outside(lambda j: south(7 - j))
        coarse_south = outside(lambda j: south(15 - j))
        fine_north = outside(north)
        coarse_north = outside(lambda j: north(8 + j))
        parts = []
        for r in range(half):
            value = coarse[level, r]
            if r < 8:
                value = value + coarse_south[r]
            if r < quarter:
                i = quarter - 1 - r
                value = value + jnp.where(second, 0.0, coarse_north[i])
            if r >= half - 8:
                value = value + jnp.where(second, coarse_north[half - 1 - r], 0.0)
            parts.append(value * scale)
        for r in range(half):
            stacked[r * 8:r * 8 + 8, :] = jnp.where(second, parts[r], parts[r // 2])
        refined[...] = exact_dot(stacked[...], refining[...])
        for block in range(blocks):
            for line in range(GROUP):
                y = block * GROUP + line
                member = rows[pl.ds((first + level) * height + y, 8, all_levels * height), :]
                for part, factor in ((0, member), (1, edge[level, y])):
                    value = (fine, extra)[part][level, y]
                    if y < 8:
                        value = value + (fine_south, coarse_south)[part][y]
                    if y >= height - 8:
                        value = value + (fine_north, coarse_north)[part][height - 1 - y]
                    value = weight * value + refined[y // 2 * 8:y // 2 * 8 + 8, part * LANES:(part + 1) * LANES]
                    weighted[part, line * 8:line * 8 + 8, :] = factor * value
            for part in range(2):
                lanes = slice(part * LANES, (part + 1) * LANES)
                total = weighted[part, pl.ds(0, 8, 8), :]
                for m in range(1, 8):
                    total = total + weighted[part, pl.ds(m, 8, 8), :]
                total = total * (1.0 / 7.0)
                combined[level, block * GROUP:(block + 1) * GROUP, lanes] = total
        return 0

    lax.fori_loop(0, levels, level_step, 0)
    for level in range(levels):
        first_row[level:level + 1, :] = combined[level, 0:1, :]


def interpolate_kernel(height, *refs):
    chunks = (len(refs) - 4) // 2
    interpolation, out, extended, rows = refs[-4:]
    levels = refs[0].shape[0]
    for chunk in range(chunks):
        combined, north = refs[chunk], refs[chunks + chunk]
        for level in range(levels):
            extended[0:height, :] = combined[level]
            extended[height:height + 1, :] = north[level:level + 1, :]
            for half in range(2):
                lanes = slice(half * LANES, (half + 1) * LANES)
                here = extended[0:height, lanes]
                rows[half, level, pl.ds(0, height, 2), :] = here
                rows[half, level, pl.ds(1, height, 2), :] = 0.5 * (here + extended[1:height + 1, lanes])
        value = exact_dot(
            jnp.concatenate([rows[half].reshape(levels * 2 * height, LANES) for half in range(2)], axis=1), interpolation[...]
        )
        out[chunk * levels:(chunk + 1) * levels] = value.reshape(levels, 2 * height, out.shape[2])


def partner(index, size, second):
    other = ((index + 1) ^ 1) - 1 if second else index ^ 1
    return other if 0 <= other < size else None


def swap(value, axis, second):
    size = lax.axis_size(axis)
    pairs = [(i, partner(i, size, second)) for i in range(size)]
    return lax.ppermute(value, axis, [(i, j) for i, j in pairs if j is not None])


def call(kernel, outs, scratch, cost, *args):
    vmem = pl.BlockSpec(memory_space=pltpu.VMEM)
    return pl.pallas_call(
        kernel,
        out_shape=tuple(jax.ShapeDtypeStruct(*out) if isinstance(out[0], tuple) else jax.ShapeDtypeStruct(out, F32) for out in outs),
        in_specs=[vmem for _ in args],
        out_specs=tuple(vmem for _ in outs),
        scratch_shapes=[pltpu.VMEM(shape, F32) for shape in scratch],
        compiler_params=pltpu.CompilerParams(vmem_limit_bytes=VMEM_LIMIT),
        cost_estimate=pl.CostEstimate(flops=cost, bytes_accessed=2**20, transcendentals=0),
    )(*args)


def halves_of(table):
    high = table.astype(np.float32).astype(BF16)
    return jnp.asarray(high), jnp.asarray((table.astype(np.float32) - high.astype(np.float32)).astype(BF16))


def shards(gradient, members):
    all_levels, fine_height, fine_width = gradient.shape
    count, _, height, width = members.shape
    assert count == 8 and width == LANES and height == 32 and lax.axis_size("gx") > 1
    assert all_levels % CHUNKS == 0
    levels = all_levels // CHUNKS
    groups = levels * height // GROUP
    ny = lax.axis_size("gy")

    up = [(i, i + 1) for i in range(ny - 1)]
    south = lax.ppermute(gradient[:, -1, :], "gy", up)

    columns = [column_table(width, i == 0, i == 2) for i in range(3)]
    high_tables, low_tables = halves_of(np.stack([table[:width] for table in columns]))
    halo_highs, halo_lows = halves_of(np.stack([halo_table(table, width) for table in columns]))
    restrict = jnp.asarray(restriction_table(width), BF16)
    packing = jnp.asarray(packing_table(width), BF16).reshape(GROUP * width, 2 * LANES)
    refining = jnp.asarray(refining_table(width), BF16)
    interpolation = jnp.asarray(interpolation_table(width), BF16)
    flops = 10**9 // CHUNKS

    packed = [
        call(
            functools.partial(pack_kernel, chunk, levels, height),
            [(GROUP, groups * 8, LANES), (groups * 8, LANES), (groups * 8, LANES)],
            [(2, levels, 8 + 2 * height, LANES), (2, height, LANES)],
            flops, gradient, members, south, restrict, packing,
        )
        for chunk in range(CHUNKS)
    ]
    got = [(swap(own_a, "gx", False), swap(own_b, "gx", True)) for _, own_a, own_b in packed]
    partials = [
        call(
            functools.partial(own_columns_kernel, levels, height),
            [(groups, GROUP, 8, 2 * LANES), ((4, LANES, 2 * LANES), BF16), ((4, LANES, 2 * LANES), BF16)],
            [],
            flops, products, high_tables, low_tables, halo_highs, halo_lows,
        )
        for products, _, _ in packed
    ]
    filtered = [
        call(
            functools.partial(columns_kernel, levels, height),
            [(groups, GROUP, 8, 2 * LANES), (levels, 16, 8, LANES), (levels, 16, 8, LANES)],
            [],
            flops, partials[chunk][0], *packed[chunk][1:], *got[chunk], *partials[chunk][1:],
        )
        for chunk in range(CHUNKS)
    ]
    far = [(swap(rows_a, "gy", False), swap(rows_b, "gy", True)) for _, rows_a, rows_b in filtered]
    own = [
        call(
            functools.partial(own_rows_kernel, levels, height),
            [(levels, height, 8, LANES), (levels, height, 8, LANES), (levels, height // 2, 8, LANES), (levels, height, 8, LANES)],
            [],
            flops, filtered[chunk][0], *got[chunk],
        )
        for chunk in range(CHUNKS)
    ]
    combined, first_rows = zip(*(
        call(
            functools.partial(combine_kernel, chunk, levels, height),
            [(levels, height, 2 * LANES), (levels, 2 * LANES)],
            [(height // 2 * 8, LANES), (height // 2 * 8, 2 * LANES), (2, 64, LANES)],
            flops, *own[chunk], *far[chunk], members, refining,
        )
        for chunk in range(CHUNKS)
    ))
    norths = [lax.ppermute(row, "gy", [(j, i) for i, j in up]) for row in first_rows]
    (out,) = call(
        functools.partial(interpolate_kernel, height),
        [(all_levels, fine_height, fine_width)],
        [(height + 8, 2 * LANES), (2, levels, 2 * height, LANES)],
        flops, *combined, *norths, interpolation,
    )
    return out


def solution(mesh):
    in_specs = (P(None, "gy", "gx"), P(None, None, "gy", "gx"))
    out_specs = P(None, "gy", "gx")
    return jax.shard_map(shards, mesh=mesh, in_specs=in_specs, out_specs=out_specs, check_vma=False)
```

```python
import functools

import jax
import jax.numpy as jnp
import numpy as np
from jax import lax
from jax.experimental import pallas as pl
from jax.experimental.pallas import tpu as pltpu
from jax.sharding import PartitionSpec as P

beta_raw = [(1.0 - (offset - 4) ** 2 / 25.0) ** 2 for offset in range(9)]
beta_taps = [value / sum(beta_raw) for value in beta_raw]
generations = ((1, 0.5), (2, 0.075), (4, 0.0125))

LANES = 128
GROUP = 8
SLOT = 16
EDGE = 15
COLUMN = 32
CHUNKS = 2
VMEM_LIMIT = 20 * 2**20
BF16, F32 = jnp.bfloat16, jnp.float32
double_taps = [
    sum(beta_taps[k + 4] * beta_taps[offset - k + 4] for k in range(-4, 5) if -4 <= offset - k <= 4) for offset in range(9)
]
edge_taps = [
    [sum(beta_taps[i - k + 4] * beta_taps[k - j + 4] for k in range(-4, 0) if i - k <= 4 and j - k <= 4) for j in range(4)]
    for i in range(4)
]

def twice_filter(width, first, last):
    low, high = (0 if first else -99), (width - 1 if last else width + 99)
    table = np.zeros((width + 17, width + 1))
    for source in range(-8, width + 9):
        if not low <= source <= high:
            continue
        for middle in range(source - 4, source + 5):
            if not low <= middle <= high:
                continue
            for target in range(max(0, middle - 4), min(width, middle + 4) + 1):
                if target <= high:
                    table[source + 8, target] += beta_taps[middle - source + 4] * beta_taps[target - middle + 4]
    return table


def column_table(width, first, last):
    filters = {factor: twice_filter(width // factor, first, last) for factor, _ in generations}
    base = {1: 0, 2: LANES, 4: LANES + width // 2}

    def row(places):
        out = np.zeros(2 * LANES)
        for factor, place in places.items():
            count = width // factor
            out[base[factor]:base[factor] + count] += filters[factor][place + 8, :count]
        return out

    rows = [row({1: c, 2: c // 2, 4: c // 4}) for c in range(width)]
    rows += [row({1: c, 2: c // 2, 4: c // 4}) for c in range(-8, 0)]
    rows += [row({2: c, 4: c // 2}) for c in range(-8, -4)]
    rows += [row({4: c}) for c in range(-8, -4)]
    rows += [row({1: c, 2: c // 2, 4: c // 4}) for c in range(width, width + 8)] + [row({1: width + 8})]
    half, quarter = width // 2, width // 4
    rows += [row({2: c, 4: c // 2}) for c in range(half + 4, half + 8)] + [row({2: half + 8})]
    rows += [row({4: c}) for c in range(quarter + 4, quarter + 9)]
    return np.stack(rows)


def message_lanes():
    places = []
    for line in range(GROUP):
        places += [(0, line * SLOT + c, c, 1, line) for c in range(8)]
        places += [(1, line * SLOT + c, 16 + c, 1, line) for c in range(9)]
        if line % 2 == 0:
            places += [(0, line * SLOT + 8 + c, 8 + c, 2, line) for c in range(4)]
            places += [(1, line * SLOT + 9 + c, 25 + c, 2, line) for c in range(5)]
        if line % 4 == 1:
            places += [(0, line * SLOT + 8 + c, 12 + c, 4, line - 1) for c in range(4)]
            places += [(1, line * SLOT + 9 + c, 30 + c, 4, line - 1) for c in range(5)]
    return places


def packing_table(width):
    table = np.zeros((GROUP, width, 2 * LANES), np.float32)
    east = list(range(width - 8, width)) + [width // 2 - 8 + c for c in range(4)] + [width // 4 - 8 + c for c in range(4)]
    west = list(range(9)) + [4 + c for c in range(5)] + [4 + c for c in range(5)]
    for side, lane, compact, factor, line in message_lanes():
        start = (west[compact - 16] if side else east[compact]) * factor
        table[line:line + factor, start:start + factor, side * LANES + lane] = 1.0
    return table


def halo_table(columns, width):
    table = np.zeros((2, 2 * SLOT, 2 * LANES))
    outer = columns[width:]
    for side, lane, compact, factor, line in message_lanes():
        if line < 2 and lane < 2 * SLOT:
            table[lane // SLOT, side * SLOT + lane % SLOT] = outer[compact]
    table[:, EDGE] = columns[0]
    table[:, SLOT + EDGE] = outer[16]
    return table


def restriction_table(width):
    table = np.zeros((2 * width, 2 * LANES), np.float32)
    for i in range(width):
        table[2 * i, i] += 1.0
        table[2 * i + 1, i] += 0.5
        table[2 * i + 1, i + 1] += 0.5
    return table


def refining_table(width):
    table = np.zeros((LANES, LANES), np.float32)
    for i in range(width):
        table[i // 2, i] = 1.0
        table[width // 2 + i // 4, i] = 1.0
    return table


def column_lane(factor, row):
    count = GROUP // factor
    return row // count * COLUMN + {1: 0, 2: 8, 4: 12}[factor] + row % count


def column_filter_table(width):
    table = np.zeros((2 * LANES, LANES))
    filters = {factor: twice_filter(width // factor, False, False)[:, width // factor] for factor, _ in generations}
    low = [width - 8 + c for c in range(8)] + [width // 2 - 8 + c for c in range(4)] + [width // 4 - 8 + c for c in range(4)]
    high = [width + c for c in range(9)] + [width // 2 + 4 + c for c in range(5)] + [width // 4 + 4 + c for c in range(5)]
    ends = {(1, 16 + 8): 1, (2, 25 + 4): 2}
    for side, lane, compact, factor, line in message_lanes():
        place = (high[compact - 16] if side else low[compact]) * factor
        for generation, _ in generations:
            if generation >= factor and generation <= ends.get((factor, compact), 4):
                weight = filters[generation][place // generation + 8]
                table[side * LANES + lane, column_lane(generation, line // generation)] += weight
    for line in range(GROUP):
        for generation, _ in generations:
            weight = filters[generation][width // generation + 8]
            table[LANES + line * SLOT + EDGE, column_lane(generation, line // generation)] += weight
    return table


def column_rows_table(height, first, last):
    table = np.zeros((3, LANES, LANES))
    for factor, weight in generations:
        count = height // factor
        filters = twice_filter(count, first, last)
        for row in range(height):
            for source in range(-8, count + 8):
                kind, place = (1, source + count) if source < 0 else (2, source - count) if source >= count else (0, source)
                table[kind, column_lane(factor, place), row] += weight * filters[source + 8, row // factor]
    return table


def edge_choice_table():
    table = np.zeros((LANES, LANES), np.float32)
    for line in range(GROUP):
        table[line * SLOT + EDGE, line] = 1.0
    return table


def interpolation_table(width):
    table = np.zeros((2 * LANES, 2 * width), np.float32)
    for i in range(width):
        table[i, 2 * i] = 1.0
        table[i, 2 * i + 1] = 0.5
        table[LANES + i, 2 * i + 1] = 0.5
    return table


def split(value):
    high = value.astype(BF16)
    return high, (value - high.astype(F32)).astype(BF16)


def mul(a, b):
    return jnp.dot(a, b, preferred_element_type=F32)


def exact_dot(value, table):
    high, low = split(value)
    return mul(high, table) + mul(low, table)


def three_dots(value, high_table, low_table):
    high, low = split(value)
    return mul(high, high_table) + mul(low, high_table) + mul(high, low_table)


def column_case():
    gx, nx = lax.axis_index("gx"), lax.axis_size("gx")
    return jnp.where(gx == 0, 0, jnp.where(gx == nx - 1, 2, 1))


def tile(index):
    return pl.ds(pl.multiple_of(index * 8, 8), 8)


def prepare_kernel(height, gradient, members, restrict, across, turned, edges, fine, raw, table, sems):
    blocks = height // GROUP
    levels = members.shape[1]
    part = levels // 4
    copies = [pltpu.make_async_copy(restrict, table, sems.at[8])]
    for i in range(4):
        span = pl.ds(i * part, part)
        copies.append(pltpu.make_async_copy(gradient.at[span], fine.at[span], sems.at[i]))
    for i in range(4):
        span = pl.ds(i * part, part)
        copies.append(pltpu.make_async_copy(members.at[:, span], raw.at[:, span], sems.at[4 + i]))
    for copy in copies:
        copy.start()
    copies[0].wait()
    for half in range(2):
        across[half, :, 0:8, :] = jnp.zeros((levels, 8, LANES), F32)
    for i in range(4):
        copies[1 + i].wait()
        value = exact_dot(fine[i * part:(i + 1) * part].reshape(part * 2 * height, fine.shape[2]), table[...])
        value = value.reshape(part, 2 * height, 2 * LANES)
        for half in range(2):
            across[half, i * part:(i + 1) * part, 8:, :] = value[:, :, half * LANES:(half + 1) * LANES]
    rows = raw.reshape(8 * levels * height, LANES)
    lane = lax.broadcasted_iota(jnp.int32, (GROUP, LANES), 1)

    def level_step(level, _):
        for block in range(blocks):
            edge = jnp.zeros((GROUP, LANES), F32)
            for line in range(GROUP):
                y = block * GROUP + line
                member = rows[pl.ds(level * height + y, 8, levels * height), :]
                turned[level, y] = member
                spot = line * SLOT + EDGE
                edge = jnp.where(lane == spot, pltpu.roll(member, spot, 1), edge)
            edges[tile(level * blocks + block), :] = edge
        return 0

    for i in range(4):
        copies[5 + i].wait()
        lax.fori_loop(i * part, (i + 1) * part, level_step, 0)


def pack_kernel(chunk, levels, height, across, turned, edges, south, restrict, packing, products, message_a, message_b, coarse, below):
    blocks = height // GROUP
    first = chunk * levels
    value = exact_dot(south[...], restrict[...])
    for half in range(2):
        below[half] = value[:, half * LANES:(half + 1) * LANES]
    lane = lax.broadcasted_iota(jnp.int32, (GROUP, LANES), 1)
    line_of = lax.broadcasted_iota(jnp.int32, (GROUP, LANES), 0)
    top = lax.broadcasted_iota(jnp.int32, (height, LANES), 0) == 0

    def level_step(level, _):
        for half in range(2):
            under = jnp.broadcast_to(below[half, pl.ds(first + level, 1), :], (height, LANES))
            under = jnp.where(top, under, across[half, first + level, pl.ds(7, height, 2), :])
            coarse[half] = across[half, first + level, pl.ds(8, height, 2), :] + 0.5 * (
                across[half, first + level, pl.ds(9, height, 2), :] + under
            )
        for block in range(blocks):
            place_rows = tile(level * blocks + block)
            for line in range(GROUP):
                y = block * GROUP + line
                products[line, place_rows, :] = turned[first + level, y] * coarse[0, y:y + 1, :]
            column = jnp.broadcast_to(coarse[1, block * GROUP:(block + 1) * GROUP, 0:1], (GROUP, LANES))
            column = jnp.sum(jnp.where(lane == line_of * SLOT + EDGE, column, 0.0), axis=0, keepdims=True)
            message_a[place_rows, :] = jnp.broadcast_to(column, (GROUP, LANES))
        return 0

    lax.fori_loop(0, levels, level_step, 0)
    total = jnp.zeros((levels * blocks * 8, 2 * LANES), F32)
    for line in range(0, GROUP, 2):
        value = jnp.concatenate([products[line], products[line + 1]], axis=1)
        total = total + exact_dot(value, packing[line * LANES:(line + 2) * LANES, :])
    to_east = total[:, :LANES] + message_a[...]
    to_west = total[:, LANES:] + edges[first * blocks * 8:(first + levels) * blocks * 8, :]
    even = lax.axis_index("gx") % 2 == 0
    message_a[...] = jnp.where(even, to_east, to_west)
    message_b[...] = jnp.where(even, to_west, to_east)


def own_columns_kernel(levels, height, products, high_tables, low_tables, halo_highs, halo_lows, filtered, halo_high, halo_low):
    groups = levels * height // GROUP
    case = column_case()
    for variant in range(4):
        for source, target in ((halo_highs, halo_high), (halo_lows, halo_low)):
            target[variant] = jnp.zeros((LANES, 2 * LANES), BF16)
            kind = variant % 2
            target[variant, variant * SLOT:(variant + 1) * SLOT, :] = source[case, kind, :SLOT, :]
            target[variant, 64 + variant * SLOT:64 + (variant + 1) * SLOT, :] = source[case, kind, SLOT:, :]
    high, low = high_tables[case], low_tables[case]
    for line in range(GROUP):
        filtered[:, line] = three_dots(products[line], high, low).reshape(groups, 8, 2 * LANES)


def columns_kernel(levels, height, partial, own_a, own_b, got_a, got_b, halo_high, halo_low, beyond_high, beyond_low, choice,
                   filtered, message_a, message_b, factors):
    blocks = height // GROUP
    groups = levels * blocks
    lane = lax.broadcasted_iota(jnp.int32, (groups * 8, LANES), 1)
    even = lax.axis_index("gx") % 2 == 0
    own_east, own_west = jnp.where(even, own_a[...], own_b[...]), jnp.where(even, own_b[...], own_a[...])
    west, east = jnp.where(even, got_b[...], got_a[...]), jnp.where(even, got_a[...], got_b[...])
    spot = lane % SLOT == EDGE
    chosen = exact_dot(east, choice[...]).reshape(levels, blocks, 8, LANES)
    total = chosen[:, 0]
    for block in range(1, blocks):
        total = total + pltpu.roll(chosen[:, block], block * GROUP, 2)
    factors[...] = total
    west = jnp.where(spot, west * own_west, west)
    east = jnp.where(spot, east * own_east, east)
    inside = jnp.where(lax.axis_index("gx") == lax.axis_size("gx") - 1, 0.0, 1.0).astype(F32)
    beyond = three_dots(jnp.concatenate([own_east, east], axis=1), beyond_high[...], beyond_low[...])
    beyond = (beyond * inside).reshape(levels, blocks, 8, LANES)
    total = beyond[:, 0]
    for block in range(1, blocks):
        total = total + pltpu.roll(beyond[:, block], block * COLUMN, 2)
    for message in (message_a, message_b):
        message[levels * 16:] = total
    halves = [
        split(jnp.where(lane < 64, west, pltpu.roll(east, 64, 1))),
        split(jnp.where(lane < 64, pltpu.roll(west, 64, 1), east)),
    ]
    for line in range(GROUP):
        high, low = halves[line // 4]
        value = mul(high, halo_high[line % 4]) + mul(low, halo_high[line % 4]) + mul(high, halo_low[line % 4])
        filtered[:, line] = partial[:, line] + value.reshape(groups, 8, 2 * LANES)
    small = lax.broadcasted_iota(jnp.int32, (8, LANES), 1)
    second = small < 64
    up_a = lax.axis_index("gy") % 2 == 0
    start_a, start_b = jnp.where(up_a, blocks - 1, 0), jnp.where(up_a, 0, blocks - 1)
    coarse_a, coarse_b = jnp.where(up_a, blocks - 2, 0), jnp.where(up_a, 0, blocks - 2)

    def level_step(level, _):
        def at(block, line):
            return filtered[level * blocks + block, line, :, LANES:]

        fourth = []
        for block in range(blocks):
            for half in range(2):
                fourth.append(sum(at(block, half * 4 + k) for k in range(1, 4)) + at(block, half * 4))
        for message, start, coarse in ((message_a, start_a, coarse_a), (message_b, start_b, coarse_b)):
            for line in range(GROUP):
                message[level * 16 + line] = filtered[level * blocks + start, line, :, :LANES]
                block, pair = coarse + line // 4, line % 4
                pairs = at(block, 2 * pair) + at(block, 2 * pair + 1)
                message[level * 16 + 8 + line] = jnp.where(second, pairs, fourth[line])
        return 0

    lax.fori_loop(0, levels, level_step, 0)


def convolve_own(load, count, low_edges, high_edges, store):
    rows = {}

    def row(r):
        if r not in rows:
            rows[r] = load(r)
        return rows[r]

    for r in range(count):
        value = double_taps[0] * row(r)
        for k in range(1, 9):
            near = [row(q) for q in (r - k, r + k) if 0 <= q < count]
            if near:
                value = value + double_taps[k] * (near[0] if len(near) == 1 else near[0] + near[1])
        if r < 4:
            fix = edge_taps[r][0] * row(0)
            for j in range(1, 4):
                fix = fix + edge_taps[r][j] * row(j)
            value = value - low_edges * fix
        for flag, end in high_edges:
            i = end - 1 - r
            if 0 <= i < 4:
                fix = edge_taps[i][0] * row(end - 1)
                for j in range(1, 4):
                    fix = fix + edge_taps[i][j] * row(end - 1 - j)
                value = value - flag * fix
        store(r, value)
        rows.pop(r - 8, None)


def own_rows_kernel(levels, height, filtered, fine, coarse):
    blocks = height // GROUP
    half, quarter = height // 2, height // 4
    gy, ny = lax.axis_index("gy"), lax.axis_size("gy")
    low, high = jnp.where(gy == 0, 1.0, 0.0).astype(F32), jnp.where(gy == ny - 1, 1.0, 0.0).astype(F32)
    second = lax.broadcasted_iota(jnp.int32, (8, LANES), 1) < 64
    high_second, high_fourth = jnp.where(second, high, 0.0), jnp.where(second, 0.0, high)

    def level_step(level, _):
        def at(y, part):
            return filtered[level * blocks + y // 8, y % 8, :, part * LANES:(part + 1) * LANES]

        def store_to(ref):
            def store(r, value):
                ref[level, r] = value
            return store

        convolve_own(lambda r: at(r, 0), height, low, [(high, height)], store_to(fine))

        def pair(r):
            return at(2 * r, 1) + at(2 * r + 1, 1)

        def load_coarse(r):
            return jnp.where(second, pair(r), pair(2 * r) + pair(2 * r + 1) if r < quarter else 0.0)

        convolve_own(load_coarse, half, low, [(high_second, half), (high_fourth, quarter)], store_to(coarse))
        return 0

    lax.fori_loop(0, levels, level_step, 0)


def combine_kernel(chunk, levels, height, fine, coarse, got_a, got_b, own_rows, factors, turned, refining,
                   row_highs, row_lows, combined, beyond, first_row, stacked, refined, weighted):
    blocks = height // GROUP
    half, quarter = height // 2, height // 4
    first = chunk * levels
    up_a = lax.axis_index("gy") % 2 == 0
    gy, ny = lax.axis_index("gy"), lax.axis_size("gy")
    second = lax.broadcasted_iota(jnp.int32, (8, LANES), 1) < 64
    scale = jnp.where(second, jnp.float32(generations[1][1]), jnp.float32(generations[2][1]))
    weight = jnp.float32(generations[0][1])

    def side(value):
        return value.reshape(levels * 8, LANES)

    case = jnp.where(gy == 0, 0, jnp.where(gy == ny - 1, 2, 1))
    far_a, far_b = side(got_a[levels * 16:]), side(got_b[levels * 16:])
    value = three_dots(side(own_rows[levels * 16:]), row_highs[case, 0], row_lows[case, 0])
    value = value + three_dots(jnp.where(up_a, far_b, far_a), row_highs[case, 1], row_lows[case, 1])
    value = value + three_dots(jnp.where(up_a, far_a, far_b), row_highs[case, 2], row_lows[case, 2])
    beyond[...] = jnp.sum(value.reshape(levels, 8, LANES) * factors[...], axis=1) * (1.0 / 7.0)

    def outside(load):
        values = [load(j) for j in range(8)]
        result = []
        for i in range(8):
            total = double_taps[i + 1] * values[0]
            for j in range(1, 8 - i):
                total = total + double_taps[i + 1 + j] * values[j]
            result.append(total)
        return result

    def level_step(level, _):
        def north(r):
            return jnp.where(up_a, got_a[level * 16 + r], got_b[level * 16 + r])

        def south(r):
            return jnp.where(up_a, got_b[level * 16 + r], got_a[level * 16 + r])

        fine_south = outside(lambda j: south(7 - j))
        coarse_south = outside(lambda j: south(15 - j))
        fine_north = outside(north)
        coarse_north = outside(lambda j: north(8 + j))
        parts = []
        for r in range(half):
            value = coarse[level, r]
            if r < 8:
                value = value + coarse_south[r]
            if r < quarter:
                i = quarter - 1 - r
                value = value + jnp.where(second, 0.0, coarse_north[i])
            if r >= half - 8:
                value = value + jnp.where(second, coarse_north[half - 1 - r], 0.0)
            parts.append(value * scale)
        for r in range(half):
            stacked[r * 8:r * 8 + 8, :] = jnp.where(second, parts[r], parts[r // 2])
        refined[...] = exact_dot(stacked[...], refining[...])
        for block in range(blocks):
            for line in range(GROUP):
                y = block * GROUP + line
                value = fine[level, y]
                if y < 8:
                    value = value + fine_south[y]
                if y >= height - 8:
                    value = value + fine_north[height - 1 - y]
                value = weight * value + refined[y // 2 * 8:y // 2 * 8 + 8, :]
                weighted[line * 8:line * 8 + 8, :] = turned[first + level, y] * value
            total = weighted[pl.ds(0, 8, 8), :]
            for m in range(1, 8):
                total = total + weighted[pl.ds(m, 8, 8), :]
            combined[level, block * GROUP:(block + 1) * GROUP, :] = total * (1.0 / 7.0)
        return 0

    lax.fori_loop(0, levels, level_step, 0)
    for level in range(levels):
        first_row[level:level + 1, :LANES] = combined[level, 0:1, :]
    first_row[:, LANES:] = beyond[...]


def interpolate_kernel(height, *refs):
    chunks = (len(refs) - 4) // 3
    interpolation, out, extended, rows = refs[-4:]
    levels = refs[0].shape[0]
    lane = lax.broadcasted_iota(jnp.int32, (height, LANES), 1)
    line = lax.broadcasted_iota(jnp.int32, (height, LANES), 0)
    row_lane = lax.broadcasted_iota(jnp.int32, (1, LANES), 1)
    for chunk in range(chunks):
        combined, beyond, north = refs[chunk], refs[chunks + chunk], refs[2 * chunks + chunk]
        for level in range(levels):
            here = combined[level]
            last = jnp.broadcast_to(beyond[level:level + 1, :], (height, LANES))
            last = jnp.sum(jnp.where(lane == line, last, 0.0), axis=1, keepdims=True)
            after = north[level:level + 1, :LANES]
            corner = jnp.broadcast_to(north[level:level + 1, LANES:LANES + 1], (1, LANES))
            extended[0, 0:height, :] = here
            extended[0, height:height + 1, :] = after
            extended[1, 0:height, :] = jnp.where(lane == LANES - 1, last, pltpu.roll(here, LANES - 1, 1))
            extended[1, height:height + 1, :] = jnp.where(row_lane == LANES - 1, corner, pltpu.roll(after, LANES - 1, 1))
            for half in range(2):
                value = extended[half, 0:height, :]
                rows[half, level, pl.ds(0, height, 2), :] = value
                rows[half, level, pl.ds(1, height, 2), :] = 0.5 * (value + extended[half, 1:height + 1, :])
        value = exact_dot(
            jnp.concatenate([rows[half].reshape(levels * 2 * height, LANES) for half in range(2)], axis=1), interpolation[...]
        )
        out[chunk * levels:(chunk + 1) * levels] = value.reshape(levels, 2 * height, out.shape[2])


def partner(index, size, second):
    other = ((index + 1) ^ 1) - 1 if second else index ^ 1
    return other if 0 <= other < size else None


def swap(value, axis, second):
    size = lax.axis_size(axis)
    pairs = [(i, partner(i, size, second)) for i in range(size)]
    return lax.ppermute(value, axis, [(i, j) for i, j in pairs if j is not None])


def call(kernel, outs, scratch, cost, *args, in_hbm=0):
    vmem = pl.BlockSpec(memory_space=pltpu.VMEM)
    return pl.pallas_call(
        kernel,
        out_shape=tuple(jax.ShapeDtypeStruct(*out) if isinstance(out[0], tuple) else jax.ShapeDtypeStruct(out, F32) for out in outs),
        in_specs=[pl.BlockSpec(memory_space=pltpu.HBM) if i < in_hbm else vmem for i in range(len(args))],
        out_specs=tuple(vmem for _ in outs),
        scratch_shapes=[pltpu.VMEM(shape, F32) if isinstance(shape, tuple) else shape for shape in scratch],
        compiler_params=pltpu.CompilerParams(vmem_limit_bytes=VMEM_LIMIT),
        cost_estimate=pl.CostEstimate(flops=cost, bytes_accessed=2**20, transcendentals=0),
    )(*args)


def halves_of(table):
    high = table.astype(np.float32).astype(BF16)
    return jnp.asarray(high), jnp.asarray((table.astype(np.float32) - high.astype(np.float32)).astype(BF16))


def shards(gradient, members):
    all_levels, fine_height, fine_width = gradient.shape
    count, _, height, width = members.shape
    assert count == 8 and width == LANES and height == 32 and lax.axis_size("gx") > 1
    assert all_levels % CHUNKS == 0
    levels = all_levels // CHUNKS
    groups = levels * height // GROUP
    ny = lax.axis_size("gy")

    up = [(i, i + 1) for i in range(ny - 1)]
    south = lax.ppermute(gradient[:, -1, :], "gy", up)

    columns = [column_table(width, i == 0, i == 2) for i in range(3)]
    high_tables, low_tables = halves_of(np.stack([table[:width] for table in columns]))
    halo_highs, halo_lows = halves_of(np.stack([halo_table(table, width) for table in columns]))
    restrict = jnp.asarray(restriction_table(width), BF16)
    packing = jnp.asarray(packing_table(width), BF16).reshape(GROUP * width, 2 * LANES)
    refining = jnp.asarray(refining_table(width), BF16)
    interpolation = jnp.asarray(interpolation_table(width), BF16)
    beyond_high, beyond_low = halves_of(column_filter_table(width))
    row_highs, row_lows = halves_of(np.stack([column_rows_table(height, i == 0, i == 2) for i in range(3)]))
    choice = jnp.asarray(edge_choice_table(), BF16)
    flops = 10**9 // CHUNKS
    far_rows = (levels * 17, 8, LANES)

    across, turned, edges = call(
        functools.partial(prepare_kernel, height),
        [(2, all_levels, 8 + 2 * height, LANES), (all_levels, height, 8, LANES), (all_levels * height, LANES)],
        [gradient.shape, members.shape, pltpu.VMEM(restrict.shape, BF16), pltpu.SemaphoreType.DMA((9,))],
        flops, gradient, members, restrict, in_hbm=3,
    )
    packed = [
        call(
            functools.partial(pack_kernel, chunk, levels, height),
            [(GROUP, groups * 8, LANES), (groups * 8, LANES), (groups * 8, LANES)],
            [(2, height, LANES), (2, all_levels, LANES)],
            flops, across, turned, edges, south, restrict, packing,
        )
        for chunk in range(CHUNKS)
    ]
    got = [(swap(own_a, "gx", False), swap(own_b, "gx", True)) for _, own_a, own_b in packed]
    partials = [
        call(
            functools.partial(own_columns_kernel, levels, height),
            [(groups, GROUP, 8, 2 * LANES), ((4, LANES, 2 * LANES), BF16), ((4, LANES, 2 * LANES), BF16)],
            [],
            flops, products, high_tables, low_tables, halo_highs, halo_lows,
        )
        for products, _, _ in packed
    ]
    filtered = [
        call(
            functools.partial(columns_kernel, levels, height),
            [(groups, GROUP, 8, 2 * LANES), far_rows, far_rows, (levels, 8, LANES)],
            [],
            flops, partials[chunk][0], *packed[chunk][1:], *got[chunk], *partials[chunk][1:], beyond_high, beyond_low, choice,
        )
        for chunk in range(CHUNKS)
    ]
    far = [(swap(rows_a, "gy", False), swap(rows_b, "gy", True)) for _, rows_a, rows_b, _ in filtered]
    own = [
        call(
            functools.partial(own_rows_kernel, levels, height),
            [(levels, height, 8, LANES), (levels, height // 2, 8, LANES)],
            [],
            flops, filtered[chunk][0],
        )
        for chunk in range(CHUNKS)
    ]
    combined, beyond, first_rows = zip(*(
        call(
            functools.partial(combine_kernel, chunk, levels, height),
            [(levels, height, LANES), (levels, LANES), (levels, 2 * LANES)],
            [(height // 2 * 8, LANES), (height // 2 * 8, LANES), (64, LANES)],
            flops, *own[chunk], *far[chunk], filtered[chunk][1], filtered[chunk][3], turned, refining, row_highs, row_lows,
        )
        for chunk in range(CHUNKS)
    ))
    norths = [lax.ppermute(row, "gy", [(j, i) for i, j in up]) for row in first_rows]
    (out,) = call(
        functools.partial(interpolate_kernel, height),
        [(all_levels, fine_height, fine_width)],
        [(2, height + 8, LANES), (2, levels, 2 * height, LANES)],
        flops, *combined, *beyond, *norths, interpolation,
    )
    return out


def solution(mesh):
    in_specs = (P(None, "gy", "gx"), P(None, None, "gy", "gx"))
    out_specs = P(None, "gy", "gx")
    return jax.shard_map(shards, mesh=mesh, in_specs=in_specs, out_specs=out_specs, check_vma=False)
```

```python
import functools

import jax
import jax.numpy as jnp
import numpy as np
from jax import lax
from jax.experimental import pallas as pl
from jax.experimental.pallas import tpu as pltpu
from jax.sharding import PartitionSpec as P

beta_raw = [(1.0 - (offset - 4) ** 2 / 25.0) ** 2 for offset in range(9)]
beta_taps = [value / sum(beta_raw) for value in beta_raw]
generations = ((1, 0.5), (2, 0.075), (4, 0.0125))

LANES = 128
GROUP = 8
SLOT = 16
EDGE = 15
COLUMN = 32
CHUNKS = 2
VMEM_LIMIT = 20 * 2**20
BF16, F32 = jnp.bfloat16, jnp.float32
double_taps = [
    sum(beta_taps[k + 4] * beta_taps[offset - k + 4] for k in range(-4, 5) if -4 <= offset - k <= 4) for offset in range(9)
]
edge_taps = [
    [sum(beta_taps[i - k + 4] * beta_taps[k - j + 4] for k in range(-4, 0) if i - k <= 4 and j - k <= 4) for j in range(4)]
    for i in range(4)
]

def twice_filter(width, first, last):
    low, high = (0 if first else -99), (width - 1 if last else width + 99)
    table = np.zeros((width + 17, width + 1))
    for source in range(-8, width + 9):
        if not low <= source <= high:
            continue
        for middle in range(source - 4, source + 5):
            if not low <= middle <= high:
                continue
            for target in range(max(0, middle - 4), min(width, middle + 4) + 1):
                if target <= high:
                    table[source + 8, target] += beta_taps[middle - source + 4] * beta_taps[target - middle + 4]
    return table


def column_table(width, first, last):
    filters = {factor: twice_filter(width // factor, first, last) for factor, _ in generations}
    base = {1: 0, 2: LANES, 4: LANES + width // 2}

    def row(places):
        out = np.zeros(2 * LANES)
        for factor, place in places.items():
            count = width // factor
            out[base[factor]:base[factor] + count] += filters[factor][place + 8, :count]
        return out

    rows = [row({1: c, 2: c // 2, 4: c // 4}) for c in range(width)]
    rows += [row({1: c, 2: c // 2, 4: c // 4}) for c in range(-8, 0)]
    rows += [row({2: c, 4: c // 2}) for c in range(-8, -4)]
    rows += [row({4: c}) for c in range(-8, -4)]
    rows += [row({1: c, 2: c // 2, 4: c // 4}) for c in range(width, width + 8)] + [row({1: width + 8})]
    half, quarter = width // 2, width // 4
    rows += [row({2: c, 4: c // 2}) for c in range(half + 4, half + 8)] + [row({2: half + 8})]
    rows += [row({4: c}) for c in range(quarter + 4, quarter + 9)]
    return np.stack(rows)


def message_lanes():
    places = []
    for line in range(GROUP):
        places += [(0, line * SLOT + c, c, 1, line) for c in range(8)]
        places += [(1, line * SLOT + c, 16 + c, 1, line) for c in range(9)]
        if line % 2 == 0:
            places += [(0, line * SLOT + 8 + c, 8 + c, 2, line) for c in range(4)]
            places += [(1, line * SLOT + 9 + c, 25 + c, 2, line) for c in range(5)]
        if line % 4 == 1:
            places += [(0, line * SLOT + 8 + c, 12 + c, 4, line - 1) for c in range(4)]
            places += [(1, line * SLOT + 9 + c, 30 + c, 4, line - 1) for c in range(5)]
    return places


def packing_table(width):
    table = np.zeros((GROUP, width, 2 * LANES), np.float32)
    east = list(range(width - 8, width)) + [width // 2 - 8 + c for c in range(4)] + [width // 4 - 8 + c for c in range(4)]
    west = list(range(9)) + [4 + c for c in range(5)] + [4 + c for c in range(5)]
    for side, lane, compact, factor, line in message_lanes():
        start = (west[compact - 16] if side else east[compact]) * factor
        table[line:line + factor, start:start + factor, side * LANES + lane] = 1.0
    return table


def halo_table(columns, width):
    table = np.zeros((2, 2 * SLOT, 2 * LANES))
    outer = columns[width:]
    for side, lane, compact, factor, line in message_lanes():
        if line < 2 and lane < 2 * SLOT:
            table[lane // SLOT, side * SLOT + lane % SLOT] = outer[compact]
    table[:, EDGE] = columns[0]
    table[:, SLOT + EDGE] = outer[16]
    return table


def restriction_table(width):
    table = np.zeros((2 * width, 2 * LANES), np.float32)
    for i in range(width):
        table[2 * i, i] += 1.0
        table[2 * i + 1, i] += 0.5
        table[2 * i + 1, i + 1] += 0.5
    return table


def refining_table(width):
    table = np.zeros((LANES, LANES), np.float32)
    for i in range(width):
        table[i // 2, i] = 1.0
        table[width // 2 + i // 4, i] = 1.0
    return table


def column_lane(factor, row):
    count = GROUP // factor
    return row // count * COLUMN + {1: 0, 2: 8, 4: 12}[factor] + row % count


def column_filter_table(width):
    table = np.zeros((2 * LANES, LANES))
    filters = {factor: twice_filter(width // factor, False, False)[:, width // factor] for factor, _ in generations}
    low = [width - 8 + c for c in range(8)] + [width // 2 - 8 + c for c in range(4)] + [width // 4 - 8 + c for c in range(4)]
    high = [width + c for c in range(9)] + [width // 2 + 4 + c for c in range(5)] + [width // 4 + 4 + c for c in range(5)]
    ends = {(1, 16 + 8): 1, (2, 25 + 4): 2}
    for side, lane, compact, factor, line in message_lanes():
        place = (high[compact - 16] if side else low[compact]) * factor
        for generation, _ in generations:
            if generation >= factor and generation <= ends.get((factor, compact), 4):
                weight = filters[generation][place // generation + 8]
                table[side * LANES + lane, column_lane(generation, line // generation)] += weight
    for line in range(GROUP):
        for generation, _ in generations:
            weight = filters[generation][width // generation + 8]
            table[LANES + line * SLOT + EDGE, column_lane(generation, line // generation)] += weight
    return table


def column_rows_table(height, first, last):
    table = np.zeros((3, LANES, LANES))
    for factor, weight in generations:
        count = height // factor
        filters = twice_filter(count, first, last)
        for row in range(height):
            for source in range(-8, count + 8):
                kind, place = (1, source + count) if source < 0 else (2, source - count) if source >= count else (0, source)
                table[kind, column_lane(factor, place), row] += weight * filters[source + 8, row // factor]
    return table


def edge_choice_table():
    table = np.zeros((LANES, LANES), np.float32)
    for line in range(GROUP):
        table[line * SLOT + EDGE, line] = 1.0
    return table


def interpolation_table(width):
    table = np.zeros((2 * LANES, 2 * width), np.float32)
    for i in range(width):
        table[i, 2 * i] = 1.0
        table[i, 2 * i + 1] = 0.5
        table[LANES + i, 2 * i + 1] = 0.5
    return table


def split(value):
    high = value.astype(BF16)
    return high, (value - high.astype(F32)).astype(BF16)


def mul(a, b):
    return jnp.dot(a, b, preferred_element_type=F32)


def exact_dot(value, table):
    high, low = split(value)
    return mul(high, table) + mul(low, table)


def three_dots(value, high_table, low_table):
    high, low = split(value)
    return mul(high, high_table) + mul(low, high_table) + mul(high, low_table)


def column_case():
    gx, nx = lax.axis_index("gx"), lax.axis_size("gx")
    return jnp.where(gx == 0, 0, jnp.where(gx == nx - 1, 2, 1))


def tile(index):
    return pl.ds(pl.multiple_of(index * 8, 8), 8)


def prepare_kernel(height, gradient, members, restrict, own_tables, halo_tables, across, turned, edges, high_weights, low_weights,
                   fine, raw, table, own_case, halo_case, sems):
    case = column_case()
    blocks = height // GROUP
    levels = members.shape[1]
    part = levels // 4
    copies = [pltpu.make_async_copy(restrict, table, sems.at[8])]
    for i in range(4):
        span = pl.ds(i * part, part)
        copies.append(pltpu.make_async_copy(gradient.at[span], fine.at[span], sems.at[i]))
    for i in range(4):
        span = pl.ds(i * part, part)
        copies.append(pltpu.make_async_copy(members.at[:, span], raw.at[:, span], sems.at[4 + i]))
    copies.append(pltpu.make_async_copy(own_tables.at[case], own_case, sems.at[9]))
    copies.append(pltpu.make_async_copy(halo_tables.at[case], halo_case, sems.at[10]))
    for copy in copies:
        copy.start()
    copies[0].wait()
    for half in range(2):
        across[half, :, 0:8, :] = jnp.zeros((levels, 8, LANES), F32)
    for i in range(4):
        copies[1 + i].wait()
        value = exact_dot(fine[i * part:(i + 1) * part].reshape(part * 2 * height, fine.shape[2]), table[...])
        value = value.reshape(part, 2 * height, 2 * LANES)
        for half in range(2):
            across[half, i * part:(i + 1) * part, 8:, :] = value[:, :, half * LANES:(half + 1) * LANES]
    copies[9].wait()
    copies[10].wait()
    for part_of, target in ((0, high_weights), (1, low_weights)):
        for variant in range(4):
            target[variant, :LANES, :] = own_case[part_of]
            target[variant, LANES:, :] = jnp.zeros((LANES, 2 * LANES), BF16)
            for side in range(2):
                start = LANES + side * 64 + variant * SLOT
                target[variant, start:start + SLOT, :] = halo_case[part_of, variant % 2, side * SLOT:(side + 1) * SLOT, :]
    rows = raw.reshape(8 * levels * height, LANES)
    lane = lax.broadcasted_iota(jnp.int32, (GROUP, LANES), 1)

    def level_step(level, _):
        for block in range(blocks):
            edge = jnp.zeros((GROUP, LANES), F32)
            for line in range(GROUP):
                y = block * GROUP + line
                member = rows[pl.ds(level * height + y, 8, levels * height), :]
                turned[level, y] = member
                spot = line * SLOT + EDGE
                edge = jnp.where(lane == spot, pltpu.roll(member, spot, 1), edge)
            edges[tile(level * blocks + block), :] = edge
        return 0

    for i in range(4):
        copies[5 + i].wait()
        lax.fori_loop(i * part, (i + 1) * part, level_step, 0)


def pack_kernel(chunk, levels, height, across, turned, edges, south, restrict, packing, products, message_a, message_b, coarse, below):
    blocks = height // GROUP
    first = chunk * levels
    value = exact_dot(south[...], restrict[...])
    for half in range(2):
        below[half] = value[:, half * LANES:(half + 1) * LANES]
    lane = lax.broadcasted_iota(jnp.int32, (GROUP, LANES), 1)
    line_of = lax.broadcasted_iota(jnp.int32, (GROUP, LANES), 0)
    top = lax.broadcasted_iota(jnp.int32, (height, LANES), 0) == 0

    def level_step(level, _):
        for half in range(2):
            under = jnp.broadcast_to(below[half, pl.ds(first + level, 1), :], (height, LANES))
            under = jnp.where(top, under, across[half, first + level, pl.ds(7, height, 2), :])
            coarse[half] = across[half, first + level, pl.ds(8, height, 2), :] + 0.5 * (
                across[half, first + level, pl.ds(9, height, 2), :] + under
            )
        for block in range(blocks):
            place_rows = tile(level * blocks + block)
            for line in range(GROUP):
                y = block * GROUP + line
                products[line, place_rows, :] = turned[first + level, y] * coarse[0, y:y + 1, :]
            column = jnp.broadcast_to(coarse[1, block * GROUP:(block + 1) * GROUP, 0:1], (GROUP, LANES))
            column = jnp.sum(jnp.where(lane == line_of * SLOT + EDGE, column, 0.0), axis=0, keepdims=True)
            message_a[place_rows, :] = jnp.broadcast_to(column, (GROUP, LANES))
        return 0

    lax.fori_loop(0, levels, level_step, 0)
    total = jnp.zeros((levels * blocks * 8, 2 * LANES), F32)
    for line in range(0, GROUP, 2):
        value = jnp.concatenate([products[line], products[line + 1]], axis=1)
        total = total + exact_dot(value, packing[line * LANES:(line + 2) * LANES, :])
    to_east = total[:, :LANES] + message_a[...]
    to_west = total[:, LANES:] + edges[first * blocks * 8:(first + levels) * blocks * 8, :]
    even = lax.axis_index("gx") % 2 == 0
    message_a[...] = jnp.where(even, to_east, to_west)
    message_b[...] = jnp.where(even, to_west, to_east)


def columns_kernel(levels, height, products, own_a, own_b, got_a, got_b, high_weights, low_weights, beyond_high, beyond_low, choice,
                   filtered, message_a, message_b, factors):
    blocks = height // GROUP
    groups = levels * blocks
    lane = lax.broadcasted_iota(jnp.int32, (groups * 8, LANES), 1)
    even = lax.axis_index("gx") % 2 == 0
    own_east, own_west = jnp.where(even, own_a[...], own_b[...]), jnp.where(even, own_b[...], own_a[...])
    west, east = jnp.where(even, got_b[...], got_a[...]), jnp.where(even, got_a[...], got_b[...])
    spot = lane % SLOT == EDGE
    chosen = exact_dot(east, choice[...]).reshape(levels, blocks, 8, LANES)
    total = chosen[:, 0]
    for block in range(1, blocks):
        total = total + pltpu.roll(chosen[:, block], block * GROUP, 2)
    factors[...] = total
    west = jnp.where(spot, west * own_west, west)
    east = jnp.where(spot, east * own_east, east)
    inside = jnp.where(lax.axis_index("gx") == lax.axis_size("gx") - 1, 0.0, 1.0).astype(F32)
    beyond = three_dots(jnp.concatenate([own_east, east], axis=1), beyond_high[...], beyond_low[...])
    beyond = (beyond * inside).reshape(levels, blocks, 8, LANES)
    total = beyond[:, 0]
    for block in range(1, blocks):
        total = total + pltpu.roll(beyond[:, block], block * COLUMN, 2)
    for message in (message_a, message_b):
        message[levels * 16:] = total
    halves = [
        split(jnp.where(lane < 64, west, pltpu.roll(east, 64, 1))),
        split(jnp.where(lane < 64, pltpu.roll(west, 64, 1), east)),
    ]
    for line in range(GROUP):
        high, low = (jnp.concatenate(pair, axis=1) for pair in zip(split(products[line]), halves[line // 4]))
        weights = high_weights[line % 4]
        value = mul(high, weights) + mul(low, weights) + mul(high, low_weights[line % 4])
        filtered[:, line] = value.reshape(groups, 8, 2 * LANES)
    small = lax.broadcasted_iota(jnp.int32, (8, LANES), 1)
    second = small < 64
    up_a = lax.axis_index("gy") % 2 == 0
    start_a, start_b = jnp.where(up_a, blocks - 1, 0), jnp.where(up_a, 0, blocks - 1)
    coarse_a, coarse_b = jnp.where(up_a, blocks - 2, 0), jnp.where(up_a, 0, blocks - 2)

    def level_step(level, _):
        def at(block, line):
            return filtered[level * blocks + block, line, :, LANES:]

        fourth = []
        for block in range(blocks):
            for half in range(2):
                fourth.append(sum(at(block, half * 4 + k) for k in range(1, 4)) + at(block, half * 4))
        for message, start, coarse in ((message_a, start_a, coarse_a), (message_b, start_b, coarse_b)):
            for line in range(GROUP):
                message[level * 16 + line] = filtered[level * blocks + start, line, :, :LANES]
                block, pair = coarse + line // 4, line % 4
                pairs = at(block, 2 * pair) + at(block, 2 * pair + 1)
                message[level * 16 + 8 + line] = jnp.where(second, pairs, fourth[line])
        return 0

    lax.fori_loop(0, levels, level_step, 0)


def convolve_own(load, count, low_edges, high_edges, store):
    rows = {}

    def row(r):
        if r not in rows:
            rows[r] = load(r)
        return rows[r]

    for r in range(count):
        value = double_taps[0] * row(r)
        for k in range(1, 9):
            near = [row(q) for q in (r - k, r + k) if 0 <= q < count]
            if near:
                value = value + double_taps[k] * (near[0] if len(near) == 1 else near[0] + near[1])
        if r < 4:
            fix = edge_taps[r][0] * row(0)
            for j in range(1, 4):
                fix = fix + edge_taps[r][j] * row(j)
            value = value - low_edges * fix
        for flag, end in high_edges:
            i = end - 1 - r
            if 0 <= i < 4:
                fix = edge_taps[i][0] * row(end - 1)
                for j in range(1, 4):
                    fix = fix + edge_taps[i][j] * row(end - 1 - j)
                value = value - flag * fix
        store(r, value)
        rows.pop(r - 8, None)


def own_rows_kernel(levels, height, filtered, fine, coarse):
    blocks = height // GROUP
    half, quarter = height // 2, height // 4
    gy, ny = lax.axis_index("gy"), lax.axis_size("gy")
    low, high = jnp.where(gy == 0, 1.0, 0.0).astype(F32), jnp.where(gy == ny - 1, 1.0, 0.0).astype(F32)
    second = lax.broadcasted_iota(jnp.int32, (8, LANES), 1) < 64
    high_second, high_fourth = jnp.where(second, high, 0.0), jnp.where(second, 0.0, high)

    def level_step(level, _):
        def at(y, part):
            return filtered[level * blocks + y // 8, y % 8, :, part * LANES:(part + 1) * LANES]

        def store_to(ref):
            def store(r, value):
                ref[level, r] = value
            return store

        convolve_own(lambda r: at(r, 0), height, low, [(high, height)], store_to(fine))

        def pair(r):
            return at(2 * r, 1) + at(2 * r + 1, 1)

        def load_coarse(r):
            return jnp.where(second, pair(r), pair(2 * r) + pair(2 * r + 1) if r < quarter else 0.0)

        convolve_own(load_coarse, half, low, [(high_second, half), (high_fourth, quarter)], store_to(coarse))
        return 0

    lax.fori_loop(0, levels, level_step, 0)


def combine_kernel(chunk, levels, height, fine, coarse, got_a, got_b, own_rows, factors, turned, refining, row_highs, row_lows, *refs):
    earlier, (combined, beyond, first_row, stacked, refined, weighted) = refs[:-6], refs[-6:]
    blocks = height // GROUP
    half, quarter = height // 2, height // 4
    first = chunk * levels
    up_a = lax.axis_index("gy") % 2 == 0
    gy, ny = lax.axis_index("gy"), lax.axis_size("gy")
    second = lax.broadcasted_iota(jnp.int32, (8, LANES), 1) < 64
    scale = jnp.where(second, jnp.float32(generations[1][1]), jnp.float32(generations[2][1]))
    weight = jnp.float32(generations[0][1])

    def side(value):
        return value.reshape(levels * 8, LANES)

    case = jnp.where(gy == 0, 0, jnp.where(gy == ny - 1, 2, 1))
    far_a, far_b = side(got_a[levels * 16:]), side(got_b[levels * 16:])
    value = three_dots(side(own_rows[levels * 16:]), row_highs[case, 0], row_lows[case, 0])
    value = value + three_dots(jnp.where(up_a, far_b, far_a), row_highs[case, 1], row_lows[case, 1])
    value = value + three_dots(jnp.where(up_a, far_a, far_b), row_highs[case, 2], row_lows[case, 2])
    beyond[...] = jnp.sum(value.reshape(levels, 8, LANES) * factors[...], axis=1) * (1.0 / 7.0)

    def outside(load):
        values = [load(j) for j in range(8)]
        result = []
        for i in range(8):
            total = double_taps[i + 1] * values[0]
            for j in range(1, 8 - i):
                total = total + double_taps[i + 1 + j] * values[j]
            result.append(total)
        return result

    def level_step(level, _):
        def north(r):
            return jnp.where(up_a, got_a[level * 16 + r], got_b[level * 16 + r])

        def south(r):
            return jnp.where(up_a, got_b[level * 16 + r], got_a[level * 16 + r])

        fine_south = outside(lambda j: south(7 - j))
        coarse_south = outside(lambda j: south(15 - j))
        fine_north = outside(north)
        coarse_north = outside(lambda j: north(8 + j))
        parts = []
        for r in range(half):
            value = coarse[level, r]
            if r < 8:
                value = value + coarse_south[r]
            if r < quarter:
                i = quarter - 1 - r
                value = value + jnp.where(second, 0.0, coarse_north[i])
            if r >= half - 8:
                value = value + jnp.where(second, coarse_north[half - 1 - r], 0.0)
            parts.append(value * scale)
        for r in range(half):
            stacked[r * 8:r * 8 + 8, :] = jnp.where(second, parts[r], parts[r // 2])
        refined[...] = exact_dot(stacked[...], refining[...])
        for block in range(blocks):
            for line in range(GROUP):
                y = block * GROUP + line
                value = fine[level, y]
                if y < 8:
                    value = value + fine_south[y]
                if y >= height - 8:
                    value = value + fine_north[height - 1 - y]
                value = weight * value + refined[y // 2 * 8:y // 2 * 8 + 8, :]
                weighted[line * 8:line * 8 + 8, :] = turned[first + level, y] * value
            total = weighted[pl.ds(0, 8, 8), :]
            for m in range(1, 8):
                total = total + weighted[pl.ds(m, 8, 8), :]
            combined[level, block * GROUP:(block + 1) * GROUP, :] = total * (1.0 / 7.0)
        return 0

    lax.fori_loop(0, levels, level_step, 0)
    for rows in earlier:
        first_row[:first, :] = rows[...]
    for level in range(levels):
        first_row[first + level:first + level + 1, :LANES] = combined[level, 0:1, :]
    first_row[first:, LANES:] = beyond[...]


def interpolate_kernel(height, *refs):
    chunks = (len(refs) - 7) // 2
    north, interpolation, out, extended, rows, ready, sems = refs[-7:]
    levels = refs[0].shape[0]
    part = levels // 2
    lane = lax.broadcasted_iota(jnp.int32, (height, LANES), 1)
    line = lax.broadcasted_iota(jnp.int32, (height, LANES), 0)
    row_lane = lax.broadcasted_iota(jnp.int32, (1, LANES), 1)
    copies = []
    for start in range(0, chunks * levels, part):
        combined, beyond = refs[start // levels], refs[chunks + start // levels]
        for i in range(part):
            level = start + i
            here = combined[level % levels]
            last = jnp.broadcast_to(beyond[level % levels:level % levels + 1, :], (height, LANES))
            last = jnp.sum(jnp.where(lane == line, last, 0.0), axis=1, keepdims=True)
            after = north[level:level + 1, :LANES]
            corner = jnp.broadcast_to(north[level:level + 1, LANES:LANES + 1], (1, LANES))
            extended[0, i, 0:height, :] = here
            extended[0, i, height:height + 1, :] = after
            extended[1, i, 0:height, :] = jnp.where(lane == LANES - 1, last, pltpu.roll(here, LANES - 1, 1))
            extended[1, i, height:height + 1, :] = jnp.where(row_lane == LANES - 1, corner, pltpu.roll(after, LANES - 1, 1))
            for half in range(2):
                value = extended[half, i, 0:height, :]
                rows[half, i, pl.ds(0, height, 2), :] = value
                rows[half, i, pl.ds(1, height, 2), :] = 0.5 * (value + extended[half, i, 1:height + 1, :])
        value = exact_dot(
            jnp.concatenate([rows[half].reshape(part * 2 * height, LANES) for half in range(2)], axis=1), interpolation[...]
        )
        span = pl.ds(start, part)
        ready[span] = value.reshape(part, 2 * height, ready.shape[2])
        copies.append(pltpu.make_async_copy(ready.at[span], out.at[span], sems.at[start // part]))
        copies[-1].start()
    for copy in copies:
        copy.wait()


def partner(index, size, second):
    other = ((index + 1) ^ 1) - 1 if second else index ^ 1
    return other if 0 <= other < size else None


def swap(value, axis, second):
    size = lax.axis_size(axis)
    pairs = [(i, partner(i, size, second)) for i in range(size)]
    return lax.ppermute(value, axis, [(i, j) for i, j in pairs if j is not None])


def call(kernel, outs, scratch, cost, *args, in_hbm=0, out_hbm=False):
    vmem = pl.BlockSpec(memory_space=pltpu.VMEM)
    return pl.pallas_call(
        kernel,
        out_shape=tuple(jax.ShapeDtypeStruct(*out) if isinstance(out[0], tuple) else jax.ShapeDtypeStruct(out, F32) for out in outs),
        in_specs=[pl.BlockSpec(memory_space=pltpu.HBM) if i < in_hbm else vmem for i in range(len(args))],
        out_specs=tuple(pl.BlockSpec(memory_space=pltpu.HBM) if out_hbm else vmem for _ in outs),
        scratch_shapes=[pltpu.VMEM(shape, F32) if isinstance(shape, tuple) else shape for shape in scratch],
        compiler_params=pltpu.CompilerParams(vmem_limit_bytes=VMEM_LIMIT),
        cost_estimate=pl.CostEstimate(flops=cost, bytes_accessed=2**20, transcendentals=0),
    )(*args)


def halves_of(table):
    high = table.astype(np.float32).astype(BF16)
    return high, (table.astype(np.float32) - high.astype(np.float32)).astype(BF16)


def shards(gradient, members):
    all_levels, fine_height, fine_width = gradient.shape
    count, _, height, width = members.shape
    assert count == 8 and width == LANES and height == 32 and lax.axis_size("gx") > 1
    assert all_levels % CHUNKS == 0
    levels = all_levels // CHUNKS
    groups = levels * height // GROUP
    ny = lax.axis_size("gy")

    up = [(i, i + 1) for i in range(ny - 1)]
    south = lax.ppermute(gradient[:, -1, :], "gy", up)

    columns = [column_table(width, i == 0, i == 2) for i in range(3)]
    own_tables = np.stack(halves_of(np.stack([table[:width] for table in columns])), axis=1)
    halo_tables = np.stack(halves_of(np.stack([halo_table(table, width) for table in columns])), axis=1)
    restrict = jnp.asarray(restriction_table(width), BF16)
    packing = jnp.asarray(packing_table(width), BF16).reshape(GROUP * width, 2 * LANES)
    refining = jnp.asarray(refining_table(width), BF16)
    interpolation = jnp.asarray(interpolation_table(width), BF16)
    beyond_high, beyond_low = map(jnp.asarray, halves_of(column_filter_table(width)))
    row_highs, row_lows = map(jnp.asarray, halves_of(np.stack([column_rows_table(height, i == 0, i == 2) for i in range(3)])))
    choice = jnp.asarray(edge_choice_table(), BF16)
    flops = 10**9 // CHUNKS
    far_rows = (levels * 17, 8, LANES)

    constants = (restrict, jnp.asarray(own_tables), jnp.asarray(halo_tables))
    across, turned, edges, high_weights, low_weights = call(
        functools.partial(prepare_kernel, height),
        [(2, all_levels, 8 + 2 * height, LANES), (all_levels, height, 8, LANES), (all_levels * height, LANES),
         ((4, 2 * LANES, 2 * LANES), BF16), ((4, 2 * LANES, 2 * LANES), BF16)],
        [gradient.shape, members.shape, pltpu.VMEM(restrict.shape, BF16), pltpu.VMEM(own_tables.shape[1:], BF16),
         pltpu.VMEM(halo_tables.shape[1:], BF16), pltpu.SemaphoreType.DMA((11,))],
        flops, *(pltpu.with_memory_space_constraint(a, pltpu.HBM) for a in (gradient, members) + constants), in_hbm=5,
    )
    packed = [
        call(
            functools.partial(pack_kernel, chunk, levels, height),
            [(GROUP, groups * 8, LANES), (groups * 8, LANES), (groups * 8, LANES)],
            [(2, height, LANES), (2, all_levels, LANES)],
            flops, across, turned, edges, south, restrict, packing,
        )
        for chunk in range(CHUNKS)
    ]
    got = [(swap(own_a, "gx", False), swap(own_b, "gx", True)) for _, own_a, own_b in packed]
    filtered = [
        call(
            functools.partial(columns_kernel, levels, height),
            [(groups, GROUP, 8, 2 * LANES), far_rows, far_rows, (levels, 8, LANES)],
            [],
            flops, *packed[chunk], *got[chunk], high_weights, low_weights, beyond_high, beyond_low, choice,
        )
        for chunk in range(CHUNKS)
    ]
    far = [(swap(rows_a, "gy", False), swap(rows_b, "gy", True)) for _, rows_a, rows_b, _ in filtered]
    own = [
        call(
            functools.partial(own_rows_kernel, levels, height),
            [(levels, height, 8, LANES), (levels, height // 2, 8, LANES)],
            [],
            flops, filtered[chunk][0],
        )
        for chunk in range(CHUNKS)
    ]
    combined, beyond, first_rows = [], [], []
    for chunk in range(CHUNKS):
        results = call(
            functools.partial(combine_kernel, chunk, levels, height),
            [(levels, height, LANES), (levels, LANES), ((chunk + 1) * levels, 2 * LANES)],
            [(height // 2 * 8, LANES), (height // 2 * 8, LANES), (64, LANES)],
            flops, *own[chunk], *far[chunk], filtered[chunk][1], filtered[chunk][3], turned, refining, row_highs, row_lows,
            *first_rows[-1:],
        )
        for result, into in zip(results, (combined, beyond, first_rows)):
            into.append(result)
    north = lax.ppermute(first_rows[-1], "gy", [(j, i) for i, j in up])
    part = levels // 2
    (out,) = call(
        functools.partial(interpolate_kernel, height),
        [(all_levels, fine_height, fine_width)],
        [(2, part, height + 8, LANES), (2, part, 2 * height, LANES), (all_levels, fine_height, fine_width),
         pltpu.SemaphoreType.DMA((2 * CHUNKS,))],
        flops, *combined, *beyond, north, interpolation, out_hbm=True,
    )
    return out


def solution(mesh):
    in_specs = (P(None, "gy", "gx"), P(None, None, "gy", "gx"))
    out_specs = P(None, "gy", "gx")
    return jax.shard_map(shards, mesh=mesh, in_specs=in_specs, out_specs=out_specs, check_vma=False)
```

```python
import functools

import jax
import jax.numpy as jnp
import numpy as np
from jax import lax
from jax.experimental import pallas as pl
from jax.experimental.pallas import tpu as pltpu
from jax.sharding import PartitionSpec as P

beta_raw = [(1.0 - (offset - 4) ** 2 / 25.0) ** 2 for offset in range(9)]
beta_taps = [value / sum(beta_raw) for value in beta_raw]
generations = ((1, 0.5), (2, 0.075), (4, 0.0125))

LANES = 128
GROUP = 8
SLOT = 16
EDGE = 15
COLUMN = 32
CHUNKS = 2
PER_LEVEL = 14
VMEM_LIMIT = 20 * 2**20
BF16, F32 = jnp.bfloat16, jnp.float32
double_taps = [
    sum(beta_taps[k + 4] * beta_taps[offset - k + 4] for k in range(-4, 5) if -4 <= offset - k <= 4) for offset in range(9)
]
edge_taps = [
    [sum(beta_taps[i - k + 4] * beta_taps[k - j + 4] for k in range(-4, 0) if i - k <= 4 and j - k <= 4) for j in range(4)]
    for i in range(4)
]

def twice_filter(width, first, last):
    low, high = (0 if first else -99), (width - 1 if last else width + 99)
    table = np.zeros((width + 17, width + 1))
    for source in range(-8, width + 9):
        if not low <= source <= high:
            continue
        for middle in range(source - 4, source + 5):
            if not low <= middle <= high:
                continue
            for target in range(max(0, middle - 4), min(width, middle + 4) + 1):
                if target <= high:
                    table[source + 8, target] += beta_taps[middle - source + 4] * beta_taps[target - middle + 4]
    return table


def column_table(width, first, last):
    filters = {factor: twice_filter(width // factor, first, last) for factor, _ in generations}
    base = {1: 0, 2: LANES, 4: LANES + width // 2}

    def row(places):
        out = np.zeros(2 * LANES)
        for factor, place in places.items():
            count = width // factor
            out[base[factor]:base[factor] + count] += filters[factor][place + 8, :count]
        return out

    rows = [row({1: c, 2: c // 2, 4: c // 4}) for c in range(width)]
    rows += [row({1: c, 2: c // 2, 4: c // 4}) for c in range(-8, 0)]
    rows += [row({2: c, 4: c // 2}) for c in range(-8, -4)]
    rows += [row({4: c}) for c in range(-8, -4)]
    rows += [row({1: c, 2: c // 2, 4: c // 4}) for c in range(width, width + 8)] + [row({1: width + 8})]
    half, quarter = width // 2, width // 4
    rows += [row({2: c, 4: c // 2}) for c in range(half + 4, half + 8)] + [row({2: half + 8})]
    rows += [row({4: c}) for c in range(quarter + 4, quarter + 9)]
    return np.stack(rows)


def message_lanes():
    places = []
    for line in range(GROUP):
        places += [(0, line * SLOT + c, c, 1, line) for c in range(8)]
        places += [(1, line * SLOT + c, 16 + c, 1, line) for c in range(9)]
        if line % 2 == 0:
            places += [(0, line * SLOT + 8 + c, 8 + c, 2, line) for c in range(4)]
            places += [(1, line * SLOT + 9 + c, 25 + c, 2, line) for c in range(5)]
        if line % 4 == 1:
            places += [(0, line * SLOT + 8 + c, 12 + c, 4, line - 1) for c in range(4)]
            places += [(1, line * SLOT + 9 + c, 30 + c, 4, line - 1) for c in range(5)]
    return places


def packing_table(width):
    table = np.zeros((GROUP, width, 2 * LANES), np.float32)
    east = list(range(width - 8, width)) + [width // 2 - 8 + c for c in range(4)] + [width // 4 - 8 + c for c in range(4)]
    west = list(range(9)) + [4 + c for c in range(5)] + [4 + c for c in range(5)]
    for side, lane, compact, factor, line in message_lanes():
        start = (west[compact - 16] if side else east[compact]) * factor
        table[line:line + factor, start:start + factor, side * LANES + lane] = 1.0
    return table


def halo_table(columns, width, first):
    table = np.zeros((2, 2 * SLOT, 2 * LANES))
    outer = columns[width:]
    for side, lane, compact, factor, line in message_lanes():
        if line < 2 and lane < 2 * SLOT:
            table[lane // SLOT, side * SLOT + lane % SLOT] = outer[compact]
    table[:, EDGE] = 0.0 if first else columns[0]
    table[:, SLOT + EDGE] = outer[16]
    return table


def restriction_table(width):
    table = np.zeros((2 * width, 2 * LANES), np.float32)
    for i in range(width):
        table[2 * i, i] += 1.0
        table[2 * i + 1, i] += 0.5
        table[2 * i + 1, i + 1] += 0.5
    return table


def refining_table(width):
    table = np.zeros((LANES, LANES), np.float32)
    for i in range(width):
        table[i // 2, i] = 1.0
        table[width // 2 + i // 4, i] = 1.0
    return table


def column_lane(factor, row):
    count = GROUP // factor
    return row // count * COLUMN + {1: 0, 2: 8, 4: 12}[factor] + row % count


def column_filter_table(width):
    table = np.zeros((2 * LANES, LANES))
    filters = {factor: twice_filter(width // factor, False, False)[:, width // factor] for factor, _ in generations}
    low = [width - 8 + c for c in range(8)] + [width // 2 - 8 + c for c in range(4)] + [width // 4 - 8 + c for c in range(4)]
    high = [width + c for c in range(9)] + [width // 2 + 4 + c for c in range(5)] + [width // 4 + 4 + c for c in range(5)]
    ends = {(1, 16 + 8): 1, (2, 25 + 4): 2}
    for side, lane, compact, factor, line in message_lanes():
        place = (high[compact - 16] if side else low[compact]) * factor
        for generation, _ in generations:
            if generation >= factor and generation <= ends.get((factor, compact), 4):
                weight = filters[generation][place // generation + 8]
                table[side * LANES + lane, column_lane(generation, line // generation)] += weight
    for line in range(GROUP):
        for generation, _ in generations:
            weight = filters[generation][width // generation + 8]
            table[LANES + line * SLOT + EDGE, column_lane(generation, line // generation)] += weight
    return table


def column_rows_table(height, first, last):
    table = np.zeros((3, LANES, LANES))
    for factor, weight in generations:
        count = height // factor
        filters = twice_filter(count, first, last)
        for row in range(height):
            for source in range(-8, count + 8):
                kind, place = (1, source + count) if source < 0 else (2, source - count) if source >= count else (0, source)
                table[kind, column_lane(factor, place), row] += weight * filters[source + 8, row // factor]
    return table


def edge_choice_table():
    table = np.zeros((LANES, LANES), np.float32)
    for line in range(GROUP):
        table[line * SLOT + EDGE, line] = 1.0
    return table


def interpolation_table(width):
    table = np.zeros((2 * LANES, 2 * width), np.float32)
    for i in range(width):
        table[i, 2 * i] = 1.0
        table[i, 2 * i + 1] = 0.5
        table[LANES + i, 2 * i + 1] = 0.5
    return table


def split(value):
    high = value.astype(BF16)
    return high, (value - high.astype(F32)).astype(BF16)


def mul(a, b):
    return jnp.dot(a, b, preferred_element_type=F32)


def exact_dot(value, table):
    high, low = split(value)
    return mul(high, table) + mul(low, table)


def three_dots(value, high_table, low_table):
    high, low = split(value)
    return mul(high, high_table) + mul(low, high_table) + mul(high, low_table)


def column_case():
    gx, nx = lax.axis_index("gx"), lax.axis_size("gx")
    return jnp.where(gx == 0, 0, jnp.where(gx == nx - 1, 2, 1))


def tile(index):
    return pl.ds(pl.multiple_of(index * 8, 8), 8)


def prepare_kernel(height, gradient, members, restrict, own_tables, halo_tables, across, turned, edges, high_weights, low_weights,
                   fine, raw, table, own_case, halo_case, sems):
    case = column_case()
    blocks = height // GROUP
    levels = members.shape[1]
    part = levels // 4
    copies = [pltpu.make_async_copy(restrict, table, sems.at[8])]
    for i in range(4):
        span = pl.ds(i * part, part)
        copies.append(pltpu.make_async_copy(gradient.at[span], fine.at[span], sems.at[i]))
    for i in range(4):
        span = pl.ds(i * part, part)
        copies.append(pltpu.make_async_copy(members.at[:, span], raw.at[:, span], sems.at[4 + i]))
    copies.append(pltpu.make_async_copy(own_tables.at[case], own_case, sems.at[9]))
    copies.append(pltpu.make_async_copy(halo_tables.at[case], halo_case, sems.at[10]))
    for copy in copies:
        copy.start()
    copies[0].wait()
    for half in range(2):
        across[half, :, 0:8, :] = jnp.zeros((levels, 8, LANES), F32)
    for i in range(4):
        copies[1 + i].wait()
        value = exact_dot(fine[i * part:(i + 1) * part].reshape(part * 2 * height, fine.shape[2]), table[...])
        value = value.reshape(part, 2 * height, 2 * LANES)
        for half in range(2):
            across[half, i * part:(i + 1) * part, 8:, :] = value[:, :, half * LANES:(half + 1) * LANES]
    copies[9].wait()
    copies[10].wait()
    for part_of, target in ((0, high_weights), (1, low_weights)):
        for variant in range(4):
            target[variant, :LANES, :] = own_case[part_of]
            target[variant, LANES:, :] = jnp.zeros((LANES, 2 * LANES), BF16)
            for side in range(2):
                start = LANES + side * 64 + variant * SLOT
                target[variant, start:start + SLOT, :] = halo_case[part_of, variant % 2, side * SLOT:(side + 1) * SLOT, :]
    lane = lax.broadcasted_iota(jnp.int32, (GROUP, LANES), 1)

    def level_step(level, _):
        for block in range(blocks):
            edge = jnp.zeros((GROUP, LANES), F32)
            span = slice(block * GROUP, (block + 1) * GROUP)
            block_rows = jnp.swapaxes(raw[:, level, span, :], 0, 1)
            turned[level, span] = block_rows
            for line in range(GROUP):
                member = block_rows[line]
                spot = line * SLOT + EDGE
                edge = jnp.where(lane == spot, pltpu.roll(member, spot, 1), edge)
            edges[tile(level * blocks + block), :] = edge
        return 0

    for i in range(4):
        copies[5 + i].wait()
        lax.fori_loop(i * part, (i + 1) * part, level_step, 0)


def pack_kernel(chunk, levels, height, across, turned, edges, south, restrict, packing, products, message_a, message_b, coarse, below):
    blocks = height // GROUP
    first = chunk * levels
    value = exact_dot(south[...], restrict[...]) * jnp.where(lax.axis_index("gy") == 0, 0.0, 1.0).astype(F32)
    for half in range(2):
        below[half] = value[:, half * LANES:(half + 1) * LANES]
    lane = lax.broadcasted_iota(jnp.int32, (GROUP, LANES), 1)
    line_of = lax.broadcasted_iota(jnp.int32, (GROUP, LANES), 0)
    top = lax.broadcasted_iota(jnp.int32, (height, LANES), 0) == 0

    def level_step(level, _):
        for half in range(2):
            under = jnp.broadcast_to(below[half, pl.ds(first + level, 1), :], (height, LANES))
            under = jnp.where(top, under, across[half, first + level, pl.ds(7, height, 2), :])
            coarse[half] = across[half, first + level, pl.ds(8, height, 2), :] + 0.5 * (
                across[half, first + level, pl.ds(9, height, 2), :] + under
            )
        for block in range(blocks):
            place_rows = tile(level * blocks + block)
            for line in range(GROUP):
                y = block * GROUP + line
                products[line, place_rows, :] = turned[first + level, y] * coarse[0, y:y + 1, :]
            column = jnp.broadcast_to(coarse[1, block * GROUP:(block + 1) * GROUP, 0:1], (GROUP, LANES))
            column = jnp.sum(jnp.where(lane == line_of * SLOT + EDGE, column, 0.0), axis=0, keepdims=True)
            message_a[place_rows, :] = jnp.broadcast_to(column, (GROUP, LANES))
        return 0

    lax.fori_loop(0, levels, level_step, 0)
    total = jnp.zeros((levels * blocks * 8, 2 * LANES), F32)
    for line in range(0, GROUP, 2):
        value = jnp.concatenate([products[line], products[line + 1]], axis=1)
        total = total + exact_dot(value, packing[line * LANES:(line + 2) * LANES, :])
    to_east = total[:, :LANES] + message_a[...]
    to_west = total[:, LANES:] + edges[first * blocks * 8:(first + levels) * blocks * 8, :]
    message_a[...] = to_east
    message_b[...] = to_west


def columns_kernel(levels, height, products, own_a, own_b, got_a, got_b, high_weights, low_weights, beyond_high, beyond_low, choice,
                   filtered, message_a, message_b, factors):
    blocks = height // GROUP
    groups = levels * blocks
    lane = lax.broadcasted_iota(jnp.int32, (groups * 8, LANES), 1)
    own_east, own_west, west, east = own_a[...], own_b[...], got_a[...], got_b[...]
    spot = lane % SLOT == EDGE
    chosen = exact_dot(east, choice[...]).reshape(levels, blocks, 8, LANES)
    total = chosen[:, 0]
    for block in range(1, blocks):
        total = total + pltpu.roll(chosen[:, block], block * GROUP, 2)
    factors[...] = total
    west = jnp.where(spot, west * own_west, west)
    east = jnp.where(spot, east * own_east, east)
    inside = jnp.where(lax.axis_index("gx") == lax.axis_size("gx") - 1, 0.0, 1.0).astype(F32)
    beyond = three_dots(jnp.concatenate([own_east, east], axis=1), beyond_high[...], beyond_low[...])
    beyond = (beyond * inside).reshape(levels, blocks, 8, LANES)
    total = beyond[:, 0]
    for block in range(1, blocks):
        total = total + pltpu.roll(beyond[:, block], block * COLUMN, 2)
    for message in (message_a, message_b):
        message[levels * PER_LEVEL:] = total
    halves = [
        split(jnp.where(lane < 64, west, pltpu.roll(east, 64, 1))),
        split(jnp.where(lane < 64, pltpu.roll(west, 64, 1), east)),
    ]
    for line in range(GROUP):
        high, low = (jnp.concatenate(pair, axis=1) for pair in zip(split(products[line]), halves[line // 4]))
        weights = high_weights[line % 4]
        value = mul(high, weights) + mul(low, weights) + mul(high, low_weights[line % 4])
        filtered[:, line] = value.reshape(groups, 8, 2 * LANES)
    small = lax.broadcasted_iota(jnp.int32, (8, LANES), 1)
    second = small < 64
    up_a = lax.axis_index("gy") % 2 == 0
    start_a, start_b = jnp.where(up_a, blocks - 1, 0), jnp.where(up_a, 0, blocks - 1)
    coarse_a, coarse_b = jnp.where(up_a, blocks - 2, 0), jnp.where(up_a, 0, blocks - 2)

    def level_step(level, _):
        def at(block, line):
            return filtered[level * blocks + block, line, :, LANES:]

        fourth = []
        for block in range(blocks):
            for half in range(2):
                fourth.append(sum(at(block, half * 4 + k) for k in range(1, 4)) + at(block, half * 4))
        for message, start, coarse in ((message_a, start_a, coarse_a), (message_b, start_b, coarse_b)):
            rows = []
            for line in range(GROUP):
                message[level * PER_LEVEL + line] = filtered[level * blocks + start, line, :, :LANES]
                block, pair = coarse + line // 4, line % 4
                pairs = at(block, 2 * pair) + at(block, 2 * pair + 1)
                rows.append(jnp.where(second, pairs, fourth[line]))
            for i in range(6):
                spare = pltpu.roll(rows[6 + i // 3], 96 - 32 * (i % 3), 1)
                message[level * PER_LEVEL + 8 + i] = jnp.where(small < 96, rows[i], spare)
        return 0

    lax.fori_loop(0, levels, level_step, 0)


def convolve_own(load, count, low_edges, high_edges, store):
    rows = {}

    def row(r):
        if r not in rows:
            rows[r] = load(r)
        return rows[r]

    for r in range(count):
        value = double_taps[0] * row(r)
        for k in range(1, 9):
            near = [row(q) for q in (r - k, r + k) if 0 <= q < count]
            if near:
                value = value + double_taps[k] * (near[0] if len(near) == 1 else near[0] + near[1])
        if r < 4:
            fix = edge_taps[r][0] * row(0)
            for j in range(1, 4):
                fix = fix + edge_taps[r][j] * row(j)
            value = value - low_edges * fix
        for flag, end in high_edges:
            i = end - 1 - r
            if 0 <= i < 4:
                fix = edge_taps[i][0] * row(end - 1)
                for j in range(1, 4):
                    fix = fix + edge_taps[i][j] * row(end - 1 - j)
                value = value - flag * fix
        store(r, value)
        rows.pop(r - 8, None)


def own_rows_kernel(levels, height, filtered, fine, coarse):
    blocks = height // GROUP
    half, quarter = height // 2, height // 4
    gy, ny = lax.axis_index("gy"), lax.axis_size("gy")
    low, high = jnp.where(gy == 0, 1.0, 0.0).astype(F32), jnp.where(gy == ny - 1, 1.0, 0.0).astype(F32)
    second = lax.broadcasted_iota(jnp.int32, (8, LANES), 1) < 64
    high_second, high_fourth = jnp.where(second, high, 0.0), jnp.where(second, 0.0, high)

    def level_step(level, _):
        def at(y, part):
            return filtered[level * blocks + y // 8, y % 8, :, part * LANES:(part + 1) * LANES]

        def store_to(ref):
            def store(r, value):
                ref[level, r] = value
            return store

        convolve_own(lambda r: at(r, 0), height, low, [(high, height)], store_to(fine))

        def pair(r):
            return at(2 * r, 1) + at(2 * r + 1, 1)

        def load_coarse(r):
            return jnp.where(second, pair(r), pair(2 * r) + pair(2 * r + 1) if r < quarter else 0.0)

        convolve_own(load_coarse, half, low, [(high_second, half), (high_fourth, quarter)], store_to(coarse))
        return 0

    lax.fori_loop(0, levels, level_step, 0)


def outside(load):
    values = [load(j) for j in range(8)]
    result = []
    for i in range(8):
        total = double_taps[i + 1] * values[0]
        for j in range(1, 8 - i):
            total = total + double_taps[i + 1 + j] * values[j]
        result.append(total)
    return result


def coarse_rows(packed, lane):
    rows = list(packed)
    for i in range(2):
        pieces = [pltpu.roll(packed[3 * i + k], 32 + 32 * k, 1) for k in range(3)]
        rows.append(jnp.where(lane < 32, pieces[0], jnp.where(lane < 64, pieces[1], pieces[2])))
    return rows


def coarse_scale(lane):
    return jnp.where(lane < 64, jnp.float32(generations[1][1]), jnp.float32(generations[2][1]))


def first_row_kernel(chunk, levels, height, fine, coarse, got_a, got_b, own_rows, factors, turned, refining, row_highs, row_lows, *refs):
    earlier, (beyond, first_row, packed) = refs[:1] if chunk else (), refs[-3:]
    first = chunk * levels
    up_a = lax.axis_index("gy") % 2 == 0
    gy, ny = lax.axis_index("gy"), lax.axis_size("gy")

    def side(value):
        return value.reshape(levels * 8, LANES)

    case = jnp.where(gy == 0, 0, jnp.where(gy == ny - 1, 2, 1))
    extra = slice(levels * PER_LEVEL, levels * (PER_LEVEL + 1))
    far_a, far_b = side(got_a[extra]), side(got_b[extra])
    value = three_dots(side(own_rows[extra]), row_highs[case, 0], row_lows[case, 0])
    value = value + three_dots(jnp.where(up_a, far_b, far_a), row_highs[case, 1], row_lows[case, 1])
    value = value + three_dots(jnp.where(up_a, far_a, far_b), row_highs[case, 2], row_lows[case, 2])
    beyond[...] = jnp.sum(value.reshape(levels, 8, LANES) * factors[...], axis=1) * (1.0 / 7.0)

    lane = lax.broadcasted_iota(jnp.int32, (8, LANES), 1)
    second = lane < 64
    weight = jnp.float32(generations[0][1])
    keep = jnp.where((gy == 0) | (gy == ny - 1), 0.0, 1.0).astype(F32)
    for level in range(levels):
        base = level * PER_LEVEL
        value = coarse[level, 0]
        below = [jnp.where(up_a, keep * got_b[base + 8 + r], got_a[base + 8 + r]) for r in range(6)]
        below = coarse_rows(below, lane)
        for j in range(8):
            value = value + double_taps[j + 1] * below[7 - j]
        above = jnp.where(up_a, got_a[base + 8], keep * got_b[base + 8])
        value = value + jnp.where(second, 0.0, double_taps[8] * above)
        packed[level * 8:level * 8 + 8, :] = value * coarse_scale(lane)
    refined = exact_dot(packed[...], refining[...])
    for rows in earlier:
        first_row[:first, :] = rows[...]
    for level in range(levels):
        base = level * PER_LEVEL
        value = fine[level, 0]
        for j in range(8):
            value = value + double_taps[j + 1] * jnp.where(up_a, keep * got_b[base + 7 - j], got_a[base + 7 - j])
        value = turned[first + level, 0] * (weight * value + refined[level * 8:level * 8 + 8, :])
        first_row[first + level:first + level + 1, :LANES] = jnp.sum(value, axis=0, keepdims=True) * (1.0 / 7.0)
    first_row[first:, LANES:] = beyond[...]


def combine_kernel(chunk, levels, height, fine, coarse, got_a, got_b, turned, refining, combined, stacked, refined):
    blocks = height // GROUP
    half, quarter = height // 2, height // 4
    first = chunk * levels
    up_a = lax.axis_index("gy") % 2 == 0
    lane = lax.broadcasted_iota(jnp.int32, (8, LANES), 1)
    second = lane < 64
    scale = coarse_scale(lane)
    weight = jnp.float32(generations[0][1])
    gy, ny = lax.axis_index("gy"), lax.axis_size("gy")
    keep = jnp.where((gy == 0) | (gy == ny - 1), 0.0, 1.0).astype(F32)

    def level_step(level, _):
        def north(r):
            return jnp.where(up_a, got_a[level * PER_LEVEL + r], keep * got_b[level * PER_LEVEL + r])

        def south(r):
            return jnp.where(up_a, keep * got_b[level * PER_LEVEL + r], got_a[level * PER_LEVEL + r])

        below = coarse_rows([south(8 + r) for r in range(6)], lane)
        above = coarse_rows([north(8 + r) for r in range(6)], lane)
        fine_south = outside(lambda j: south(7 - j))
        coarse_south = outside(lambda j: below[7 - j])
        fine_north = outside(north)
        coarse_north = outside(lambda j: above[j])
        parts = []
        for r in range(half):
            value = coarse[level, r]
            if r < 8:
                value = value + coarse_south[r]
            if r < quarter:
                i = quarter - 1 - r
                value = value + jnp.where(second, 0.0, coarse_north[i])
            if r >= half - 8:
                value = value + jnp.where(second, coarse_north[half - 1 - r], 0.0)
            parts.append(value * scale)
        for r in range(half):
            stacked[r * 8:r * 8 + 8, :] = jnp.where(second, parts[r], parts[r // 2])
        refined[...] = exact_dot(stacked[...], refining[...])
        for block in range(blocks):
            weighted = []
            for line in range(GROUP):
                y = block * GROUP + line
                value = fine[level, y]
                if y < 8:
                    value = value + fine_south[y]
                if y >= height - 8:
                    value = value + fine_north[height - 1 - y]
                value = weight * value + refined[y // 2 * 8:y // 2 * 8 + 8, :]
                weighted.append(turned[first + level, y] * value)
            total = jnp.sum(jnp.swapaxes(jnp.stack(weighted), 0, 1), axis=0)
            combined[level, block * GROUP:(block + 1) * GROUP, :] = total * (1.0 / 7.0)
        return 0

    lax.fori_loop(0, levels, level_step, 0)


def interpolate_levels(combined, beyond, north, first, start, part, interpolation, extended, rows):
    height = combined.shape[1]
    lane = lax.broadcasted_iota(jnp.int32, (height, LANES), 1)
    line = lax.broadcasted_iota(jnp.int32, (height, LANES), 0)
    for i in range(part):
        level = start + i
        here = combined[level]
        last = jnp.broadcast_to(beyond[level:level + 1, :], (height, LANES))
        last = jnp.sum(jnp.where(lane == line, last, 0.0), axis=1, keepdims=True)
        extended[0, i, 0:height, :] = here
        extended[1, i, 0:height, :] = jnp.where(lane == LANES - 1, last, pltpu.roll(here, LANES - 1, 1))
        for half in range(2):
            if north is None:
                extended[half, i, height:height + 1, :] = jnp.zeros((1, LANES), F32)
            else:
                extended[half, i, height:height + 1, :] = north[half][first + level:first + level + 1, :]
            value = extended[half, i, 0:height, :]
            rows[half, i, pl.ds(0, height, 2), :] = value
            rows[half, i, pl.ds(1, height, 2), :] = 0.5 * (value + extended[half, i, 1:height + 1, :])
    value = exact_dot(
        jnp.concatenate([rows[half].reshape(part * 2 * height, LANES) for half in range(2)], axis=1), interpolation[...]
    )
    return value.reshape(part, 2 * height, interpolation.shape[1])


def early_kernel(combined, beyond, interpolation, out, tails, extended, rows, ready, sems):
    levels = combined.shape[0]
    part = levels // 2
    done = ready.shape[1] - 8
    copies = []
    for start in range(0, levels, part):
        span = pl.ds(start, part)
        ready[span] = interpolate_levels(combined, beyond, None, 0, start, part, interpolation, extended, rows)
        copies.append(pltpu.make_async_copy(ready.at[span, pl.ds(0, done)], out.at[span, pl.ds(0, done)], sems.at[start // part]))
        copies[-1].start()
    tails[...] = ready[:, done:, :]
    for copy in copies:
        copy.wait()


def late_kernel(first, before, combined, beyond, north, interpolation, tails, out, extended, rows, ready, ends, kept, shifted, sems):
    levels = combined.shape[0]
    part = levels // 2
    lane = lax.broadcasted_iota(jnp.int32, shifted.shape, 1)
    inside = jnp.where(lax.axis_index("gy") == lax.axis_size("gy") - 1, 0.0, 1.0).astype(F32)
    corner = jnp.broadcast_to(north[:, LANES:LANES + 1], shifted.shape) * inside
    after = north[:, :LANES] * inside
    kept[...] = after
    shifted[...] = jnp.where(lane == LANES - 1, corner, pltpu.roll(after, LANES - 1, 1))
    copies = []
    row = 0.5 * exact_dot(jnp.concatenate([after, shifted[...]], axis=1), interpolation[...])
    ends[...] = tails[...]
    for level in range(first):
        ends[level, 7:8, :] = ends[level, 7:8, :] + row[level:level + 1, :]
    done = ready.shape[1] - 8
    copies.append(pltpu.make_async_copy(ends, out.at[pl.ds(0, first), pl.ds(done, 8)], sems.at[2]))
    copies[-1].start()
    for start in range(0, levels, part):
        span = pl.ds(start, part)
        rows_north = (kept, shifted)
        ready[span] = interpolate_levels(combined, beyond, rows_north, first, start, part, interpolation, extended, rows)
        copies.append(pltpu.make_async_copy(ready.at[span], out.at[pl.ds(first + start, part)], sems.at[start // part]))
        copies[-1].start()
    for copy in copies:
        copy.wait()


def around(value, axis, step):
    size = lax.axis_size(axis)
    return lax.ppermute(value, axis, [(i, (i + step) % size) for i in range(size)])


def swap(value, second):
    nx, ny = lax.axis_size("gx"), lax.axis_size("gy")
    pairs = []
    for x in range(nx):
        for y in range(ny):
            other = ((y + 1) ^ 1) - 1 if second else y ^ 1
            pairs.append((x * ny + y, x * ny + other if 0 <= other < ny else (x ^ 1) * ny + y))
    return lax.ppermute(value, ("gx", "gy"), pairs)


def call(kernel, outs, scratch, cost, *args, in_hbm=0):
    vmem = pl.BlockSpec(memory_space=pltpu.VMEM)
    return pl.pallas_call(
        kernel,
        out_shape=tuple(jax.ShapeDtypeStruct(*out) if isinstance(out[0], tuple) else jax.ShapeDtypeStruct(out, F32) for out in outs),
        in_specs=[pl.BlockSpec(memory_space=pltpu.HBM) if i < in_hbm else vmem for i in range(len(args))],
        out_specs=tuple(vmem for _ in outs),
        scratch_shapes=[pltpu.VMEM(shape, F32) if isinstance(shape, tuple) else shape for shape in scratch],
        compiler_params=pltpu.CompilerParams(vmem_limit_bytes=VMEM_LIMIT),
        cost_estimate=pl.CostEstimate(flops=cost, bytes_accessed=2**20, transcendentals=0),
    )(*args)


def halves_of(table):
    high = table.astype(np.float32).astype(BF16)
    return high, (table.astype(np.float32) - high.astype(np.float32)).astype(BF16)


def shards(gradient, members):
    all_levels, fine_height, fine_width = gradient.shape
    count, _, height, width = members.shape
    assert count == 8 and width == LANES and height == 32 and lax.axis_size("gx") % 2 == 0 and lax.axis_size("gy") % 2 == 0
    assert all_levels % CHUNKS == 0
    levels = all_levels // CHUNKS
    groups = levels * height // GROUP

    south = around(gradient[:, -1, :], "gy", 1)

    columns = [column_table(width, i == 0, i == 2) for i in range(3)]
    own_tables = np.stack(halves_of(np.stack([table[:width] for table in columns])), axis=1)
    halo_tables = np.stack(halves_of(np.stack([halo_table(table, width, i == 0) for i, table in enumerate(columns)])), axis=1)
    restrict = jnp.asarray(restriction_table(width), BF16)
    packing = jnp.asarray(packing_table(width), BF16).reshape(GROUP * width, 2 * LANES)
    refining = jnp.asarray(refining_table(width), BF16)
    interpolation = jnp.asarray(interpolation_table(width), BF16)
    beyond_high, beyond_low = map(jnp.asarray, halves_of(column_filter_table(width)))
    row_highs, row_lows = map(jnp.asarray, halves_of(np.stack([column_rows_table(height, i == 0, i == 2) for i in range(3)])))
    choice = jnp.asarray(edge_choice_table(), BF16)
    flops = 10**9 // CHUNKS
    far_rows = (levels * (PER_LEVEL + 1), 8, LANES)

    constants = (restrict, jnp.asarray(own_tables), jnp.asarray(halo_tables))
    across, turned, edges, high_weights, low_weights = call(
        functools.partial(prepare_kernel, height),
        [(2, all_levels, 8 + 2 * height, LANES), (all_levels, height, 8, LANES), (all_levels * height, LANES),
         ((4, 2 * LANES, 2 * LANES), BF16), ((4, 2 * LANES, 2 * LANES), BF16)],
        [gradient.shape, members.shape, pltpu.VMEM(restrict.shape, BF16), pltpu.VMEM(own_tables.shape[1:], BF16),
         pltpu.VMEM(halo_tables.shape[1:], BF16), pltpu.SemaphoreType.DMA((11,))],
        flops, *(pltpu.with_memory_space_constraint(a, pltpu.HBM) for a in (gradient, members) + constants), in_hbm=5,
    )
    packed = [
        call(
            functools.partial(pack_kernel, chunk, levels, height),
            [(GROUP, groups * 8, LANES), (groups * 8, LANES), (groups * 8, LANES)],
            [(2, height, LANES), (2, all_levels, LANES)],
            flops, across, turned, edges, south, restrict, packing,
        )
        for chunk in range(CHUNKS)
    ]
    got = [(around(to_east, "gx", 1), around(to_west, "gx", -1)) for _, to_east, to_west in packed]
    filtered = [
        call(
            functools.partial(columns_kernel, levels, height),
            [(groups, GROUP, 8, 2 * LANES), far_rows, far_rows, (levels, 8, LANES)],
            [],
            flops, *packed[chunk], *got[chunk], high_weights, low_weights, beyond_high, beyond_low, choice,
        )
        for chunk in range(CHUNKS)
    ]
    far = [(swap(rows_a, False), swap(rows_b, True)) for _, rows_a, rows_b, _ in filtered]
    own = [
        call(
            functools.partial(own_rows_kernel, levels, height),
            [(levels, height, 8, LANES), (levels, height // 2, 8, LANES)],
            [],
            flops, filtered[chunk][0],
        )
        for chunk in range(CHUNKS)
    ]
    part = levels // 2
    buffers = [(2, part, height + 8, LANES), (2, part, 2 * height, LANES), (levels, fine_height, fine_width)]
    vmem, hbm = pl.BlockSpec(memory_space=pltpu.VMEM), pl.BlockSpec(memory_space=pltpu.HBM)
    out_shape = jax.ShapeDtypeStruct(gradient.shape, F32)
    params = pltpu.CompilerParams(vmem_limit_bytes=VMEM_LIMIT)
    cost = pl.CostEstimate(flops=flops, bytes_accessed=2**20, transcendentals=0)

    def first_rows_of(chunk, *earlier):
        return call(
            functools.partial(first_row_kernel, chunk, levels, height),
            [(levels, LANES), ((chunk + 1) * levels, 2 * LANES)],
            [(levels * 8, LANES)],
            flops, *own[chunk], *far[chunk], filtered[chunk][1], filtered[chunk][3], turned, refining, row_highs, row_lows, *earlier,
        )

    def combined_of(chunk):
        return call(
            functools.partial(combine_kernel, chunk, levels, height),
            [(levels, height, LANES)],
            [(height // 2 * 8, LANES), (height // 2 * 8, LANES)],
            flops, *own[chunk], *far[chunk], turned, refining,
        )[0]

    early_beyond, early_rows = first_rows_of(0)
    out, tails = pl.pallas_call(
        early_kernel,
        out_shape=(out_shape, jax.ShapeDtypeStruct((levels, 8, fine_width), F32)),
        in_specs=[vmem] * 3, out_specs=(hbm, vmem),
        scratch_shapes=[pltpu.VMEM(shape, F32) for shape in buffers] + [pltpu.SemaphoreType.DMA((2,))],
        compiler_params=params, cost_estimate=cost,
    )(combined_of(0), early_beyond, interpolation)
    beyond, rows = first_rows_of(1, early_rows, tails)
    north = around(rows, "gy", -1)
    out = pl.pallas_call(
        functools.partial(late_kernel, levels),
        out_shape=out_shape,
        in_specs=[hbm] + [vmem] * 5, out_specs=hbm,
        scratch_shapes=[pltpu.VMEM(shape, F32) for shape in buffers + [(levels, 8, fine_width), (all_levels, LANES), (all_levels, LANES)]]
        + [pltpu.SemaphoreType.DMA((3,))],
        input_output_aliases={0: 0},
        compiler_params=params, cost_estimate=cost,
    )(out, combined_of(1), beyond, north, interpolation, tails)
    return out


def solution(mesh):
    in_specs = (P(None, "gy", "gx"), P(None, None, "gy", "gx"))
    out_specs = P(None, "gy", "gx")
    return jax.shard_map(shards, mesh=mesh, in_specs=in_specs, out_specs=out_specs, check_vma=False)
```

```python
import functools

import jax
import jax.numpy as jnp
import numpy as np
from jax import lax
from jax.experimental import pallas as pl
from jax.experimental.pallas import tpu as pltpu
from jax.sharding import PartitionSpec as P

beta_raw = [(1.0 - (offset - 4) ** 2 / 25.0) ** 2 for offset in range(9)]
beta_taps = [value / sum(beta_raw) for value in beta_raw]
generations = ((1, 0.5), (2, 0.075), (4, 0.0125))

LANES = 128
GROUP = 8
SLOTS = (12, 14)
FREE = (8, 9)
USED = (8 * 12, 8 * 14)
COMPACT = 64
COLUMN = 32
CHUNKS = 2
PER_LEVEL = 14
VMEM_LIMIT = 20 * 2**20
BF16, F32 = jnp.bfloat16, jnp.float32
double_taps = [
    sum(beta_taps[k + 4] * beta_taps[offset - k + 4] for k in range(-4, 5) if -4 <= offset - k <= 4) for offset in range(9)
]
edge_taps = [
    [sum(beta_taps[i - k + 4] * beta_taps[k - j + 4] for k in range(-4, 0) if i - k <= 4 and j - k <= 4) for j in range(4)]
    for i in range(4)
]

def twice_filter(width, first, last):
    low, high = (0 if first else -99), (width - 1 if last else width + 99)
    table = np.zeros((width + 17, width + 1))
    for source in range(-8, width + 9):
        if not low <= source <= high:
            continue
        for middle in range(source - 4, source + 5):
            if not low <= middle <= high:
                continue
            for target in range(max(0, middle - 4), min(width, middle + 4) + 1):
                if target <= high:
                    table[source + 8, target] += beta_taps[middle - source + 4] * beta_taps[target - middle + 4]
    return table


def column_table(width, first, last):
    filters = {factor: twice_filter(width // factor, first, last) for factor, _ in generations}
    base = {1: 0, 2: LANES, 4: LANES + width // 2}

    def row(places):
        out = np.zeros(2 * LANES)
        for factor, place in places.items():
            count = width // factor
            out[base[factor]:base[factor] + count] += filters[factor][place + 8, :count]
        return out

    rows = [row({1: c, 2: c // 2, 4: c // 4}) for c in range(width)]
    rows += [row({1: c, 2: c // 2, 4: c // 4}) for c in range(-8, 0)]
    rows += [row({2: c, 4: c // 2}) for c in range(-8, -4)]
    rows += [row({4: c}) for c in range(-8, -4)]
    rows += [row({1: c, 2: c // 2, 4: c // 4}) for c in range(width, width + 8)] + [row({1: width + 8})]
    half, quarter = width // 2, width // 4
    rows += [row({2: c, 4: c // 2}) for c in range(half + 4, half + 8)] + [row({2: half + 8})]
    rows += [row({4: c}) for c in range(quarter + 4, quarter + 9)]
    return np.stack(rows)


def edge_lane(side, line):
    return SLOTS[side] * (line // 4 * 4 + 3) + FREE[side] + line % 4


def message_lanes():
    places = []
    for line in range(GROUP):
        for side, (first, second, fourth) in enumerate(((0, 8, 12), (16, 25, 30))):
            start = line * SLOTS[side]
            places += [(side, start + c, first + c, 1, line, line) for c in range(FREE[side])]
            rest = [start + c for c in range(FREE[side], SLOTS[side])]
            if line % 2 == 0:
                places += [(side, lane, second + c, 2, line, line) for c, lane in enumerate(rest)]
            if line % 4 == 1:
                places += [(side, lane, fourth + c, 4, line - 1, line) for c, lane in enumerate(rest)]
    return places


def packing_table(width):
    table = np.zeros((GROUP, width, 2 * LANES), np.float32)
    east = list(range(width - 8, width)) + [width // 2 - 8 + c for c in range(4)] + [width // 4 - 8 + c for c in range(4)]
    west = list(range(9)) + [4 + c for c in range(5)] + [4 + c for c in range(5)]
    for side, lane, compact, factor, line, _ in message_lanes():
        start = (west[compact - 16] if side else east[compact]) * factor
        table[line:line + factor, start:start + factor, side * LANES + lane] = 1.0
    return table


def halo_table(columns, width, first):
    table = np.zeros((COMPACT, 2 * LANES))
    table[:35] = columns[width:]
    table[35] = 0.0 if first else columns[0]
    return table


def halo_places():
    table = np.zeros((4, LANES, COMPACT), np.float32)
    for side, lane, compact, _, _, line in message_lanes():
        if line < 4:
            table[line, side * 64 + lane, compact] = 1.0
    for line in range(4):
        table[line, edge_lane(0, line), 35] = 1.0
        table[line, 64 + edge_lane(1, line), 16] = 1.0
    return table


def restriction_table(width):
    table = np.zeros((2 * width, 2 * LANES), np.float32)
    for i in range(width):
        table[2 * i, i] += 1.0
        table[2 * i + 1, i] += 0.5
        table[2 * i + 1, i + 1] += 0.5
    return table


def refining_table(width):
    table = np.zeros((LANES, LANES), np.float32)
    for i in range(width):
        table[i // 2, i] = 1.0
        table[width // 2 + i // 4, i] = 1.0
    return table


def column_lane(factor, row):
    count = GROUP // factor
    return row // count * COLUMN + {1: 0, 2: 8, 4: 12}[factor] + row % count


def column_filter_table(width):
    table = np.zeros((2 * LANES, LANES))
    filters = {factor: twice_filter(width // factor, False, False)[:, width // factor] for factor, _ in generations}
    low = [width - 8 + c for c in range(8)] + [width // 2 - 8 + c for c in range(4)] + [width // 4 - 8 + c for c in range(4)]
    high = [width + c for c in range(9)] + [width // 2 + 4 + c for c in range(5)] + [width // 4 + 4 + c for c in range(5)]
    ends = {(1, 16 + 8): 1, (2, 25 + 4): 2}
    for side, lane, compact, factor, line, _ in message_lanes():
        place = (high[compact - 16] if side else low[compact]) * factor
        for generation, _ in generations:
            if generation >= factor and generation <= ends.get((factor, compact), 4):
                weight = filters[generation][place // generation + 8]
                table[side * LANES + lane, column_lane(generation, line // generation)] += weight
    for line in range(GROUP):
        for generation, _ in generations:
            weight = filters[generation][width // generation + 8]
            table[LANES + edge_lane(1, line), column_lane(generation, line // generation)] += weight
    return table


def column_rows_table(height, first, last):
    table = np.zeros((3, LANES, LANES))
    for factor, weight in generations:
        count = height // factor
        filters = twice_filter(count, first, last)
        for row in range(height):
            for source in range(-8, count + 8):
                kind, place = (1, source + count) if source < 0 else (2, source - count) if source >= count else (0, source)
                table[kind, column_lane(factor, place), row] += weight * filters[source + 8, row // factor]
    return table


def edge_choice_table():
    table = np.zeros((LANES, LANES), np.float32)
    for line in range(GROUP):
        table[edge_lane(1, line), line] = 1.0
    return table


def interpolation_table(width):
    table = np.zeros((2 * LANES, 2 * width), np.float32)
    for i in range(width):
        table[i, 2 * i] = 1.0
        table[i, 2 * i + 1] = 0.5
        table[LANES + i, 2 * i + 1] = 0.5
    return table


def split(value):
    high = value.astype(BF16)
    return high, (value - high.astype(F32)).astype(BF16)


def mul(a, b):
    return jnp.dot(a, b, preferred_element_type=F32)


def exact_dot(value, table):
    high, low = split(value)
    return mul(high, table) + mul(low, table)


def three_dots(value, high_table, low_table):
    high, low = split(value)
    return mul(high, high_table) + mul(low, high_table) + mul(high, low_table)


def column_case():
    gx, nx = lax.axis_index("gx"), lax.axis_size("gx")
    return jnp.where(gx == 0, 0, jnp.where(gx == nx - 1, 2, 1))


def tile(index):
    return pl.ds(pl.multiple_of(index * 8, 8), 8)


def prepare_kernel(chunk, levels, height, *refs):
    if chunk:
        (gradient, members, restrict, _), (across, turned, edges), (fine, raw, table, sems) = refs[:4], refs[4:7], refs[7:]
    else:
        (gradient, members, restrict, own_tables, halo_tables, places, refine), refs = refs[:7], refs[7:]
        across, turned, edges, high_weights, low_weights, refine_out, fine, raw, table, own_case, halo_case, placing, sems = refs
    blocks = height // GROUP
    first, part = chunk * levels, levels // 2
    copies = [pltpu.make_async_copy(restrict, table, sems.at[0])]
    for i in range(2):
        span = pl.ds(first + i * part, part)
        copies.append(pltpu.make_async_copy(gradient.at[span], fine.at[pl.ds(i * part, part)], sems.at[1 + i]))
    for i in range(2):
        span = pl.ds(first + i * part, part)
        copies.append(pltpu.make_async_copy(members.at[:, span], raw.at[:, pl.ds(i * part, part)], sems.at[3 + i]))
    if not chunk:
        case = column_case()
        copies.append(pltpu.make_async_copy(own_tables.at[case], own_case, sems.at[5]))
        copies.append(pltpu.make_async_copy(halo_tables.at[case], halo_case, sems.at[6]))
        copies.append(pltpu.make_async_copy(places, placing, sems.at[7]))
        copies.append(pltpu.make_async_copy(refine, refine_out, sems.at[8]))
    for copy in copies:
        copy.start()
    copies[0].wait()
    for half in range(2):
        across[half, :, 0:8, :] = jnp.zeros((levels, 8, LANES), F32)
    for i in range(2):
        copies[1 + i].wait()
        value = exact_dot(fine[i * part:(i + 1) * part].reshape(part * 2 * height, fine.shape[2]), table[...])
        value = value.reshape(part, 2 * height, 2 * LANES)
        for half in range(2):
            across[half, i * part:(i + 1) * part, 8:, :] = value[:, :, half * LANES:(half + 1) * LANES]
    lane = lax.broadcasted_iota(jnp.int32, (GROUP, LANES), 1)

    def level_step(level, _):
        for block in range(blocks):
            edge = jnp.zeros((GROUP, LANES), F32)
            span = slice(block * GROUP, (block + 1) * GROUP)
            block_rows = jnp.swapaxes(raw[:, level, span, :], 0, 1)
            turned[level, span] = block_rows
            for line in range(GROUP):
                spot = edge_lane(1, line)
                edge = jnp.where(lane == spot, pltpu.roll(block_rows[line], spot, 1), edge)
            edges[tile(level * blocks + block), :] = edge
        return 0

    for i in range(2):
        copies[3 + i].wait()
        lax.fori_loop(i * part, (i + 1) * part, level_step, 0, unroll=4)
    if not chunk:
        for copy in copies[5:]:
            copy.wait()
        for which, target in ((0, high_weights), (1, low_weights)):
            for variant in range(4):
                target[variant, :LANES, :] = own_case[which]
                target[variant, LANES:, :] = mul(placing[variant], halo_case[which]).astype(BF16)


def pack_kernel(chunk, levels, height, across, turned, edges, south, restrict, packing, products, own_east, own_west, to_east, to_west,
                coarse, below):
    blocks = height // GROUP
    first = chunk * levels
    value = exact_dot(south[...], restrict[...]) * jnp.where(lax.axis_index("gy") == 0, 0.0, 1.0).astype(F32)
    for half in range(2):
        below[half] = value[:, half * LANES:(half + 1) * LANES]
    lane = lax.broadcasted_iota(jnp.int32, (GROUP, LANES), 1)
    line_of = lax.broadcasted_iota(jnp.int32, (GROUP, LANES), 0)
    spots = (line_of >> 2) * (4 * SLOTS[0]) + edge_lane(0, 0) + (line_of & 3)
    top = lax.broadcasted_iota(jnp.int32, (height, LANES), 0) == 0

    def level_step(level, _):
        for half in range(2):
            under = jnp.broadcast_to(below[half, pl.ds(first + level, 1), :], (height, LANES))
            under = jnp.where(top, under, across[half, level, pl.ds(7, height, 2), :])
            coarse[half] = across[half, level, pl.ds(8, height, 2), :] + 0.5 * (
                across[half, level, pl.ds(9, height, 2), :] + under
            )
        for block in range(blocks):
            place_rows = tile(level * blocks + block)
            for line in range(GROUP):
                y = block * GROUP + line
                products[line, place_rows, :] = turned[level, y] * coarse[0, y:y + 1, :]
            column = jnp.broadcast_to(coarse[1, block * GROUP:(block + 1) * GROUP, 0:1], (GROUP, LANES))
            column = jnp.sum(jnp.where(lane == spots, column, 0.0), axis=0, keepdims=True)
            own_east[place_rows, :] = jnp.broadcast_to(column, (GROUP, LANES))
        return 0

    lax.fori_loop(0, levels, level_step, 0, unroll=4)
    total = jnp.zeros((levels * blocks * 8, 2 * LANES), F32)
    for line in range(0, GROUP, 2):
        value = jnp.concatenate([products[line], products[line + 1]], axis=1)
        total = total + exact_dot(value, packing[line * LANES:(line + 2) * LANES, :])
    own_east[...] = own_east[...] + total[:, :LANES]
    own_west[...] = total[:, LANES:] + edges[...]
    lane = lax.broadcasted_iota(jnp.int32, (levels, 8, LANES), 2)
    groups = [own_east[...].reshape(levels, 4, 8, LANES)[:, i] for i in range(4)]
    for i in range(3):
        to_east[i] = jnp.where(lane < USED[0], groups[i], pltpu.roll(groups[3], USED[0] - 32 * i, 2))
    lane = lane[:levels // 2]
    groups = [own_west[...].reshape(levels // 2, 8, 8, LANES)[:, i] for i in range(8)]
    for i in range(7):
        to_west[i] = jnp.where(lane < USED[1], groups[i], pltpu.roll(groups[7], USED[1] - 16 * i, 2))


def columns_kernel(levels, height, products, own_a, own_b, from_west, from_east, high_weights, low_weights, beyond_high, beyond_low, choice,
                   filtered, message_a, message_b, factors):
    blocks = height // GROUP
    groups = levels * blocks
    lane = lax.broadcasted_iota(jnp.int32, (groups * 8, LANES), 1)
    own_east, own_west = own_a[...], own_b[...]
    whole = lax.broadcasted_iota(jnp.int32, (levels, 8, LANES), 2)
    parts = [from_west[i] for i in range(3)]
    last = pltpu.roll(parts[2], 96, 2)
    for i in range(2):
        last = jnp.where((whole >= 32 * i) & (whole < 32 * i + 32), pltpu.roll(parts[i], 32 * i + 32, 2), last)
    west = jnp.stack(parts + [last], axis=1).reshape(groups * 8, LANES)
    whole = whole[:levels // 2]
    parts = [from_east[i] for i in range(7)]
    last = pltpu.roll(parts[6], 112, 2)
    for i in range(6):
        last = jnp.where((whole >= 16 * i) & (whole < 16 * i + 16), pltpu.roll(parts[i], 16 * i + 16, 2), last)
    east = jnp.stack(parts + [last], axis=1).reshape(groups * 8, LANES)
    chosen = exact_dot(east, choice[...]).reshape(levels, blocks, 8, LANES)
    total = chosen[:, 0]
    for block in range(1, blocks):
        total = total + pltpu.roll(chosen[:, block], block * GROUP, 2)
    factors[...] = total
    shifts = [edge_lane(1, line) - edge_lane(0, line) for line in (0, 4)]
    for line, shift in zip((0, 4), shifts):
        spot = (lane >= edge_lane(0, line)) & (lane < edge_lane(0, line) + 4)
        west = jnp.where(spot, west * pltpu.roll(own_west, LANES - shift, 1), west)
        spot = (lane >= edge_lane(1, line)) & (lane < edge_lane(1, line) + 4)
        east = jnp.where(spot, east * pltpu.roll(own_east, shift, 1), east)
    inside = jnp.where(lax.axis_index("gx") == lax.axis_size("gx") - 1, 0.0, 1.0).astype(F32)
    beyond = three_dots(jnp.concatenate([own_east, east], axis=1), beyond_high[...], beyond_low[...])
    beyond = (beyond * inside).reshape(levels, blocks, 8, LANES)
    total = beyond[:, 0]
    for block in range(1, blocks):
        total = total + pltpu.roll(beyond[:, block], block * COLUMN, 2)
    for message in (message_a, message_b):
        message[levels * PER_LEVEL:] = total
    halves = [
        split(jnp.where(lane < 64, west, pltpu.roll(east, 64, 1))),
        split(jnp.where(lane < 64, pltpu.roll(west, LANES - USED[0] // 2, 1), pltpu.roll(east, 64 - USED[1] // 2, 1))),
    ]
    for line in range(GROUP):
        high, low = (jnp.concatenate(pair, axis=1) for pair in zip(split(products[line]), halves[line // 4]))
        weights = high_weights[line % 4]
        value = mul(high, weights) + mul(low, weights) + mul(high, low_weights[line % 4])
        filtered[:, line] = value.reshape(groups, 8, 2 * LANES)
    small = lax.broadcasted_iota(jnp.int32, (8, LANES), 1)
    second = small < 64
    up_a = lax.axis_index("gy") % 2 == 0
    start_a, start_b = jnp.where(up_a, blocks - 1, 0), jnp.where(up_a, 0, blocks - 1)
    coarse_a, coarse_b = jnp.where(up_a, blocks - 2, 0), jnp.where(up_a, 0, blocks - 2)

    def level_step(level, _):
        def at(block, line):
            return filtered[level * blocks + block, line, :, LANES:]

        fourth = []
        for block in range(blocks):
            for half in range(2):
                fourth.append(sum(at(block, half * 4 + k) for k in range(1, 4)) + at(block, half * 4))
        for message, start, coarse in ((message_a, start_a, coarse_a), (message_b, start_b, coarse_b)):
            rows = []
            for line in range(GROUP):
                message[level * PER_LEVEL + line] = filtered[level * blocks + start, line, :, :LANES]
                block, pair = coarse + line // 4, line % 4
                pairs = at(block, 2 * pair) + at(block, 2 * pair + 1)
                rows.append(jnp.where(second, pairs, fourth[line]))
            for i in range(6):
                spare = pltpu.roll(rows[6 + i // 3], 96 - 32 * (i % 3), 1)
                message[level * PER_LEVEL + 8 + i] = jnp.where(small < 96, rows[i], spare)
        return 0

    lax.fori_loop(0, levels, level_step, 0, unroll=4)


def convolve_own(load, count, low_edges, high_edges, store):
    rows = {}

    def row(r):
        if r not in rows:
            rows[r] = load(r)
        return rows[r]

    for r in range(count):
        value = double_taps[0] * row(r)
        for k in range(1, 9):
            near = [row(q) for q in (r - k, r + k) if 0 <= q < count]
            if near:
                value = value + double_taps[k] * (near[0] if len(near) == 1 else near[0] + near[1])
        if r < 4:
            fix = edge_taps[r][0] * row(0)
            for j in range(1, 4):
                fix = fix + edge_taps[r][j] * row(j)
            value = value - low_edges * fix
        for flag, end in high_edges:
            i = end - 1 - r
            if 0 <= i < 4:
                fix = edge_taps[i][0] * row(end - 1)
                for j in range(1, 4):
                    fix = fix + edge_taps[i][j] * row(end - 1 - j)
                value = value - flag * fix
        store(r, value)
        rows.pop(r - 8, None)


def own_rows_kernel(levels, height, filtered, fine, coarse):
    blocks = height // GROUP
    half, quarter = height // 2, height // 4
    gy, ny = lax.axis_index("gy"), lax.axis_size("gy")
    low, high = jnp.where(gy == 0, 1.0, 0.0).astype(F32), jnp.where(gy == ny - 1, 1.0, 0.0).astype(F32)
    second = lax.broadcasted_iota(jnp.int32, (8, LANES), 1) < 64
    high_second, high_fourth = jnp.where(second, high, 0.0), jnp.where(second, 0.0, high)

    def level_step(level, _):
        def at(y, part):
            return filtered[level * blocks + y // 8, y % 8, :, part * LANES:(part + 1) * LANES]

        def store_to(ref):
            def store(r, value):
                ref[level, r] = value
            return store

        convolve_own(lambda r: at(r, 0), height, low, [(high, height)], store_to(fine))

        def pair(r):
            return at(2 * r, 1) + at(2 * r + 1, 1)

        def load_coarse(r):
            return jnp.where(second, pair(r), pair(2 * r) + pair(2 * r + 1) if r < quarter else 0.0)

        convolve_own(load_coarse, half, low, [(high_second, half), (high_fourth, quarter)], store_to(coarse))
        return 0

    lax.fori_loop(0, levels, level_step, 0, unroll=4)


def outside(load):
    values = [load(j) for j in range(8)]
    result = []
    for i in range(8):
        total = double_taps[i + 1] * values[0]
        for j in range(1, 8 - i):
            total = total + double_taps[i + 1 + j] * values[j]
        result.append(total)
    return result


def coarse_rows(packed, lane):
    rows = list(packed)
    for i in range(2):
        pieces = [pltpu.roll(packed[3 * i + k], 32 + 32 * k, 1) for k in range(3)]
        rows.append(jnp.where(lane < 32, pieces[0], jnp.where(lane < 64, pieces[1], pieces[2])))
    return rows


def coarse_scale(lane):
    return jnp.where(lane < 64, jnp.float32(generations[1][1]), jnp.float32(generations[2][1]))


def first_row_kernel(chunk, levels, height, fine, coarse, got_a, got_b, own_rows, factors, turned, refining, row_highs, row_lows, *refs):
    earlier, (beyond, first_row, packed) = refs[:1] if chunk else (), refs[-3:]
    first = chunk * levels
    up_a = lax.axis_index("gy") % 2 == 0
    gy, ny = lax.axis_index("gy"), lax.axis_size("gy")

    def side(value):
        return value.reshape(levels * 8, LANES)

    case = jnp.where(gy == 0, 0, jnp.where(gy == ny - 1, 2, 1))
    extra = slice(levels * PER_LEVEL, levels * (PER_LEVEL + 1))
    far_a, far_b = side(got_a[extra]), side(got_b[extra])
    value = three_dots(side(own_rows[extra]), row_highs[case, 0], row_lows[case, 0])
    value = value + three_dots(jnp.where(up_a, far_b, far_a), row_highs[case, 1], row_lows[case, 1])
    value = value + three_dots(jnp.where(up_a, far_a, far_b), row_highs[case, 2], row_lows[case, 2])
    beyond[...] = jnp.sum(value.reshape(levels, 8, LANES) * factors[...], axis=1) * (1.0 / 7.0)

    lane = lax.broadcasted_iota(jnp.int32, (8, LANES), 1)
    second = lane < 64
    weight = jnp.float32(generations[0][1])
    keep = jnp.where((gy == 0) | (gy == ny - 1), 0.0, 1.0).astype(F32)
    for level in range(levels):
        base = level * PER_LEVEL
        value = coarse[level, 0]
        below = [jnp.where(up_a, keep * got_b[base + 8 + r], got_a[base + 8 + r]) for r in range(6)]
        below = coarse_rows(below, lane)
        for j in range(8):
            value = value + double_taps[j + 1] * below[7 - j]
        above = jnp.where(up_a, got_a[base + 8], keep * got_b[base + 8])
        value = value + jnp.where(second, 0.0, double_taps[8] * above)
        packed[level * 8:level * 8 + 8, :] = value * coarse_scale(lane)
    refined = exact_dot(packed[...], refining[...])
    for rows in earlier:
        first_row[:first, :] = rows[...]
    for level in range(levels):
        base = level * PER_LEVEL
        value = fine[level, 0]
        for j in range(8):
            value = value + double_taps[j + 1] * jnp.where(up_a, keep * got_b[base + 7 - j], got_a[base + 7 - j])
        value = turned[level, 0] * (weight * value + refined[level * 8:level * 8 + 8, :])
        first_row[first + level:first + level + 1, :LANES] = jnp.sum(value, axis=0, keepdims=True) * (1.0 / 7.0)
    first_row[first:, LANES:] = beyond[...]


def combine_kernel(chunk, levels, height, fine, coarse, got_a, got_b, turned, refining, combined, stacked, refined):
    blocks = height // GROUP
    half, quarter = height // 2, height // 4
    first = chunk * levels
    up_a = lax.axis_index("gy") % 2 == 0
    lane = lax.broadcasted_iota(jnp.int32, (8, LANES), 1)
    second = lane < 64
    scale = coarse_scale(lane)
    weight = jnp.float32(generations[0][1])
    gy, ny = lax.axis_index("gy"), lax.axis_size("gy")
    keep = jnp.where((gy == 0) | (gy == ny - 1), 0.0, 1.0).astype(F32)

    def level_step(level, _):
        def north(r):
            return jnp.where(up_a, got_a[level * PER_LEVEL + r], keep * got_b[level * PER_LEVEL + r])

        def south(r):
            return jnp.where(up_a, keep * got_b[level * PER_LEVEL + r], got_a[level * PER_LEVEL + r])

        below = coarse_rows([south(8 + r) for r in range(6)], lane)
        above = coarse_rows([north(8 + r) for r in range(6)], lane)
        fine_south = outside(lambda j: south(7 - j))
        coarse_south = outside(lambda j: below[7 - j])
        fine_north = outside(north)
        coarse_north = outside(lambda j: above[j])
        parts = []
        for r in range(half):
            value = coarse[level, r]
            if r < 8:
                value = value + coarse_south[r]
            if r < quarter:
                i = quarter - 1 - r
                value = value + jnp.where(second, 0.0, coarse_north[i])
            if r >= half - 8:
                value = value + jnp.where(second, coarse_north[half - 1 - r], 0.0)
            parts.append(value * scale)
        for r in range(half):
            stacked[r * 8:r * 8 + 8, :] = jnp.where(second, parts[r], parts[r // 2])
        refined[...] = exact_dot(stacked[...], refining[...])
        for block in range(blocks):
            weighted = []
            for line in range(GROUP):
                y = block * GROUP + line
                value = fine[level, y]
                if y < 8:
                    value = value + fine_south[y]
                if y >= height - 8:
                    value = value + fine_north[height - 1 - y]
                value = weight * value + refined[y // 2 * 8:y // 2 * 8 + 8, :]
                weighted.append(turned[level, y] * value)
            total = jnp.sum(jnp.swapaxes(jnp.stack(weighted), 0, 1), axis=0)
            combined[level, block * GROUP:(block + 1) * GROUP, :] = total * (1.0 / 7.0)
        return 0

    lax.fori_loop(0, levels, level_step, 0, unroll=4)


def interpolate_levels(combined, beyond, north, first, start, part, interpolation, extended, rows):
    height = combined.shape[1]
    lane = lax.broadcasted_iota(jnp.int32, (height, LANES), 1)
    line = lax.broadcasted_iota(jnp.int32, (height, LANES), 0)
    for i in range(part):
        level = start + i
        here = combined[level]
        last = jnp.broadcast_to(beyond[level:level + 1, :], (height, LANES))
        last = jnp.sum(jnp.where(lane == line, last, 0.0), axis=1, keepdims=True)
        extended[0, i, 0:height, :] = here
        extended[1, i, 0:height, :] = jnp.where(lane == LANES - 1, last, pltpu.roll(here, LANES - 1, 1))
        for half in range(2):
            if north is None:
                extended[half, i, height:height + 1, :] = jnp.zeros((1, LANES), F32)
            else:
                extended[half, i, height:height + 1, :] = north[half][first + level:first + level + 1, :]
            value = extended[half, i, 0:height, :]
            rows[half, i, pl.ds(0, height, 2), :] = value
            rows[half, i, pl.ds(1, height, 2), :] = 0.5 * (value + extended[half, i, 1:height + 1, :])
    value = exact_dot(
        jnp.concatenate([rows[half].reshape(part * 2 * height, LANES) for half in range(2)], axis=1), interpolation[...]
    )
    return value.reshape(part, 2 * height, interpolation.shape[1])


def early_kernel(combined, beyond, interpolation, out, tails, extended, rows, ready, sems):
    levels = combined.shape[0]
    part = levels // 2
    done = ready.shape[1] - 8
    copies = []
    for start in range(0, levels, part):
        span = pl.ds(start, part)
        ready[span] = interpolate_levels(combined, beyond, None, 0, start, part, interpolation, extended, rows)
        copies.append(pltpu.make_async_copy(ready.at[span, pl.ds(0, done)], out.at[span, pl.ds(0, done)], sems.at[start // part]))
        copies[-1].start()
    tails[...] = ready[:, done:, :]
    for copy in copies:
        copy.wait()


def late_kernel(first, before, combined, beyond, north, interpolation, tails, out, extended, rows, ready, ends, kept, shifted, sems):
    levels = combined.shape[0]
    part = levels // 2
    lane = lax.broadcasted_iota(jnp.int32, shifted.shape, 1)
    inside = jnp.where(lax.axis_index("gy") == lax.axis_size("gy") - 1, 0.0, 1.0).astype(F32)
    corner = jnp.broadcast_to(north[:, LANES:LANES + 1], shifted.shape) * inside
    after = north[:, :LANES] * inside
    kept[...] = after
    shifted[...] = jnp.where(lane == LANES - 1, corner, pltpu.roll(after, LANES - 1, 1))
    copies = []
    row = 0.5 * exact_dot(jnp.concatenate([after, shifted[...]], axis=1), interpolation[...])
    ends[...] = tails[...]
    for level in range(first):
        ends[level, 7:8, :] = ends[level, 7:8, :] + row[level:level + 1, :]
    done = ready.shape[1] - 8
    copies.append(pltpu.make_async_copy(ends, out.at[pl.ds(0, first), pl.ds(done, 8)], sems.at[2]))
    copies[-1].start()
    for start in range(0, levels, part):
        span = pl.ds(start, part)
        rows_north = (kept, shifted)
        ready[span] = interpolate_levels(combined, beyond, rows_north, first, start, part, interpolation, extended, rows)
        copies.append(pltpu.make_async_copy(ready.at[span], out.at[pl.ds(first + start, part)], sems.at[start // part]))
        copies[-1].start()
    for copy in copies:
        copy.wait()


def around(value, axis, step):
    size = lax.axis_size(axis)
    return lax.ppermute(value, axis, [(i, (i + step) % size) for i in range(size)])


def swap(value, second):
    nx, ny = lax.axis_size("gx"), lax.axis_size("gy")
    pairs = []
    for x in range(nx):
        for y in range(ny):
            other = ((y + 1) ^ 1) - 1 if second else y ^ 1
            pairs.append((x * ny + y, x * ny + other if 0 <= other < ny else (x ^ 1) * ny + y))
    return lax.ppermute(value, ("gx", "gy"), pairs)


def call(kernel, outs, scratch, cost, *args, in_hbm=0):
    vmem = pl.BlockSpec(memory_space=pltpu.VMEM)
    return pl.pallas_call(
        kernel,
        out_shape=tuple(jax.ShapeDtypeStruct(*out) if isinstance(out[0], tuple) else jax.ShapeDtypeStruct(out, F32) for out in outs),
        in_specs=[pl.BlockSpec(memory_space=pltpu.HBM) if i < in_hbm else vmem for i in range(len(args))],
        out_specs=tuple(vmem for _ in outs),
        scratch_shapes=[pltpu.VMEM(shape, F32) if isinstance(shape, tuple) else shape for shape in scratch],
        compiler_params=pltpu.CompilerParams(vmem_limit_bytes=VMEM_LIMIT),
        cost_estimate=pl.CostEstimate(flops=cost, bytes_accessed=2**20, transcendentals=0),
    )(*args)


def halves_of(table):
    high = table.astype(np.float32).astype(BF16)
    return high, (table.astype(np.float32) - high.astype(np.float32)).astype(BF16)


def shards(gradient, members):
    all_levels, fine_height, fine_width = gradient.shape
    count, _, height, width = members.shape
    assert count == 8 and width == LANES and height == 32 and lax.axis_size("gx") % 2 == 0 and lax.axis_size("gy") % 2 == 0
    assert all_levels % CHUNKS == 0
    levels = all_levels // CHUNKS
    groups = levels * height // GROUP

    south = around(gradient[:, -1, :], "gy", 1)

    columns = [column_table(width, i == 0, i == 2) for i in range(3)]
    own_tables = np.stack(halves_of(np.stack([table[:width] for table in columns])), axis=1)
    halo_tables = np.stack(halves_of(np.stack([halo_table(table, width, i == 0) for i, table in enumerate(columns)])), axis=1)
    places = halo_places()
    restrict = jnp.asarray(restriction_table(width), BF16)
    packing = jnp.asarray(packing_table(width), BF16).reshape(GROUP * width, 2 * LANES)
    refining = jnp.asarray(refining_table(width), BF16)
    interpolation = jnp.asarray(interpolation_table(width), BF16)
    beyond_high, beyond_low = map(jnp.asarray, halves_of(column_filter_table(width)))
    row_highs, row_lows = map(jnp.asarray, halves_of(np.stack([column_rows_table(height, i == 0, i == 2) for i in range(3)])))
    choice = jnp.asarray(edge_choice_table(), BF16)
    flops = 10**9 // CHUNKS
    far_rows = (levels * (PER_LEVEL + 1), 8, LANES)

    hbm_of = functools.partial(pltpu.with_memory_space_constraint, memory_space=pltpu.HBM)
    constants = tuple(map(hbm_of, (jnp.asarray(own_tables), jnp.asarray(halo_tables), jnp.asarray(places, BF16), interpolation)))
    gradient, members, far_restrict = map(hbm_of, (gradient, members, restrict))
    prepared, packed = [], []
    for chunk in range(CHUNKS):
        outs = [(2, levels, 8 + 2 * height, LANES), (levels, height, 8, LANES), (levels * height, LANES)]
        scratch = [(levels, fine_height, fine_width), (8, levels, height, LANES), pltpu.VMEM(restrict.shape, BF16)]
        if chunk == 0:
            outs += [((4, 2 * LANES, 2 * LANES), BF16), ((4, 2 * LANES, 2 * LANES), BF16), (interpolation.shape, BF16)]
            scratch += [pltpu.VMEM(shape, BF16) for shape in (own_tables.shape[1:], halo_tables.shape[1:], places.shape)]
        extra = constants if chunk == 0 else (packed[-1][3],)
        prepared.append(call(
            functools.partial(prepare_kernel, chunk, levels, height), outs, scratch + [pltpu.SemaphoreType.DMA((9,))],
            flops, gradient, members, far_restrict, *extra, in_hbm=3 if chunk else 7,
        ))
        packed.append(call(
            functools.partial(pack_kernel, chunk, levels, height),
            [(GROUP, groups * 8, LANES), (groups * 8, LANES), (groups * 8, LANES), (3, levels, 8, LANES), (7, levels // 2, 8, LANES)],
            [(2, height, LANES), (2, all_levels, LANES)],
            flops, *prepared[-1][:3], south, restrict, packing,
        ))
    high_weights, low_weights, interpolation = prepared[0][3:]
    got = [(around(to_east, "gx", 1), around(to_west, "gx", -1)) for *_, to_east, to_west in packed]
    filtered = [
        call(
            functools.partial(columns_kernel, levels, height),
            [(groups, GROUP, 8, 2 * LANES), far_rows, far_rows, (levels, 8, LANES)],
            [],
            flops, *packed[chunk][:3], *got[chunk], high_weights, low_weights, beyond_high, beyond_low, choice,
        )
        for chunk in range(CHUNKS)
    ]
    far = [(swap(rows_a, False), swap(rows_b, True)) for _, rows_a, rows_b, _ in filtered]
    own = [
        call(
            functools.partial(own_rows_kernel, levels, height),
            [(levels, height, 8, LANES), (levels, height // 2, 8, LANES)],
            [],
            flops, filtered[chunk][0],
        )
        for chunk in range(CHUNKS)
    ]
    part = levels // 2
    buffers = [(2, part, height + 8, LANES), (2, part, 2 * height, LANES), (levels, fine_height, fine_width)]
    vmem, hbm = pl.BlockSpec(memory_space=pltpu.VMEM), pl.BlockSpec(memory_space=pltpu.HBM)
    out_shape = jax.ShapeDtypeStruct(gradient.shape, F32)
    params = pltpu.CompilerParams(vmem_limit_bytes=VMEM_LIMIT)
    cost = pl.CostEstimate(flops=flops, bytes_accessed=2**20, transcendentals=0)

    def first_rows_of(chunk, *earlier):
        return call(
            functools.partial(first_row_kernel, chunk, levels, height),
            [(levels, LANES), ((chunk + 1) * levels, 2 * LANES)],
            [(levels * 8, LANES)],
            flops, *own[chunk], *far[chunk], filtered[chunk][1], filtered[chunk][3], prepared[chunk][1], refining, row_highs, row_lows, *earlier,
        )

    def combined_of(chunk):
        return call(
            functools.partial(combine_kernel, chunk, levels, height),
            [(levels, height, LANES)],
            [(height // 2 * 8, LANES), (height // 2 * 8, LANES)],
            flops, *own[chunk], *far[chunk], prepared[chunk][1], refining,
        )[0]

    early_beyond, early_rows = first_rows_of(0)
    out, tails = pl.pallas_call(
        early_kernel,
        out_shape=(out_shape, jax.ShapeDtypeStruct((levels, 8, fine_width), F32)),
        in_specs=[vmem] * 3, out_specs=(hbm, vmem),
        scratch_shapes=[pltpu.VMEM(shape, F32) for shape in buffers] + [pltpu.SemaphoreType.DMA((2,))],
        compiler_params=params, cost_estimate=cost,
    )(combined_of(0), early_beyond, interpolation)
    beyond, rows = first_rows_of(1, early_rows, tails)
    north = around(rows, "gy", -1)
    out = pl.pallas_call(
        functools.partial(late_kernel, levels),
        out_shape=out_shape,
        in_specs=[hbm] + [vmem] * 5, out_specs=hbm,
        scratch_shapes=[pltpu.VMEM(shape, F32) for shape in buffers + [(levels, 8, fine_width), (all_levels, LANES), (all_levels, LANES)]]
        + [pltpu.SemaphoreType.DMA((3,))],
        input_output_aliases={0: 0},
        compiler_params=params, cost_estimate=cost,
    )(out, combined_of(1), beyond, north, interpolation, tails)
    return out


def solution(mesh):
    in_specs = (P(None, "gy", "gx"), P(None, None, "gy", "gx"))
    out_specs = P(None, "gy", "gx")
    return jax.shard_map(shards, mesh=mesh, in_specs=in_specs, out_specs=out_specs, check_vma=False)
```

```python
import functools

import jax
import jax.numpy as jnp
import numpy as np
from jax import lax
from jax.experimental import pallas as pl
from jax.experimental.pallas import tpu as pltpu
from jax.sharding import PartitionSpec as P


beta_raw = [(1.0 - (offset - 4) ** 2 / 25.0) ** 2 for offset in range(9)]
beta_taps = [value / sum(beta_raw) for value in beta_raw]
generations = ((1, 0.5), (2, 0.075), (4, 0.0125))

LANES = 128
GROUP = 8
SLOTS = (12, 14)
FREE = (8, 9)
USED = (8 * 12, 8 * 14)
COMPACT = 64
COLUMN = 32
CHUNKS = 2
PARTS = 4
VMEM_LIMIT = 20 * 2**20
BF16, F32 = jnp.bfloat16, jnp.float32
double_taps = [
    sum(beta_taps[k + 4] * beta_taps[offset - k + 4] for k in range(-4, 5) if -4 <= offset - k <= 4) for offset in range(9)
]
edge_taps = [
    [sum(beta_taps[i - k + 4] * beta_taps[k - j + 4] for k in range(-4, 0) if i - k <= 4 and j - k <= 4) for j in range(4)]
    for i in range(4)
]


def twice_filter(width, first, last):
    low, high = (0 if first else -99), (width - 1 if last else width + 99)
    table = np.zeros((width + 17, width + 1))
    for source in range(-8, width + 9):
        if not low <= source <= high:
            continue
        for middle in range(source - 4, source + 5):
            if not low <= middle <= high:
                continue
            for target in range(max(0, middle - 4), min(width, middle + 4) + 1):
                if target <= high:
                    table[source + 8, target] += beta_taps[middle - source + 4] * beta_taps[target - middle + 4]
    return table


def column_table(width, first, last):
    filters = {factor: twice_filter(width // factor, first, last) for factor, _ in generations}
    base = {1: 0, 2: LANES, 4: LANES + width // 2}

    def row(places):
        out = np.zeros(2 * LANES)
        for factor, place in places.items():
            count = width // factor
            out[base[factor]:base[factor] + count] += filters[factor][place + 8, :count]
        return out

    rows = [row({1: c, 2: c // 2, 4: c // 4}) for c in range(width)]
    rows += [row({1: c, 2: c // 2, 4: c // 4}) for c in range(-8, 0)]
    rows += [row({2: c, 4: c // 2}) for c in range(-8, -4)]
    rows += [row({4: c}) for c in range(-8, -4)]
    rows += [row({1: c, 2: c // 2, 4: c // 4}) for c in range(width, width + 8)] + [row({1: width + 8})]
    half, quarter = width // 2, width // 4
    rows += [row({2: c, 4: c // 2}) for c in range(half + 4, half + 8)] + [row({2: half + 8})]
    rows += [row({4: c}) for c in range(quarter + 4, quarter + 9)]
    return np.stack(rows)


def edge_lane(side, line):
    return SLOTS[side] * (line // 4 * 4 + 3) + FREE[side] + line % 4


def message_lanes():
    places = []
    for line in range(GROUP):
        for side, (first, second, fourth) in enumerate(((0, 8, 12), (16, 25, 30))):
            start = line * SLOTS[side]
            places += [(side, start + c, first + c, 1, line, line) for c in range(FREE[side])]
            rest = [start + c for c in range(FREE[side], SLOTS[side])]
            if line % 2 == 0:
                places += [(side, lane, second + c, 2, line, line) for c, lane in enumerate(rest)]
            if line % 4 == 1:
                places += [(side, lane, fourth + c, 4, line - 1, line) for c, lane in enumerate(rest)]
    return places


def packing_table(width):
    table = np.zeros((GROUP, width, 2 * LANES), np.float32)
    east = list(range(width - 8, width)) + [width // 2 - 8 + c for c in range(4)] + [width // 4 - 8 + c for c in range(4)]
    west = list(range(9)) + [4 + c for c in range(5)] + [4 + c for c in range(5)]
    for side, lane, compact, factor, line, _ in message_lanes():
        start = (west[compact - 16] if side else east[compact]) * factor
        table[line:line + factor, start:start + factor, side * LANES + lane] = 1.0
    return table


def halo_table(columns, width, first):
    table = np.zeros((COMPACT, 2 * LANES))
    table[:35] = columns[width:]
    table[35] = 0.0 if first else columns[0]
    return table


def halo_places():
    table = np.zeros((4, LANES, COMPACT), np.float32)
    for side, lane, compact, _, _, line in message_lanes():
        if line < 4:
            table[line, side * 64 + lane, compact] = 1.0
    for line in range(4):
        table[line, edge_lane(0, line), 35] = 1.0
        table[line, 64 + edge_lane(1, line), 16] = 1.0
    return table


def restriction_table(width):
    table = np.zeros((2 * width, 2 * LANES), np.float32)
    for i in range(width):
        table[2 * i, i] += 1.0
        table[2 * i + 1, i] += 0.5
        table[2 * i + 1, i + 1] += 0.5
    return table


def refining_table(width):
    table = np.zeros((LANES, LANES), np.float32)
    for i in range(width):
        table[i // 2, i] = 1.0
        table[width // 2 + i // 4, i] = 1.0
    return table


def column_lane(factor, row):
    count = GROUP // factor
    return row // count * COLUMN + {1: 0, 2: 8, 4: 12}[factor] + row % count


def column_filter_table(width):
    table = np.zeros((2 * LANES, LANES))
    filters = {factor: twice_filter(width // factor, False, False)[:, width // factor] for factor, _ in generations}
    low = [width - 8 + c for c in range(8)] + [width // 2 - 8 + c for c in range(4)] + [width // 4 - 8 + c for c in range(4)]
    high = [width + c for c in range(9)] + [width // 2 + 4 + c for c in range(5)] + [width // 4 + 4 + c for c in range(5)]
    ends = {(1, 16 + 8): 1, (2, 25 + 4): 2}
    for side, lane, compact, factor, line, _ in message_lanes():
        place = (high[compact - 16] if side else low[compact]) * factor
        for generation, _ in generations:
            if generation >= factor and generation <= ends.get((factor, compact), 4):
                weight = filters[generation][place // generation + 8]
                table[side * LANES + lane, column_lane(generation, line // generation)] += weight
    for line in range(GROUP):
        for generation, _ in generations:
            weight = filters[generation][width // generation + 8]
            table[LANES + edge_lane(1, line), column_lane(generation, line // generation)] += weight
    return table


def column_rows_table(height, first, last):
    table = np.zeros((3, LANES, LANES))
    for factor, weight in generations:
        count = height // factor
        filters = twice_filter(count, first, last)
        for row in range(height):
            for source in range(-8, count + 8):
                kind, place = (1, source + count) if source < 0 else (2, source - count) if source >= count else (0, source)
                table[kind, column_lane(factor, place), row] += weight * filters[source + 8, row // factor]
    return table


def edge_choice_table():
    table = np.zeros((LANES, LANES), np.float32)
    for line in range(GROUP):
        table[edge_lane(1, line), line] = 1.0
    return table


def interpolation_table(width):
    table = np.zeros((2 * LANES, 2 * width), np.float32)
    for i in range(width):
        table[i, 2 * i] = 1.0
        table[i, 2 * i + 1] = 0.5
        table[LANES + i, 2 * i + 1] = 0.5
    return table


def split(value):
    high = value.astype(BF16)
    return high, (value - high.astype(F32)).astype(BF16)


def mul(a, b):
    return jnp.dot(a, b, preferred_element_type=F32)


def exact_dot(value, table):
    high, low = split(value)
    return mul(high, table) + mul(low, table)


def three_dots(value, high_table, low_table):
    high, low = split(value)
    return mul(high, high_table) + mul(low, high_table) + mul(high, low_table)


def column_case():
    gx, nx = lax.axis_index("gx"), lax.axis_size("gx")
    return jnp.where(gx == 0, 0, jnp.where(gx == nx - 1, 2, 1))


def tile(index):
    return pl.ds(pl.multiple_of(index * 8, 8), 8)


def turn_members(height, raw, first, turned, edges, start, stop, rims=None):
    blocks = height // GROUP
    lane = lax.broadcasted_iota(jnp.int32, (GROUP, LANES), 1)
    up_a = lax.axis_index("gy") % 2 == 0

    def level_step(level, _):
        ends = []
        for block in range(blocks):
            edge = jnp.zeros((GROUP, LANES), F32)
            span = slice(block * GROUP, (block + 1) * GROUP)
            block_rows = jnp.swapaxes(raw[:, first + level, span, :], 0, 1)
            turned[level, span] = block_rows
            for line in range(GROUP):
                spot = edge_lane(1, line)
                edge = jnp.where(lane == spot, pltpu.roll(block_rows[line], spot, 1), edge)
            edges[tile(level * blocks + block), :] = edge
            ends.append(block_rows)
        if rims:
            rims[0][level] = jnp.where(up_a, ends[-1], ends[0])
            rims[1][level] = jnp.where(up_a, ends[0], ends[-1])
        return 0

    lax.fori_loop(start, stop, level_step, 0, unroll=4)


def reduce_columns(fine, first, count, height, table, across, start):
    value = exact_dot(fine[first:first + count].reshape(count * 2 * height, fine.shape[2]), table[...])
    value = value.reshape(count, 2 * height, 2 * LANES)
    for half in range(2):
        across[half, start:start + count, 8:, :] = value[:, :, half * LANES:(half + 1) * LANES]
        across[half, start:start + count, 0:8, :] = jnp.zeros((count, 8, LANES), F32)


def prepare_kernel(levels, height, gradient, members, restrict, own_tables, halo_tables, places, refine,
                   across, turned, edges, high_weights, low_weights, refine_out, fine, raw, table, own_case, halo_case, placing, sems):
    part = levels // 2
    case = column_case()
    moves = [(restrict, table)]
    moves += [(gradient.at[pl.ds(i * part, part)], fine.at[pl.ds(i * part, part)]) for i in range(2)]
    moves += [(members.at[:, pl.ds(i * part, part)], raw.at[:, pl.ds(i * part, part)]) for i in range(2)]
    moves += [(own_tables.at[case], own_case), (halo_tables.at[case], halo_case), (places, placing), (refine, refine_out)]
    copies = [pltpu.make_async_copy(source, target, sems.at[i]) for i, (source, target) in enumerate(moves)]
    for copy in copies:
        copy.start()
    copies[0].wait()
    for i in range(2):
        copies[1 + i].wait()
        reduce_columns(fine, i * part, part, height, table, across, i * part)
    for i in range(2):
        copies[3 + i].wait()
        turn_members(height, raw, 0, turned, edges, i * part, (i + 1) * part)
    for copy in copies[5:]:
        copy.wait()
    for which, target in ((0, high_weights), (1, low_weights)):
        for variant in range(4):
            target[variant, :LANES, :] = own_case[which]
            target[variant, LANES:, :] = mul(placing[variant], halo_case[which]).astype(BF16)


def prepare_more_kernel(chunk, levels, height, gradient, members, restrict, _, across, turned, edges, rim_a, rim_b):
    reduce_columns(gradient, chunk * levels, levels, height, restrict, across, 0)
    turn_members(height, members, chunk * levels, turned, edges, 0, levels, (rim_a, rim_b))


def pack_kernel(chunk, levels, height, across, turned, edges, south, restrict, packing, products, own_east, own_west, to_east, to_west,
                coarse, below):
    blocks = height // GROUP
    first = chunk * levels
    value = exact_dot(south[...], restrict[...]) * jnp.where(lax.axis_index("gy") == 0, 0.0, 1.0).astype(F32)
    for half in range(2):
        below[half] = value[:, half * LANES:(half + 1) * LANES]
    lane = lax.broadcasted_iota(jnp.int32, (GROUP, LANES), 1)
    line_of = lax.broadcasted_iota(jnp.int32, (GROUP, LANES), 0)
    spots = (line_of >> 2) * (4 * SLOTS[0]) + edge_lane(0, 0) + (line_of & 3)
    top = lax.broadcasted_iota(jnp.int32, (height, LANES), 0) == 0

    def level_step(level, _):
        for half in range(2):
            under = jnp.broadcast_to(below[half, pl.ds(first + level, 1), :], (height, LANES))
            under = jnp.where(top, under, across[half, level, pl.ds(7, height, 2), :])
            coarse[half] = across[half, level, pl.ds(8, height, 2), :] + 0.5 * (
                across[half, level, pl.ds(9, height, 2), :] + under
            )
        for block in range(blocks):
            place_rows = tile(level * blocks + block)
            for line in range(GROUP):
                y = block * GROUP + line
                products[line, place_rows, :] = turned[level, y] * coarse[0, y:y + 1, :]
            column = jnp.broadcast_to(coarse[1, block * GROUP:(block + 1) * GROUP, 0:1], (GROUP, LANES))
            column = jnp.sum(jnp.where(lane == spots, column, 0.0), axis=0, keepdims=True)
            own_east[place_rows, :] = jnp.broadcast_to(column, (GROUP, LANES))
        return 0

    lax.fori_loop(0, levels, level_step, 0, unroll=4)
    total = jnp.zeros((levels * blocks * 8, 2 * LANES), F32)
    for line in range(0, GROUP, 2):
        value = jnp.concatenate([products[line], products[line + 1]], axis=1)
        total = total + exact_dot(value, packing[line * LANES:(line + 2) * LANES, :])
    own_east[...] = own_east[...] + total[:, :LANES]
    own_west[...] = total[:, LANES:] + edges[...]
    lane = lax.broadcasted_iota(jnp.int32, (levels, 8, LANES), 2)
    groups = [own_east[...].reshape(levels, 4, 8, LANES)[:, i] for i in range(4)]
    for i in range(3):
        to_east[i] = jnp.where(lane < USED[0], groups[i], pltpu.roll(groups[3], USED[0] - 32 * i, 2))
    lane = lane[:levels // 2]
    groups = [own_west[...].reshape(levels // 2, 8, 8, LANES)[:, i] for i in range(8)]
    for i in range(7):
        to_west[i] = jnp.where(lane < USED[1], groups[i], pltpu.roll(groups[7], USED[1] - 16 * i, 2))


def outside(load):
    values = [load(j) for j in range(8)]
    result = []
    for i in range(8):
        total = double_taps[i + 1] * values[0]
        for j in range(1, 8 - i):
            total = total + double_taps[i + 1 + j] * values[j]
        result.append(total)
    return result


def per_level_of(chunk):
    return 7 if chunk else 14


def columns_kernel(chunk, levels, height, products, own_a, own_b, from_west, from_east, high_weights, low_weights,
                   beyond_high, beyond_low, choice, *refs):
    if chunk:
        rims, refs, weighted = refs[:2], refs[3:-1], refs[-1]
    else:
        refs = refs[1:]
    filtered, message_a, message_b, factors = refs
    per_level = per_level_of(chunk)
    blocks = height // GROUP
    groups = levels * blocks
    lane = lax.broadcasted_iota(jnp.int32, (groups * 8, LANES), 1)
    own_east, own_west = own_a[...], own_b[...]
    whole = lax.broadcasted_iota(jnp.int32, (levels, 8, LANES), 2)
    parts = [from_west[i] for i in range(3)]
    last = pltpu.roll(parts[2], 96, 2)
    for i in range(2):
        last = jnp.where((whole >= 32 * i) & (whole < 32 * i + 32), pltpu.roll(parts[i], 32 * i + 32, 2), last)
    west = jnp.stack(parts + [last], axis=1).reshape(groups * 8, LANES)
    whole = whole[:levels // 2]
    parts = [from_east[i] for i in range(7)]
    last = pltpu.roll(parts[6], 112, 2)
    for i in range(6):
        last = jnp.where((whole >= 16 * i) & (whole < 16 * i + 16), pltpu.roll(parts[i], 16 * i + 16, 2), last)
    east = jnp.stack(parts + [last], axis=1).reshape(groups * 8, LANES)
    chosen = exact_dot(east, choice[...]).reshape(levels, blocks, 8, LANES)
    total = chosen[:, 0]
    for block in range(1, blocks):
        total = total + pltpu.roll(chosen[:, block], block * GROUP, 2)
    factors[...] = total
    shifts = [edge_lane(1, line) - edge_lane(0, line) for line in (0, 4)]
    for line, shift in zip((0, 4), shifts):
        spot = (lane >= edge_lane(0, line)) & (lane < edge_lane(0, line) + 4)
        west = jnp.where(spot, west * pltpu.roll(own_west, LANES - shift, 1), west)
        spot = (lane >= edge_lane(1, line)) & (lane < edge_lane(1, line) + 4)
        east = jnp.where(spot, east * pltpu.roll(own_east, shift, 1), east)
    inside = jnp.where(lax.axis_index("gx") == lax.axis_size("gx") - 1, 0.0, 1.0).astype(F32)
    beyond = three_dots(jnp.concatenate([own_east, east], axis=1), beyond_high[...], beyond_low[...])
    beyond = (beyond * inside).reshape(levels, blocks, 8, LANES)
    total = beyond[:, 0]
    for block in range(1, blocks):
        total = total + pltpu.roll(beyond[:, block], block * COLUMN, 2)
    for message in (message_a, message_b):
        message[levels * per_level:] = total
    halves = [
        split(jnp.where(lane < 64, west, pltpu.roll(east, 64, 1))),
        split(jnp.where(lane < 64, pltpu.roll(west, LANES - USED[0] // 2, 1), pltpu.roll(east, 64 - USED[1] // 2, 1))),
    ]
    for line in range(GROUP):
        high, low = (jnp.concatenate(pair, axis=1) for pair in zip(split(products[line]), halves[line // 4]))
        weights = high_weights[line % 4]
        value = mul(high, weights) + mul(low, weights) + mul(high, low_weights[line % 4])
        filtered[:, line] = value.reshape(groups, 8, 2 * LANES)
    small = lax.broadcasted_iota(jnp.int32, (8, LANES), 1)
    second = small < 64
    up_a = lax.axis_index("gy") % 2 == 0
    start_a, start_b = jnp.where(up_a, blocks - 1, 0), jnp.where(up_a, 0, blocks - 1)
    coarse_a, coarse_b = jnp.where(up_a, blocks - 2, 0), jnp.where(up_a, 0, blocks - 2)

    def level_step(level, _):
        def at(block, line):
            return filtered[level * blocks + block, line, :, LANES:]

        fourth = []
        for block in range(blocks):
            for half in range(2):
                fourth.append(sum(at(block, half * 4 + k) for k in range(1, 4)) + at(block, half * 4))
        sides = ((message_a, start_a, coarse_a, up_a), (message_b, start_b, coarse_b, jnp.logical_not(up_a)))
        for side, (message, start, coarse, upward) in enumerate(sides):
            if chunk:
                def nearest(j):
                    return filtered[level * blocks + start, jnp.where(upward, 7 - j, j), :, :LANES]

                for i, value in enumerate(outside(nearest)):
                    place = jnp.where(upward, i, 7 - i)
                    weighted[side, place] = rims[side][level, place] * value
                total = jnp.sum(jnp.swapaxes(weighted[side], 0, 1), axis=0)
                message[level * per_level] = jnp.float32(generations[0][1]) * total
            rows = []
            for line in range(GROUP):
                if not chunk:
                    message[level * per_level + line] = filtered[level * blocks + start, line, :, :LANES]
                block, pair = coarse + line // 4, line % 4
                pairs = at(block, 2 * pair) + at(block, 2 * pair + 1)
                rows.append(jnp.where(second, pairs, fourth[line]))
            for i in range(6):
                spare = pltpu.roll(rows[6 + i // 3], 96 - 32 * (i % 3), 1)
                message[level * per_level + per_level - 6 + i] = jnp.where(small < 96, rows[i], spare)
        return 0

    lax.fori_loop(0, levels, level_step, 0, unroll=4)


def convolve_own(load, count, low_edges, high_edges, store):
    rows = {}

    def row(r):
        if r not in rows:
            rows[r] = load(r)
        return rows[r]

    for r in range(count):
        value = double_taps[0] * row(r)
        for k in range(1, 9):
            near = [row(q) for q in (r - k, r + k) if 0 <= q < count]
            if near:
                value = value + double_taps[k] * (near[0] if len(near) == 1 else near[0] + near[1])
        if r < 4:
            fix = edge_taps[r][0] * row(0)
            for j in range(1, 4):
                fix = fix + edge_taps[r][j] * row(j)
            value = value - low_edges * fix
        for flag, end in high_edges:
            i = end - 1 - r
            if 0 <= i < 4:
                fix = edge_taps[i][0] * row(end - 1)
                for j in range(1, 4):
                    fix = fix + edge_taps[i][j] * row(end - 1 - j)
                value = value - flag * fix
        store(r, value)
        rows.pop(r - 8, None)


def own_rows_kernel(levels, height, filtered, fine, coarse):
    blocks = height // GROUP
    half, quarter = height // 2, height // 4
    gy, ny = lax.axis_index("gy"), lax.axis_size("gy")
    low, high = jnp.where(gy == 0, 1.0, 0.0).astype(F32), jnp.where(gy == ny - 1, 1.0, 0.0).astype(F32)
    second = lax.broadcasted_iota(jnp.int32, (8, LANES), 1) < 64
    high_second, high_fourth = jnp.where(second, high, 0.0), jnp.where(second, 0.0, high)

    def level_step(level, _):
        def at(y, part):
            return filtered[level * blocks + y // 8, y % 8, :, part * LANES:(part + 1) * LANES]

        def store_to(ref):
            def store(r, value):
                ref[level, r] = value

            return store

        convolve_own(lambda r: at(r, 0), height, low, [(high, height)], store_to(fine))

        def pair(r):
            return at(2 * r, 1) + at(2 * r + 1, 1)

        def load_coarse(r):
            return jnp.where(second, pair(r), pair(2 * r) + pair(2 * r + 1) if r < quarter else 0.0)

        convolve_own(load_coarse, half, low, [(high_second, half), (high_fourth, quarter)], store_to(coarse))
        return 0

    lax.fori_loop(0, levels, level_step, 0, unroll=4)


def coarse_rows(packed, lane):
    rows = list(packed)
    for i in range(2):
        pieces = [pltpu.roll(packed[3 * i + k], 32 + 32 * k, 1) for k in range(3)]
        rows.append(jnp.where(lane < 32, pieces[0], jnp.where(lane < 64, pieces[1], pieces[2])))
    return rows


def coarse_scale(lane):
    return jnp.where(lane < 64, jnp.float32(generations[1][1]), jnp.float32(generations[2][1]))


def first_row_kernel(chunk, levels, fine, coarse, got_a, got_b, own_rows, factors, turned, refining, row_highs, row_lows, *refs):
    earlier, (beyond, first_row, packed) = refs[:1] if chunk else (), refs[-3:]
    first = chunk * levels
    up_a = lax.axis_index("gy") % 2 == 0
    gy, ny = lax.axis_index("gy"), lax.axis_size("gy")

    def side(value):
        return value.reshape(levels * 8, LANES)

    case = jnp.where(gy == 0, 0, jnp.where(gy == ny - 1, 2, 1))
    per_level = per_level_of(chunk)
    skip = per_level - 6
    extra = slice(levels * per_level, levels * (per_level + 1))
    far_a, far_b = side(got_a[extra]), side(got_b[extra])
    value = three_dots(side(own_rows[extra]), row_highs[case, 0], row_lows[case, 0])
    value = value + three_dots(jnp.where(up_a, far_b, far_a), row_highs[case, 1], row_lows[case, 1])
    value = value + three_dots(jnp.where(up_a, far_a, far_b), row_highs[case, 2], row_lows[case, 2])
    beyond[...] = jnp.sum(value.reshape(levels, 8, LANES) * factors[...], axis=1) * (1.0 / 7.0)

    lane = lax.broadcasted_iota(jnp.int32, (8, LANES), 1)
    second = lane < 64
    weight = jnp.float32(generations[0][1])
    keep = jnp.where((gy == 0) | (gy == ny - 1), 0.0, 1.0).astype(F32)
    for level in range(levels):
        base = level * per_level
        value = coarse[level, 0]
        below = [jnp.where(up_a, keep * got_b[base + skip + r], got_a[base + skip + r]) for r in range(6)]
        below = coarse_rows(below, lane)
        for j in range(8):
            value = value + double_taps[j + 1] * below[7 - j]
        above = jnp.where(up_a, got_a[base + skip], keep * got_b[base + skip])
        value = value + jnp.where(second, 0.0, double_taps[8] * above)
        packed[level * 8:level * 8 + 8, :] = value * coarse_scale(lane)
    refined = exact_dot(packed[...], refining[...])
    for rows in earlier:
        first_row[:first, :] = rows[...]
    for level in range(levels):
        base = level * per_level
        value = fine[level, 0]
        if not chunk:
            for j in range(8):
                value = value + double_taps[j + 1] * jnp.where(up_a, keep * got_b[base + 7 - j], got_a[base + 7 - j])
        value = turned[level, 0] * (weight * value + refined[level * 8:level * 8 + 8, :])
        value = jnp.sum(value, axis=0, keepdims=True)
        if chunk:
            value = value + jnp.where(up_a, keep * got_b[base, 0:1, :], got_a[base, 0:1, :])
        first_row[first + level:first + level + 1, :LANES] = value * (1.0 / 7.0)
    first_row[first:, LANES:] = beyond[...]


def combine_kernel(chunk, levels, height, fine, coarse, got_a, got_b, turned, refining, combined, stacked, refined):
    blocks = height // GROUP
    half, quarter = height // 2, height // 4
    per_level = per_level_of(chunk)
    up_a = lax.axis_index("gy") % 2 == 0
    lane = lax.broadcasted_iota(jnp.int32, (8, LANES), 1)
    second = lane < 64
    scale = coarse_scale(lane)
    weight = jnp.float32(generations[0][1])
    gy, ny = lax.axis_index("gy"), lax.axis_size("gy")
    keep = jnp.where((gy == 0) | (gy == ny - 1), 0.0, 1.0).astype(F32)

    def level_step(level, _):
        base = level * per_level

        def north(r):
            return jnp.where(up_a, got_a[base + r], keep * got_b[base + r])

        def south(r):
            return jnp.where(up_a, keep * got_b[base + r], got_a[base + r])

        below = coarse_rows([south(per_level - 6 + r) for r in range(6)], lane)
        above = coarse_rows([north(per_level - 6 + r) for r in range(6)], lane)
        if not chunk:
            fine_south = outside(lambda j: south(7 - j))
            fine_north = outside(north)
        coarse_south = outside(lambda j: below[7 - j])
        coarse_north = outside(lambda j: above[j])
        parts = []
        for r in range(half):
            value = coarse[level, r]
            if r < 8:
                value = value + coarse_south[r]
            if r < quarter:
                i = quarter - 1 - r
                value = value + jnp.where(second, 0.0, coarse_north[i])
            if r >= half - 8:
                value = value + jnp.where(second, coarse_north[half - 1 - r], 0.0)
            parts.append(value * scale)
        for r in range(half):
            stacked[r * 8:r * 8 + 8, :] = jnp.where(second, parts[r], parts[r // 2])
        refined[...] = exact_dot(stacked[...], refining[...])
        for block in range(blocks):
            weighted = []
            for line in range(GROUP):
                y = block * GROUP + line
                value = fine[level, y]
                if y < 8 and not chunk:
                    value = value + fine_south[y]
                if y >= height - 8 and not chunk:
                    value = value + fine_north[height - 1 - y]
                value = weight * value + refined[y // 2 * 8:y // 2 * 8 + 8, :]
                weighted.append(turned[level, y] * value)
            total = jnp.sum(jnp.swapaxes(jnp.stack(weighted), 0, 1), axis=0)
            if chunk and block == 0:
                total = total + south(0)
            if chunk and block == blocks - 1:
                total = total + north(0)
            combined[level, block * GROUP:(block + 1) * GROUP, :] = total * (1.0 / 7.0)
        return 0

    lax.fori_loop(0, levels, level_step, 0, unroll=4)


def interpolate_levels(combined, beyond, north, first, start, part, interpolation, extended, rows):
    height = combined.shape[1]
    lane = lax.broadcasted_iota(jnp.int32, (height, LANES), 1)
    line = lax.broadcasted_iota(jnp.int32, (height, LANES), 0)
    for i in range(part):
        level = start + i
        here = combined[level]
        last = jnp.broadcast_to(beyond[level:level + 1, :], (height, LANES))
        last = jnp.sum(jnp.where(lane == line, last, 0.0), axis=1, keepdims=True)
        extended[0, i, 0:height, :] = here
        extended[1, i, 0:height, :] = jnp.where(lane == LANES - 1, last, pltpu.roll(here, LANES - 1, 1))
        for half in range(2):
            if north is None:
                extended[half, i, height:height + 1, :] = jnp.zeros((1, LANES), F32)
            else:
                extended[half, i, height:height + 1, :] = north[half][first + level:first + level + 1, :]
            value = extended[half, i, 0:height, :]
            rows[half, i, pl.ds(0, height, 2), :] = value
            rows[half, i, pl.ds(1, height, 2), :] = 0.5 * (value + extended[half, i, 1:height + 1, :])
    value = exact_dot(
        jnp.concatenate([rows[half].reshape(part * 2 * height, LANES) for half in range(2)], axis=1), interpolation[...]
    )
    return value.reshape(part, 2 * height, interpolation.shape[1])


def early_kernel(combined, beyond, interpolation, out, tails, extended, rows, ready, sems):
    levels = combined.shape[0]
    part = levels // PARTS
    done = ready.shape[1] - 8
    copies = []
    for start in range(0, levels, part):
        span = pl.ds(start, part)
        ready[span] = interpolate_levels(combined, beyond, None, 0, start, part, interpolation, extended, rows)
        copies.append(pltpu.make_async_copy(ready.at[span, pl.ds(0, done)], out.at[span, pl.ds(0, done)], sems.at[start // part]))
        copies[-1].start()
    tails[...] = ready[:, done:, :]
    for copy in copies:
        copy.wait()


def late_kernel(first, before, combined, beyond, north, interpolation, tails, out, extended, rows, ready, ends, kept, shifted, sems):
    levels = combined.shape[0]
    part = levels // PARTS
    lane = lax.broadcasted_iota(jnp.int32, shifted.shape, 1)
    inside = jnp.where(lax.axis_index("gy") == lax.axis_size("gy") - 1, 0.0, 1.0).astype(F32)
    corner = jnp.broadcast_to(north[:, LANES:LANES + 1], shifted.shape) * inside
    after = north[:, :LANES] * inside
    kept[...] = after
    shifted[...] = jnp.where(lane == LANES - 1, corner, pltpu.roll(after, LANES - 1, 1))
    copies = []
    row = 0.5 * exact_dot(jnp.concatenate([after, shifted[...]], axis=1), interpolation[...])
    ends[...] = tails[...]
    for level in range(first):
        ends[level, 7:8, :] = ends[level, 7:8, :] + row[level:level + 1, :]
    done = ready.shape[1] - 8
    copies.append(pltpu.make_async_copy(ends, out.at[pl.ds(0, first), pl.ds(done, 8)], sems.at[PARTS]))
    copies[-1].start()
    for start in range(0, levels, part):
        span = pl.ds(start, part)
        rows_north = (kept, shifted)
        ready[span] = interpolate_levels(combined, beyond, rows_north, first, start, part, interpolation, extended, rows)
        copies.append(pltpu.make_async_copy(ready.at[span], out.at[pl.ds(first + start, part)], sems.at[start // part]))
        copies[-1].start()
    for copy in copies:
        copy.wait()


def around(value, axis, step):
    size = lax.axis_size(axis)
    return lax.ppermute(value, axis, [(i, (i + step) % size) for i in range(size)])


def swap(value, second):
    nx, ny = lax.axis_size("gx"), lax.axis_size("gy")
    pairs = []
    for x in range(nx):
        for y in range(ny):
            other = ((y + 1) ^ 1) - 1 if second else y ^ 1
            pairs.append((x * ny + y, x * ny + other if 0 <= other < ny else (x ^ 1) * ny + y))
    return lax.ppermute(value, ("gx", "gy"), pairs)


def call(kernel, outs, scratch, cost, *args, in_hbm=0):
    vmem = pl.BlockSpec(memory_space=pltpu.VMEM)
    return pl.pallas_call(
        kernel,
        out_shape=tuple(jax.ShapeDtypeStruct(*out) if isinstance(out[0], tuple) else jax.ShapeDtypeStruct(out, F32) for out in outs),
        in_specs=[pl.BlockSpec(memory_space=pltpu.HBM) if i < in_hbm else vmem for i in range(len(args))],
        out_specs=tuple(vmem for _ in outs),
        scratch_shapes=[pltpu.VMEM(shape, F32) if isinstance(shape, tuple) else shape for shape in scratch],
        compiler_params=pltpu.CompilerParams(vmem_limit_bytes=VMEM_LIMIT),
        cost_estimate=pl.CostEstimate(flops=cost, bytes_accessed=2**20, transcendentals=0),
    )(*args)


def halves_of(table):
    high = table.astype(np.float32).astype(BF16)
    return high, (table.astype(np.float32) - high.astype(np.float32)).astype(BF16)


def shards(gradient, members):
    all_levels, fine_height, fine_width = gradient.shape
    count, _, height, width = members.shape
    assert count == 8 and width == LANES and height == 32 and lax.axis_size("gx") % 2 == 0 and lax.axis_size("gy") % 2 == 0
    assert all_levels % CHUNKS == 0
    levels = all_levels // CHUNKS
    groups = levels * height // GROUP

    south = around(gradient[:, -1, :], "gy", 1)

    columns = [column_table(width, i == 0, i == 2) for i in range(3)]
    own_tables = np.stack(halves_of(np.stack([table[:width] for table in columns])), axis=1)
    halo_tables = np.stack(halves_of(np.stack([halo_table(table, width, i == 0) for i, table in enumerate(columns)])), axis=1)
    places = halo_places()
    restrict = jnp.asarray(restriction_table(width), BF16)
    packing = jnp.asarray(packing_table(width), BF16).reshape(GROUP * width, 2 * LANES)
    refining = jnp.asarray(refining_table(width), BF16)
    interpolation = jnp.asarray(interpolation_table(width), BF16)
    beyond_high, beyond_low = map(jnp.asarray, halves_of(column_filter_table(width)))
    row_highs, row_lows = map(jnp.asarray, halves_of(np.stack([column_rows_table(height, i == 0, i == 2) for i in range(3)])))
    choice = jnp.asarray(edge_choice_table(), BF16)
    flops = 10**9 // CHUNKS

    hbm_of = functools.partial(pltpu.with_memory_space_constraint, memory_space=pltpu.HBM)
    constants = tuple(map(hbm_of, (jnp.asarray(own_tables), jnp.asarray(halo_tables), jnp.asarray(places, BF16), interpolation)))
    far_inputs = tuple(map(hbm_of, (gradient, members, restrict)))
    prepared, packed = [], []
    for chunk in range(CHUNKS):
        outs = [(2, levels, 8 + 2 * height, LANES), (levels, height, 8, LANES), (levels * height, LANES)]
        if chunk == 0:
            outs += [((4, 2 * LANES, 2 * LANES), BF16), ((4, 2 * LANES, 2 * LANES), BF16), (interpolation.shape, BF16)]
            scratch = [(levels, fine_height, fine_width), (8, levels, height, LANES)]
            shapes = (restrict.shape, own_tables.shape[1:], halo_tables.shape[1:], places.shape)
            scratch += [pltpu.VMEM(shape, BF16) for shape in shapes] + [pltpu.SemaphoreType.DMA((9,))]
            kernel = functools.partial(prepare_kernel, levels, height)
            prepared.append(call(kernel, outs, scratch, flops, *far_inputs, *constants, in_hbm=7))
        else:
            outs += [(levels, 8, 8, LANES), (levels, 8, 8, LANES)]
            kernel = functools.partial(prepare_more_kernel, chunk, levels, height)
            prepared.append(call(kernel, outs, [], flops, gradient, members, restrict, packed[-1][3]))
        packed.append(call(
            functools.partial(pack_kernel, chunk, levels, height),
            [(GROUP, groups * 8, LANES), (groups * 8, LANES), (groups * 8, LANES), (3, levels, 8, LANES), (7, levels // 2, 8, LANES)],
            [(2, height, LANES), (2, all_levels, LANES)],
            flops, *prepared[-1][:3], south, restrict, packing,
        ))
    high_weights, low_weights, interpolation = prepared[0][3:]
    got = [(around(packed[chunk][3], "gx", 1), around(packed[chunk][4], "gx", -1)) for chunk in range(CHUNKS)]
    rim_a, rim_b = prepared[1][3:]
    rims = swap(rim_a, False), swap(rim_b, True)
    filtered, far, own = [], [], []
    for chunk in range(CHUNKS):
        far_rows = (levels * (per_level_of(chunk) + 1), 8, LANES)
        more = (*rims, own[0][1]) if chunk else (packed[1][3],)
        filtered.append(call(
            functools.partial(columns_kernel, chunk, levels, height),
            [(groups, GROUP, 8, 2 * LANES), far_rows, far_rows, (levels, 8, LANES)],
            [(2, 8, 8, LANES)] if chunk else [],
            flops, *packed[chunk][:3], *got[chunk], high_weights, low_weights, beyond_high, beyond_low, choice, *more,
        ))
        far.append((swap(filtered[-1][1], False), swap(filtered[-1][2], True)))
        own.append(call(
            functools.partial(own_rows_kernel, levels, height),
            [(levels, height, 8, LANES), (levels, height // 2, 8, LANES)],
            [],
            flops, filtered[-1][0],
        ))
    part = levels // PARTS
    buffers = [(2, part, height + 8, LANES), (2, part, 2 * height, LANES), (levels, fine_height, fine_width)]
    vmem, hbm = pl.BlockSpec(memory_space=pltpu.VMEM), pl.BlockSpec(memory_space=pltpu.HBM)
    out_shape = jax.ShapeDtypeStruct(gradient.shape, F32)
    params = pltpu.CompilerParams(vmem_limit_bytes=VMEM_LIMIT)
    cost = pl.CostEstimate(flops=flops, bytes_accessed=2**20, transcendentals=0)

    def first_rows_of(chunk, *earlier):
        return call(
            functools.partial(first_row_kernel, chunk, levels),
            [(levels, LANES), ((chunk + 1) * levels, 2 * LANES)],
            [(levels * 8, LANES)],
            flops, *own[chunk], *far[chunk], filtered[chunk][1], filtered[chunk][3], prepared[chunk][1], refining, row_highs, row_lows, *earlier,
        )

    def combined_of(chunk):
        return call(
            functools.partial(combine_kernel, chunk, levels, height),
            [(levels, height, LANES)],
            [(height // 2 * 8, LANES), (height // 2 * 8, LANES)],
            flops, *own[chunk], *far[chunk], prepared[chunk][1], refining,
        )[0]

    early_beyond, early_rows = first_rows_of(0)
    out, tails = pl.pallas_call(
        early_kernel,
        out_shape=(out_shape, jax.ShapeDtypeStruct((levels, 8, fine_width), F32)),
        in_specs=[vmem] * 3, out_specs=(hbm, vmem),
        scratch_shapes=[pltpu.VMEM(shape, F32) for shape in buffers] + [pltpu.SemaphoreType.DMA((PARTS,))],
        compiler_params=params, cost_estimate=cost,
    )(combined_of(0), early_beyond, interpolation)
    beyond, rows = first_rows_of(1, early_rows, tails)
    north = around(rows, "gy", -1)
    out = pl.pallas_call(
        functools.partial(late_kernel, levels),
        out_shape=out_shape,
        in_specs=[hbm] + [vmem] * 5, out_specs=hbm,
        scratch_shapes=[pltpu.VMEM(shape, F32) for shape in buffers + [(levels, 8, fine_width), (all_levels, LANES), (all_levels, LANES)]]
        + [pltpu.SemaphoreType.DMA((PARTS + 1,))],
        input_output_aliases={0: 0},
        compiler_params=params, cost_estimate=cost,
    )(out, combined_of(1), beyond, north, interpolation, tails)
    return out


def solution(mesh):
    in_specs = (P(None, "gy", "gx"), P(None, None, "gy", "gx"))
    out_specs = P(None, "gy", "gx")

    return jax.shard_map(shards, mesh=mesh, in_specs=in_specs, out_specs=out_specs, check_vma=False)
```

```python
import functools

import jax
import jax.numpy as jnp
import numpy as np
from jax import lax
from jax.experimental import pallas as pl
from jax.experimental.pallas import tpu as pltpu
from jax.sharding import PartitionSpec as P


beta_raw = [(1.0 - (offset - 4) ** 2 / 25.0) ** 2 for offset in range(9)]
beta_taps = [value / sum(beta_raw) for value in beta_raw]
generations = ((1, 0.5), (2, 0.075), (4, 0.0125))

LANES = 128
GROUP = 8
SLOTS = (12, 14)
FREE = (8, 9)
USED = (8 * 12, 8 * 14)
COMPACT = 64
COLUMN = 32
CHUNKS = 2
PARTS = 4
VMEM_LIMIT = 20 * 2**20
BF16, F32 = jnp.bfloat16, jnp.float32
double_taps = [
    sum(beta_taps[k + 4] * beta_taps[offset - k + 4] for k in range(-4, 5) if -4 <= offset - k <= 4) for offset in range(9)
]
edge_taps = [
    [sum(beta_taps[i - k + 4] * beta_taps[k - j + 4] for k in range(-4, 0) if i - k <= 4 and j - k <= 4) for j in range(4)]
    for i in range(4)
]


def twice_filter(width, first, last):
    low, high = (0 if first else -99), (width - 1 if last else width + 99)
    table = np.zeros((width + 17, width + 1))
    for source in range(-8, width + 9):
        if not low <= source <= high:
            continue
        for middle in range(source - 4, source + 5):
            if not low <= middle <= high:
                continue
            for target in range(max(0, middle - 4), min(width, middle + 4) + 1):
                if target <= high:
                    table[source + 8, target] += beta_taps[middle - source + 4] * beta_taps[target - middle + 4]
    return table


def column_table(width, first, last):
    filters = {factor: twice_filter(width // factor, first, last) for factor, _ in generations}
    base = {1: 0, 2: LANES, 4: LANES + width // 2}

    def row(places):
        out = np.zeros(2 * LANES)
        for factor, place in places.items():
            count = width // factor
            out[base[factor]:base[factor] + count] += filters[factor][place + 8, :count]
        return out

    rows = [row({1: c, 2: c // 2, 4: c // 4}) for c in range(width)]
    rows += [row({1: c, 2: c // 2, 4: c // 4}) for c in range(-8, 0)]
    rows += [row({2: c, 4: c // 2}) for c in range(-8, -4)]
    rows += [row({4: c}) for c in range(-8, -4)]
    rows += [row({1: c, 2: c // 2, 4: c // 4}) for c in range(width, width + 8)] + [row({1: width + 8})]
    half, quarter = width // 2, width // 4
    rows += [row({2: c, 4: c // 2}) for c in range(half + 4, half + 8)] + [row({2: half + 8})]
    rows += [row({4: c}) for c in range(quarter + 4, quarter + 9)]
    return np.stack(rows)


def edge_lane(side, line):
    return SLOTS[side] * (line // 4 * 4 + 3) + FREE[side] + line % 4


def message_lanes():
    places = []
    for line in range(GROUP):
        for side, (first, second, fourth) in enumerate(((0, 8, 12), (16, 25, 30))):
            start = line * SLOTS[side]
            places += [(side, start + c, first + c, 1, line, line) for c in range(FREE[side])]
            rest = [start + c for c in range(FREE[side], SLOTS[side])]
            if line % 2 == 0:
                places += [(side, lane, second + c, 2, line, line) for c, lane in enumerate(rest)]
            if line % 4 == 1:
                places += [(side, lane, fourth + c, 4, line - 1, line) for c, lane in enumerate(rest)]
    return places


def packing_table(width):
    table = np.zeros((GROUP, width, 2 * LANES), np.float32)
    east = list(range(width - 8, width)) + [width // 2 - 8 + c for c in range(4)] + [width // 4 - 8 + c for c in range(4)]
    west = list(range(9)) + [4 + c for c in range(5)] + [4 + c for c in range(5)]
    for side, lane, compact, factor, line, _ in message_lanes():
        start = (west[compact - 16] if side else east[compact]) * factor
        table[line:line + factor, start:start + factor, side * LANES + lane] = 1.0
    return table


def halo_table(columns, width, first):
    table = np.zeros((COMPACT, 2 * LANES))
    table[:35] = columns[width:]
    table[35] = 0.0 if first else columns[0]
    return table


def halo_places():
    table = np.zeros((4, LANES, COMPACT), np.float32)
    for side, lane, compact, _, _, line in message_lanes():
        if line < 4:
            table[line, side * 64 + lane, compact] = 1.0
    for line in range(4):
        table[line, edge_lane(0, line), 35] = 1.0
        table[line, 64 + edge_lane(1, line), 16] = 1.0
    return table


def restriction_table(width):
    table = np.zeros((2 * width, 2 * LANES), np.float32)
    for i in range(width):
        table[2 * i, i] += 1.0
        table[2 * i + 1, i] += 0.5
        table[2 * i + 1, i + 1] += 0.5
    return table


def refining_table(width):
    table = np.zeros((LANES, LANES), np.float32)
    for i in range(width):
        table[i // 2, i] = 1.0
        table[width // 2 + i // 4, i] = 1.0
    return table


def column_lane(factor, row):
    count = GROUP // factor
    return row // count * COLUMN + {1: 0, 2: 8, 4: 12}[factor] + row % count


def column_filter_table(width):
    table = np.zeros((2 * LANES, LANES))
    filters = {factor: twice_filter(width // factor, False, False)[:, width // factor] for factor, _ in generations}
    low = [width - 8 + c for c in range(8)] + [width // 2 - 8 + c for c in range(4)] + [width // 4 - 8 + c for c in range(4)]
    high = [width + c for c in range(9)] + [width // 2 + 4 + c for c in range(5)] + [width // 4 + 4 + c for c in range(5)]
    ends = {(1, 16 + 8): 1, (2, 25 + 4): 2}
    for side, lane, compact, factor, line, _ in message_lanes():
        place = (high[compact - 16] if side else low[compact]) * factor
        for generation, _ in generations:
            if generation >= factor and generation <= ends.get((factor, compact), 4):
                weight = filters[generation][place // generation + 8]
                table[side * LANES + lane, column_lane(generation, line // generation)] += weight
    for line in range(GROUP):
        for generation, _ in generations:
            weight = filters[generation][width // generation + 8]
            table[LANES + edge_lane(1, line), column_lane(generation, line // generation)] += weight
    return table


def column_rows_table(height, first, last):
    table = np.zeros((3, LANES, LANES))
    for factor, weight in generations:
        count = height // factor
        filters = twice_filter(count, first, last)
        for row in range(height):
            for source in range(-8, count + 8):
                kind, place = (1, source + count) if source < 0 else (2, source - count) if source >= count else (0, source)
                table[kind, column_lane(factor, place), row] += weight * filters[source + 8, row // factor]
    return table


def edge_choice_table():
    table = np.zeros((LANES, LANES), np.float32)
    for line in range(GROUP):
        table[edge_lane(1, line), line] = 1.0
    return table


def interpolation_table(width):
    table = np.zeros((2 * LANES, 2 * width), np.float32)
    for i in range(width):
        table[i, 2 * i] = 1.0
        table[i, 2 * i + 1] = 0.5
        table[LANES + i, 2 * i + 1] = 0.5
    return table


def split(value):
    high = value.astype(BF16)
    return high, (value - high.astype(F32)).astype(BF16)


def mul(a, b):
    return jnp.dot(a, b, preferred_element_type=F32)


def exact_dot(value, table):
    high, low = split(value)
    return mul(high, table) + mul(low, table)


def three_dots(value, high_table, low_table):
    high, low = split(value)
    return mul(high, high_table) + mul(low, high_table) + mul(high, low_table)


def column_case():
    gx, nx = lax.axis_index("gx"), lax.axis_size("gx")
    return jnp.where(gx == 0, 0, jnp.where(gx == nx - 1, 2, 1))


def tile(index):
    return pl.ds(pl.multiple_of(index * 8, 8), 8)


def turn_members(height, raw, first, turned, edges, start, stop, rims=None):
    blocks = height // GROUP
    lane = lax.broadcasted_iota(jnp.int32, (GROUP, LANES), 1)
    up_a = lax.axis_index("gy") % 2 == 0

    def level_step(level, _):
        ends = []
        for block in range(blocks):
            edge = jnp.zeros((GROUP, LANES), F32)
            span = slice(block * GROUP, (block + 1) * GROUP)
            block_rows = jnp.swapaxes(raw[:, first + level, span, :], 0, 1)
            turned[level, span] = block_rows
            for line in range(GROUP):
                spot = edge_lane(1, line)
                edge = jnp.where(lane == spot, pltpu.roll(block_rows[line], spot, 1), edge)
            edges[tile(level * blocks + block), :] = edge
            ends.append(block_rows)
        if rims:
            rims[0][level] = jnp.where(up_a, ends[-1], ends[0])
            rims[1][level] = jnp.where(up_a, ends[0], ends[-1])
        return 0

    lax.fori_loop(start, stop, level_step, 0, unroll=4)


def reduce_columns(fine, first, count, height, table, across, start):
    value = exact_dot(fine[first:first + count].reshape(count * 2 * height, fine.shape[2]), table[...])
    value = value.reshape(count, 2 * height, 2 * LANES)
    for half in range(2):
        across[half, start:start + count, 8:, :] = value[:, :, half * LANES:(half + 1) * LANES]
        across[half, start:start + count, 0:8, :] = jnp.zeros((count, 8, LANES), F32)


def prepare_kernel(levels, height, gradient, members, restrict, across, turned, edges, fine, raw, table, sems):
    part = levels // 2
    moves = [(restrict, table)]
    moves += [(gradient.at[pl.ds(i * part, part)], fine.at[pl.ds(i * part, part)]) for i in range(2)]
    moves += [(members.at[:, pl.ds(i * part, part)], raw.at[:, pl.ds(i * part, part)]) for i in range(2)]
    copies = [pltpu.make_async_copy(source, target, sems.at[i]) for i, (source, target) in enumerate(moves)]
    for copy in copies:
        copy.start()
    copies[0].wait()
    for i in range(2):
        copies[1 + i].wait()
        reduce_columns(fine, i * part, part, height, table, across, i * part)
    for i in range(2):
        copies[3 + i].wait()
        turn_members(height, raw, 0, turned, edges, i * part, (i + 1) * part)


def prepare_more_kernel(chunk, levels, height, gradient, members, restrict, _, own_tables, halo_tables, places, refine,
                        across, turned, edges, rim_a, rim_b, high_weights, low_weights, refine_out):
    case = column_case()
    refine_out[...] = refine[...]
    for which, target in ((0, high_weights), (1, low_weights)):
        for variant in range(4):
            target[variant, :LANES, :] = own_tables[case, which]
            target[variant, LANES:, :] = mul(places[variant], halo_tables[case, which]).astype(BF16)
    reduce_columns(gradient, chunk * levels, levels, height, restrict, across, 0)
    turn_members(height, members, chunk * levels, turned, edges, 0, levels, (rim_a, rim_b))


def pack_kernel(chunk, levels, height, across, turned, edges, south, restrict, packing, products, own_east, own_west, to_east, to_west,
                coarse, below):
    blocks = height // GROUP
    first = chunk * levels
    value = exact_dot(south[...], restrict[...]) * jnp.where(lax.axis_index("gy") == 0, 0.0, 1.0).astype(F32)
    for half in range(2):
        below[half] = value[:, half * LANES:(half + 1) * LANES]
    lane = lax.broadcasted_iota(jnp.int32, (GROUP, LANES), 1)
    line_of = lax.broadcasted_iota(jnp.int32, (GROUP, LANES), 0)
    spots = (line_of >> 2) * (4 * SLOTS[0]) + edge_lane(0, 0) + (line_of & 3)
    top = lax.broadcasted_iota(jnp.int32, (height, LANES), 0) == 0

    def level_step(level, _):
        for half in range(2):
            under = jnp.broadcast_to(below[half, pl.ds(first + level, 1), :], (height, LANES))
            under = jnp.where(top, under, across[half, level, pl.ds(7, height, 2), :])
            coarse[half] = across[half, level, pl.ds(8, height, 2), :] + 0.5 * (
                across[half, level, pl.ds(9, height, 2), :] + under
            )
        for block in range(blocks):
            place_rows = tile(level * blocks + block)
            for line in range(GROUP):
                y = block * GROUP + line
                products[line, place_rows, :] = turned[level, y] * coarse[0, y:y + 1, :]
            column = jnp.broadcast_to(coarse[1, block * GROUP:(block + 1) * GROUP, 0:1], (GROUP, LANES))
            column = jnp.sum(jnp.where(lane == spots, column, 0.0), axis=0, keepdims=True)
            own_east[place_rows, :] = jnp.broadcast_to(column, (GROUP, LANES))
        return 0

    lax.fori_loop(0, levels, level_step, 0, unroll=4)
    total = jnp.zeros((levels * blocks * 8, 2 * LANES), F32)
    for line in range(0, GROUP, 2):
        value = jnp.concatenate([products[line], products[line + 1]], axis=1)
        total = total + exact_dot(value, packing[line * LANES:(line + 2) * LANES, :])
    own_east[...] = own_east[...] + total[:, :LANES]
    own_west[...] = total[:, LANES:] + edges[...]
    lane = lax.broadcasted_iota(jnp.int32, (levels, 8, LANES), 2)
    groups = [own_east[...].reshape(levels, 4, 8, LANES)[:, i] for i in range(4)]
    for i in range(3):
        to_east[i] = jnp.where(lane < USED[0], groups[i], pltpu.roll(groups[3], USED[0] - 32 * i, 2))
    lane = lane[:levels // 2]
    groups = [own_west[...].reshape(levels // 2, 8, 8, LANES)[:, i] for i in range(8)]
    for i in range(7):
        to_west[i] = jnp.where(lane < USED[1], groups[i], pltpu.roll(groups[7], USED[1] - 16 * i, 2))


def outside(load):
    values = [load(j) for j in range(8)]
    result = []
    for i in range(8):
        total = double_taps[i + 1] * values[0]
        for j in range(1, 8 - i):
            total = total + double_taps[i + 1 + j] * values[j]
        result.append(total)
    return result


def per_level_of(chunk):
    return 7 if chunk else 14


def columns_kernel(chunk, levels, height, products, own_a, own_b, from_west, from_east, high_weights, low_weights,
                   beyond_high, beyond_low, choice, *refs):
    if chunk:
        rims, refs, weighted = refs[:2], refs[3:-1], refs[-1]
    else:
        refs = refs[1:]
    filtered, message_a, message_b, factors = refs
    per_level = per_level_of(chunk)
    blocks = height // GROUP
    groups = levels * blocks
    lane = lax.broadcasted_iota(jnp.int32, (groups * 8, LANES), 1)
    own_east, own_west = own_a[...], own_b[...]
    whole = lax.broadcasted_iota(jnp.int32, (levels, 8, LANES), 2)
    parts = [from_west[i] for i in range(3)]
    last = pltpu.roll(parts[2], 96, 2)
    for i in range(2):
        last = jnp.where((whole >= 32 * i) & (whole < 32 * i + 32), pltpu.roll(parts[i], 32 * i + 32, 2), last)
    west = jnp.stack(parts + [last], axis=1).reshape(groups * 8, LANES)
    whole = whole[:levels // 2]
    parts = [from_east[i] for i in range(7)]
    last = pltpu.roll(parts[6], 112, 2)
    for i in range(6):
        last = jnp.where((whole >= 16 * i) & (whole < 16 * i + 16), pltpu.roll(parts[i], 16 * i + 16, 2), last)
    east = jnp.stack(parts + [last], axis=1).reshape(groups * 8, LANES)
    chosen = exact_dot(east, choice[...]).reshape(levels, blocks, 8, LANES)
    total = chosen[:, 0]
    for block in range(1, blocks):
        total = total + pltpu.roll(chosen[:, block], block * GROUP, 2)
    factors[...] = total
    shifts = [edge_lane(1, line) - edge_lane(0, line) for line in (0, 4)]
    for line, shift in zip((0, 4), shifts):
        spot = (lane >= edge_lane(0, line)) & (lane < edge_lane(0, line) + 4)
        west = jnp.where(spot, west * pltpu.roll(own_west, LANES - shift, 1), west)
        spot = (lane >= edge_lane(1, line)) & (lane < edge_lane(1, line) + 4)
        east = jnp.where(spot, east * pltpu.roll(own_east, shift, 1), east)
    inside = jnp.where(lax.axis_index("gx") == lax.axis_size("gx") - 1, 0.0, 1.0).astype(F32)
    beyond = three_dots(jnp.concatenate([own_east, east], axis=1), beyond_high[...], beyond_low[...])
    beyond = (beyond * inside).reshape(levels, blocks, 8, LANES)
    total = beyond[:, 0]
    for block in range(1, blocks):
        total = total + pltpu.roll(beyond[:, block], block * COLUMN, 2)
    for message in (message_a, message_b):
        message[levels * per_level:] = total
    halves = [
        split(jnp.where(lane < 64, west, pltpu.roll(east, 64, 1))),
        split(jnp.where(lane < 64, pltpu.roll(west, LANES - USED[0] // 2, 1), pltpu.roll(east, 64 - USED[1] // 2, 1))),
    ]
    for line in range(GROUP):
        high, low = (jnp.concatenate(pair, axis=1) for pair in zip(split(products[line]), halves[line // 4]))
        weights = high_weights[line % 4]
        value = mul(high, weights) + mul(low, weights) + mul(high, low_weights[line % 4])
        filtered[:, line] = value.reshape(groups, 8, 2 * LANES)
    small = lax.broadcasted_iota(jnp.int32, (8, LANES), 1)
    second = small < 64
    up_a = lax.axis_index("gy") % 2 == 0
    start_a, start_b = jnp.where(up_a, blocks - 1, 0), jnp.where(up_a, 0, blocks - 1)
    coarse_a, coarse_b = jnp.where(up_a, blocks - 2, 0), jnp.where(up_a, 0, blocks - 2)

    def level_step(level, _):
        def at(block, line):
            return filtered[level * blocks + block, line, :, LANES:]

        fourth = []
        for block in range(blocks):
            for half in range(2):
                fourth.append(sum(at(block, half * 4 + k) for k in range(1, 4)) + at(block, half * 4))
        sides = ((message_a, start_a, coarse_a, up_a), (message_b, start_b, coarse_b, jnp.logical_not(up_a)))
        for side, (message, start, coarse, upward) in enumerate(sides):
            if chunk:
                def nearest(j):
                    return filtered[level * blocks + start, jnp.where(upward, 7 - j, j), :, :LANES]

                for i, value in enumerate(outside(nearest)):
                    place = jnp.where(upward, i, 7 - i)
                    weighted[side, place] = rims[side][level, place] * value
                total = jnp.sum(jnp.swapaxes(weighted[side], 0, 1), axis=0)
                message[level * per_level] = jnp.float32(generations[0][1]) * total
            rows = []
            for line in range(GROUP):
                if not chunk:
                    message[level * per_level + line] = filtered[level * blocks + start, line, :, :LANES]
                block, pair = coarse + line // 4, line % 4
                pairs = at(block, 2 * pair) + at(block, 2 * pair + 1)
                rows.append(jnp.where(second, pairs, fourth[line]))
            for i in range(6):
                spare = pltpu.roll(rows[6 + i // 3], 96 - 32 * (i % 3), 1)
                message[level * per_level + per_level - 6 + i] = jnp.where(small < 96, rows[i], spare)
        return 0

    lax.fori_loop(0, levels, level_step, 0, unroll=4)


def convolve_own(load, count, low_edges, high_edges, store):
    rows = {}

    def row(r):
        if r not in rows:
            rows[r] = load(r)
        return rows[r]

    for r in range(count):
        value = double_taps[0] * row(r)
        for k in range(1, 9):
            near = [row(q) for q in (r - k, r + k) if 0 <= q < count]
            if near:
                value = value + double_taps[k] * (near[0] if len(near) == 1 else near[0] + near[1])
        if r < 4:
            fix = edge_taps[r][0] * row(0)
            for j in range(1, 4):
                fix = fix + edge_taps[r][j] * row(j)
            value = value - low_edges * fix
        for flag, end in high_edges:
            i = end - 1 - r
            if 0 <= i < 4:
                fix = edge_taps[i][0] * row(end - 1)
                for j in range(1, 4):
                    fix = fix + edge_taps[i][j] * row(end - 1 - j)
                value = value - flag * fix
        store(r, value)
        rows.pop(r - 8, None)


def own_rows_kernel(levels, height, filtered, fine, coarse):
    blocks = height // GROUP
    half, quarter = height // 2, height // 4
    gy, ny = lax.axis_index("gy"), lax.axis_size("gy")
    low, high = jnp.where(gy == 0, 1.0, 0.0).astype(F32), jnp.where(gy == ny - 1, 1.0, 0.0).astype(F32)
    second = lax.broadcasted_iota(jnp.int32, (8, LANES), 1) < 64
    high_second, high_fourth = jnp.where(second, high, 0.0), jnp.where(second, 0.0, high)

    def level_step(level, _):
        def at(y, part):
            return filtered[level * blocks + y // 8, y % 8, :, part * LANES:(part + 1) * LANES]

        def store_to(ref):
            def store(r, value):
                ref[level, r] = value

            return store

        convolve_own(lambda r: at(r, 0), height, low, [(high, height)], store_to(fine))

        def pair(r):
            return at(2 * r, 1) + at(2 * r + 1, 1)

        def load_coarse(r):
            return jnp.where(second, pair(r), pair(2 * r) + pair(2 * r + 1) if r < quarter else 0.0)

        convolve_own(load_coarse, half, low, [(high_second, half), (high_fourth, quarter)], store_to(coarse))
        return 0

    lax.fori_loop(0, levels, level_step, 0, unroll=4)


def coarse_rows(packed, lane):
    rows = list(packed)
    for i in range(2):
        pieces = [pltpu.roll(packed[3 * i + k], 32 + 32 * k, 1) for k in range(3)]
        rows.append(jnp.where(lane < 32, pieces[0], jnp.where(lane < 64, pieces[1], pieces[2])))
    return rows


def coarse_scale(lane):
    return jnp.where(lane < 64, jnp.float32(generations[1][1]), jnp.float32(generations[2][1]))


def first_row_kernel(chunk, levels, fine, coarse, got_a, got_b, own_rows, factors, turned, refining, row_highs, row_lows, *refs):
    earlier, (beyond, first_row, packed) = refs[:1] if chunk else (), refs[-3:]
    first = chunk * levels
    up_a = lax.axis_index("gy") % 2 == 0
    gy, ny = lax.axis_index("gy"), lax.axis_size("gy")

    def side(value):
        return value.reshape(levels * 8, LANES)

    case = jnp.where(gy == 0, 0, jnp.where(gy == ny - 1, 2, 1))
    per_level = per_level_of(chunk)
    skip = per_level - 6
    extra = slice(levels * per_level, levels * (per_level + 1))
    far_a, far_b = side(got_a[extra]), side(got_b[extra])
    value = three_dots(side(own_rows[extra]), row_highs[case, 0], row_lows[case, 0])
    value = value + three_dots(jnp.where(up_a, far_b, far_a), row_highs[case, 1], row_lows[case, 1])
    value = value + three_dots(jnp.where(up_a, far_a, far_b), row_highs[case, 2], row_lows[case, 2])
    beyond[...] = jnp.sum(value.reshape(levels, 8, LANES) * factors[...], axis=1) * (1.0 / 7.0)

    lane = lax.broadcasted_iota(jnp.int32, (8, LANES), 1)
    second = lane < 64
    weight = jnp.float32(generations[0][1])
    keep = jnp.where((gy == 0) | (gy == ny - 1), 0.0, 1.0).astype(F32)
    for level in range(levels):
        base = level * per_level
        value = coarse[level, 0]
        below = [jnp.where(up_a, keep * got_b[base + skip + r], got_a[base + skip + r]) for r in range(6)]
        below = coarse_rows(below, lane)
        for j in range(8):
            value = value + double_taps[j + 1] * below[7 - j]
        above = jnp.where(up_a, got_a[base + skip], keep * got_b[base + skip])
        value = value + jnp.where(second, 0.0, double_taps[8] * above)
        packed[level * 8:level * 8 + 8, :] = value * coarse_scale(lane)
    refined = exact_dot(packed[...], refining[...])
    for rows in earlier:
        first_row[:first, :] = rows[...]
    for level in range(levels):
        base = level * per_level
        value = fine[level, 0]
        if not chunk:
            for j in range(8):
                value = value + double_taps[j + 1] * jnp.where(up_a, keep * got_b[base + 7 - j], got_a[base + 7 - j])
        value = turned[level, 0] * (weight * value + refined[level * 8:level * 8 + 8, :])
        value = jnp.sum(value, axis=0, keepdims=True)
        if chunk:
            value = value + jnp.where(up_a, keep * got_b[base, 0:1, :], got_a[base, 0:1, :])
        first_row[first + level:first + level + 1, :LANES] = value * (1.0 / 7.0)
    first_row[first:, LANES:] = beyond[...]


def combine_kernel(chunk, levels, height, fine, coarse, got_a, got_b, turned, refining, combined, stacked, refined):
    blocks = height // GROUP
    half, quarter = height // 2, height // 4
    per_level = per_level_of(chunk)
    up_a = lax.axis_index("gy") % 2 == 0
    lane = lax.broadcasted_iota(jnp.int32, (8, LANES), 1)
    second = lane < 64
    scale = coarse_scale(lane)
    weight = jnp.float32(generations[0][1])
    gy, ny = lax.axis_index("gy"), lax.axis_size("gy")
    keep = jnp.where((gy == 0) | (gy == ny - 1), 0.0, 1.0).astype(F32)

    def level_step(level, _):
        base = level * per_level

        def north(r):
            return jnp.where(up_a, got_a[base + r], keep * got_b[base + r])

        def south(r):
            return jnp.where(up_a, keep * got_b[base + r], got_a[base + r])

        below = coarse_rows([south(per_level - 6 + r) for r in range(6)], lane)
        above = coarse_rows([north(per_level - 6 + r) for r in range(6)], lane)
        if not chunk:
            fine_south = outside(lambda j: south(7 - j))
            fine_north = outside(north)
        coarse_south = outside(lambda j: below[7 - j])
        coarse_north = outside(lambda j: above[j])
        parts = []
        for r in range(half):
            value = coarse[level, r]
            if r < 8:
                value = value + coarse_south[r]
            if r < quarter:
                i = quarter - 1 - r
                value = value + jnp.where(second, 0.0, coarse_north[i])
            if r >= half - 8:
                value = value + jnp.where(second, coarse_north[half - 1 - r], 0.0)
            parts.append(value * scale)
        for r in range(half):
            stacked[r * 8:r * 8 + 8, :] = jnp.where(second, parts[r], parts[r // 2])
        refined[...] = exact_dot(stacked[...], refining[...])
        for block in range(blocks):
            weighted = []
            for line in range(GROUP):
                y = block * GROUP + line
                value = fine[level, y]
                if y < 8 and not chunk:
                    value = value + fine_south[y]
                if y >= height - 8 and not chunk:
                    value = value + fine_north[height - 1 - y]
                value = weight * value + refined[y // 2 * 8:y // 2 * 8 + 8, :]
                weighted.append(turned[level, y] * value)
            total = jnp.sum(jnp.swapaxes(jnp.stack(weighted), 0, 1), axis=0)
            if chunk and block == 0:
                total = total + south(0)
            if chunk and block == blocks - 1:
                total = total + north(0)
            combined[level, block * GROUP:(block + 1) * GROUP, :] = total * (1.0 / 7.0)
        return 0

    lax.fori_loop(0, levels, level_step, 0, unroll=4)


def interpolate_levels(combined, beyond, north, first, start, part, interpolation, extended, rows):
    height = combined.shape[1]
    lane = lax.broadcasted_iota(jnp.int32, (height, LANES), 1)
    line = lax.broadcasted_iota(jnp.int32, (height, LANES), 0)
    for i in range(part):
        level = start + i
        here = combined[level]
        last = jnp.broadcast_to(beyond[level:level + 1, :], (height, LANES))
        last = jnp.sum(jnp.where(lane == line, last, 0.0), axis=1, keepdims=True)
        extended[0, i, 0:height, :] = here
        extended[1, i, 0:height, :] = jnp.where(lane == LANES - 1, last, pltpu.roll(here, LANES - 1, 1))
        for half in range(2):
            if north is None:
                extended[half, i, height:height + 1, :] = jnp.zeros((1, LANES), F32)
            else:
                extended[half, i, height:height + 1, :] = north[half][first + level:first + level + 1, :]
            value = extended[half, i, 0:height, :]
            rows[half, i, pl.ds(0, height, 2), :] = value
            rows[half, i, pl.ds(1, height, 2), :] = 0.5 * (value + extended[half, i, 1:height + 1, :])
    value = exact_dot(
        jnp.concatenate([rows[half].reshape(part * 2 * height, LANES) for half in range(2)], axis=1), interpolation[...]
    )
    return value.reshape(part, 2 * height, interpolation.shape[1])


def early_kernel(combined, beyond, interpolation, out, tails, extended, rows, ready, sems):
    levels = combined.shape[0]
    part = levels // PARTS
    done = ready.shape[1] - 8
    copies = []
    for start in range(0, levels, part):
        span = pl.ds(start, part)
        ready[span] = interpolate_levels(combined, beyond, None, 0, start, part, interpolation, extended, rows)
        copies.append(pltpu.make_async_copy(ready.at[span, pl.ds(0, done)], out.at[span, pl.ds(0, done)], sems.at[start // part]))
        copies[-1].start()
    tails[...] = ready[:, done:, :]
    for copy in copies:
        copy.wait()


def late_kernel(first, before, combined, beyond, north, interpolation, tails, out, extended, rows, ready, ends, kept, shifted, sems):
    levels = combined.shape[0]
    part = levels // PARTS
    lane = lax.broadcasted_iota(jnp.int32, shifted.shape, 1)
    inside = jnp.where(lax.axis_index("gy") == lax.axis_size("gy") - 1, 0.0, 1.0).astype(F32)
    corner = jnp.broadcast_to(north[:, LANES:LANES + 1], shifted.shape) * inside
    after = north[:, :LANES] * inside
    kept[...] = after
    shifted[...] = jnp.where(lane == LANES - 1, corner, pltpu.roll(after, LANES - 1, 1))
    copies = []
    row = 0.5 * exact_dot(jnp.concatenate([after, shifted[...]], axis=1), interpolation[...])
    ends[...] = tails[...]
    for level in range(first):
        ends[level, 7:8, :] = ends[level, 7:8, :] + row[level:level + 1, :]
    done = ready.shape[1] - 8
    copies.append(pltpu.make_async_copy(ends, out.at[pl.ds(0, first), pl.ds(done, 8)], sems.at[PARTS]))
    copies[-1].start()
    for start in range(0, levels, part):
        span = pl.ds(start, part)
        rows_north = (kept, shifted)
        ready[span] = interpolate_levels(combined, beyond, rows_north, first, start, part, interpolation, extended, rows)
        copies.append(pltpu.make_async_copy(ready.at[span], out.at[pl.ds(first + start, part)], sems.at[start // part]))
        copies[-1].start()
    for copy in copies:
        copy.wait()


def around(value, axis, step):
    size = lax.axis_size(axis)
    return lax.ppermute(value, axis, [(i, (i + step) % size) for i in range(size)])


def swap(value, second):
    nx, ny = lax.axis_size("gx"), lax.axis_size("gy")
    pairs = []
    for x in range(nx):
        for y in range(ny):
            other = ((y + 1) ^ 1) - 1 if second else y ^ 1
            pairs.append((x * ny + y, x * ny + other if 0 <= other < ny else (x ^ 1) * ny + y))
    return lax.ppermute(value, ("gx", "gy"), pairs)


def call(kernel, outs, scratch, cost, *args, in_hbm=0):
    vmem = pl.BlockSpec(memory_space=pltpu.VMEM)
    return pl.pallas_call(
        kernel,
        out_shape=tuple(jax.ShapeDtypeStruct(*out) if isinstance(out[0], tuple) else jax.ShapeDtypeStruct(out, F32) for out in outs),
        in_specs=[pl.BlockSpec(memory_space=pltpu.HBM) if i < in_hbm else vmem for i in range(len(args))],
        out_specs=tuple(vmem for _ in outs),
        scratch_shapes=[pltpu.VMEM(shape, F32) if isinstance(shape, tuple) else shape for shape in scratch],
        compiler_params=pltpu.CompilerParams(vmem_limit_bytes=VMEM_LIMIT),
        cost_estimate=pl.CostEstimate(flops=cost, bytes_accessed=2**20, transcendentals=0),
    )(*args)


def halves_of(table):
    high = table.astype(np.float32).astype(BF16)
    return high, (table.astype(np.float32) - high.astype(np.float32)).astype(BF16)


def shards(gradient, members):
    all_levels, fine_height, fine_width = gradient.shape
    count, _, height, width = members.shape
    assert count == 8 and width == LANES and height == 32 and lax.axis_size("gx") % 2 == 0 and lax.axis_size("gy") % 2 == 0
    assert all_levels % CHUNKS == 0
    levels = all_levels // CHUNKS
    groups = levels * height // GROUP

    south = around(gradient[:, -1, :], "gy", 1)

    columns = [column_table(width, i == 0, i == 2) for i in range(3)]
    own_tables = np.stack(halves_of(np.stack([table[:width] for table in columns])), axis=1)
    halo_tables = np.stack(halves_of(np.stack([halo_table(table, width, i == 0) for i, table in enumerate(columns)])), axis=1)
    places = halo_places()
    restrict = jnp.asarray(restriction_table(width), BF16)
    packing = jnp.asarray(packing_table(width), BF16).reshape(GROUP * width, 2 * LANES)
    refining = jnp.asarray(refining_table(width), BF16)
    interpolation = jnp.asarray(interpolation_table(width), BF16)
    beyond_high, beyond_low = map(jnp.asarray, halves_of(column_filter_table(width)))
    row_highs, row_lows = map(jnp.asarray, halves_of(np.stack([column_rows_table(height, i == 0, i == 2) for i in range(3)])))
    choice = jnp.asarray(edge_choice_table(), BF16)
    flops = 10**9 // CHUNKS

    hbm_of = functools.partial(pltpu.with_memory_space_constraint, memory_space=pltpu.HBM)
    constants = (jnp.asarray(own_tables), jnp.asarray(halo_tables), jnp.asarray(places, BF16), interpolation)
    far_inputs = tuple(map(hbm_of, (gradient, members, restrict)))
    prepared, packed = [], []
    for chunk in range(CHUNKS):
        outs = [(2, levels, 8 + 2 * height, LANES), (levels, height, 8, LANES), (levels * height, LANES)]
        if chunk == 0:
            scratch = [(levels, fine_height, fine_width), (8, levels, height, LANES), pltpu.VMEM(restrict.shape, BF16)]
            kernel = functools.partial(prepare_kernel, levels, height)
            prepared.append(call(kernel, outs, scratch + [pltpu.SemaphoreType.DMA((5,))], flops, *far_inputs, in_hbm=3))
        else:
            outs += [(levels, 8, 8, LANES), (levels, 8, 8, LANES)]
            outs += [((4, 2 * LANES, 2 * LANES), BF16), ((4, 2 * LANES, 2 * LANES), BF16), (interpolation.shape, BF16)]
            kernel = functools.partial(prepare_more_kernel, chunk, levels, height)
            prepared.append(call(kernel, outs, [], flops, gradient, members, restrict, packed[-1][3], *constants))
        packed.append(call(
            functools.partial(pack_kernel, chunk, levels, height),
            [(GROUP, groups * 8, LANES), (groups * 8, LANES), (groups * 8, LANES), (3, levels, 8, LANES), (7, levels // 2, 8, LANES)],
            [(2, height, LANES), (2, all_levels, LANES)],
            flops, *prepared[-1][:3], south, restrict, packing,
        ))
    high_weights, low_weights, interpolation = prepared[1][5:]
    got = [(around(packed[chunk][3], "gx", 1), around(packed[chunk][4], "gx", -1)) for chunk in range(CHUNKS)]
    rim_a, rim_b = prepared[1][3:5]
    rims = swap(rim_a, False), swap(rim_b, True)
    filtered, far, own = [], [], []
    for chunk in range(CHUNKS):
        far_rows = (levels * (per_level_of(chunk) + 1), 8, LANES)
        more = (*rims, own[0][1]) if chunk else (packed[1][3],)
        filtered.append(call(
            functools.partial(columns_kernel, chunk, levels, height),
            [(groups, GROUP, 8, 2 * LANES), far_rows, far_rows, (levels, 8, LANES)],
            [(2, 8, 8, LANES)] if chunk else [],
            flops, *packed[chunk][:3], *got[chunk], high_weights, low_weights, beyond_high, beyond_low, choice, *more,
        ))
        far.append((swap(filtered[-1][1], False), swap(filtered[-1][2], True)))
        own.append(call(
            functools.partial(own_rows_kernel, levels, height),
            [(levels, height, 8, LANES), (levels, height // 2, 8, LANES)],
            [],
            flops, filtered[-1][0],
        ))
    part = levels // PARTS
    buffers = [(2, part, height + 8, LANES), (2, part, 2 * height, LANES), (levels, fine_height, fine_width)]
    vmem, hbm = pl.BlockSpec(memory_space=pltpu.VMEM), pl.BlockSpec(memory_space=pltpu.HBM)
    out_shape = jax.ShapeDtypeStruct(gradient.shape, F32)
    params = pltpu.CompilerParams(vmem_limit_bytes=VMEM_LIMIT)
    cost = pl.CostEstimate(flops=flops, bytes_accessed=2**20, transcendentals=0)

    def first_rows_of(chunk, *earlier):
        return call(
            functools.partial(first_row_kernel, chunk, levels),
            [(levels, LANES), ((chunk + 1) * levels, 2 * LANES)],
            [(levels * 8, LANES)],
            flops, *own[chunk], *far[chunk], filtered[chunk][1], filtered[chunk][3], prepared[chunk][1], refining, row_highs, row_lows, *earlier,
        )

    def combined_of(chunk):
        return call(
            functools.partial(combine_kernel, chunk, levels, height),
            [(levels, height, LANES)],
            [(height // 2 * 8, LANES), (height // 2 * 8, LANES)],
            flops, *own[chunk], *far[chunk], prepared[chunk][1], refining,
        )[0]

    early_beyond, early_rows = first_rows_of(0)
    out, tails = pl.pallas_call(
        early_kernel,
        out_shape=(out_shape, jax.ShapeDtypeStruct((levels, 8, fine_width), F32)),
        in_specs=[vmem] * 3, out_specs=(hbm, vmem),
        scratch_shapes=[pltpu.VMEM(shape, F32) for shape in buffers] + [pltpu.SemaphoreType.DMA((PARTS,))],
        compiler_params=params, cost_estimate=cost,
    )(combined_of(0), early_beyond, interpolation)
    beyond, rows = first_rows_of(1, early_rows, tails)
    north = around(rows, "gy", -1)
    out = pl.pallas_call(
        functools.partial(late_kernel, levels),
        out_shape=out_shape,
        in_specs=[hbm] + [vmem] * 5, out_specs=hbm,
        scratch_shapes=[pltpu.VMEM(shape, F32) for shape in buffers + [(levels, 8, fine_width), (all_levels, LANES), (all_levels, LANES)]]
        + [pltpu.SemaphoreType.DMA((PARTS + 1,))],
        input_output_aliases={0: 0},
        compiler_params=params, cost_estimate=cost,
    )(out, combined_of(1), beyond, north, interpolation, tails)
    return out


def solution(mesh):
    in_specs = (P(None, "gy", "gx"), P(None, None, "gy", "gx"))
    out_specs = P(None, "gy", "gx")

    return jax.shard_map(shards, mesh=mesh, in_specs=in_specs, out_specs=out_specs, check_vma=False)
```
